32 devices in a mesh: shard: 8 (over z, x), tensor: 4 (over y, core).
Axes of the slice: x: 2, y: 2, z: 4, core: 2. Of those that a mesh axis runs over, the one named last changes fastest.
Arguments:
- att_grads: float32 [2, 4, 768, 768], P(None, None, 'shard', 'tensor'), may hold values from -6 to 6
- glu_grads: float32 [2, 4, 768, 1024], P(None, None, 'shard', 'tensor'), may hold values from -6 to 6
- att_weight: float32 [4, 768, 768], P(None, 'shard', 'tensor'), may hold values from -0.21875 to 0.21875
- att_moment: float32 [4, 768, 768], P(None, 'shard', 'tensor'), may hold values from -4 to 4
- att_second: float32 [4, 768, 768], P(None, 'shard', 'tensor'), may hold values from 0.05 to 1
- glu_weight: float32 [4, 768, 1024], P(None, 'shard', 'tensor'), may hold values from -0.21875 to 0.21875
- glu_moment: float32 [4, 768, 1024], P(None, 'shard', 'tensor'), may hold values from -4 to 4
- glu_second: float32 [4, 768, 1024], P(None, 'shard', 'tensor'), may hold values from 0.05 to 1
- att_stats: float32 [8, 2, 768, 768], P('shard', None, 'tensor'), may hold values from -1 to 10
- att_left_root: bfloat16 [8, 768, 768], P('shard', 'tensor'), may hold values from -1 to 2
- att_right_root: bfloat16 [8, 768, 768], P('shard', None, 'tensor'), may hold values from -1 to 2
- glu_left_stat: float32 [8, 768, 768], P('shard', 'tensor'), may hold values from -1 to 10
- glu_right_stat: float32 [8, 1024, 1024], P('shard', 'tensor'), may hold values from -1 to 10
- glu_left_root: bfloat16 [8, 768, 768], P('shard', 'tensor'), may hold values from -1 to 2
- glu_right_root: bfloat16 [8, 1024, 1024], P('shard', None, 'tensor'), may hold values from -1 to 2
- att_owner: int32 [4], replicated, may hold values from 0 to 7, as said below
- glu_owner: int32 [4], replicated, may hold values from 0 to 7, as said below
Outputs:
- att_weight_out: float32 [4, 768, 768], P(None, 'shard', 'tensor')
- att_moment_out: float32 [4, 768, 768], P(None, 'shard', 'tensor')
- att_second_out: float32 [4, 768, 768], P(None, 'shard', 'tensor')
- glu_weight_out: float32 [4, 768, 1024], P(None, 'shard', 'tensor')
- glu_moment_out: float32 [4, 768, 1024], P(None, 'shard', 'tensor')
- glu_second_out: float32 [4, 768, 1024], P(None, 'shard', 'tensor')
- att_stats_out: float32 [8, 2, 768, 768], P('shard', None, 'tensor')
- glu_left_out: float32 [8, 768, 768], P('shard', 'tensor')
- glu_right_out: float32 [8, 1024, 1024], P('shard', 'tensor')
The draws below stay inside these ranges and needn't reach their ends.
Inputs may be any that keep to these rules, and one draw needn't show every extreme that they name: `att_owner`: distinct owners; no owner holds more than one attention matrix. `glu_owner`: distinct owners; no owner holds more than one GeGLU block; in every draw some owner holds an attention matrix and a GeGLU block.
All inputs are finite; a program needn't handle non-finite values.
Results may differ from the reference program's by a relative error of at most 0.0014.
Values may be sent and summed in bfloat16 or wider, within the bound.
No kernel may reach another device: no remote copies, remote signals or barrier semaphores. Data moves between devices by JAX's collectives and lax.ppermute only.
A program may use at most 128 MiB of HBM per device.

```python
import math
import jax
import jax.numpy as jnp
from jax import lax

D = 768
BLK = 1024
MICRO = 2
ATT = 4
BLOCKS = 4
N_SHARD = 8


def dominant(key, shape, lower, upper, spread):
    size = shape[-1]
    diagonal = jnp.exp(jax.random.uniform(jax.random.fold_in(key, 3), shape[:-1], jnp.float32, math.log(lower), math.log(upper)))
    noise = jax.random.uniform(jax.random.fold_in(key, 5), shape, jnp.float32, -1.0, 1.0) * (spread * math.sqrt(1.5 / size))
    noise = noise + jnp.swapaxes(noise, -1, -2)
    row_ids = lax.broadcasted_iota(jnp.int32, shape, len(shape) - 2)
    col_ids = lax.broadcasted_iota(jnp.int32, shape, len(shape) - 1)
    return jnp.where(row_ids == col_ids, diagonal[..., None], noise)


def statistic(key, shape):
    return dominant(key, shape, 1.0, 3.0, 0.4)


def inverse_root(key, shape):
    return dominant(key, shape, 0.7, 1.4, 0.25).astype(jnp.bfloat16)


def owner_pair(key):
    order = jax.random.permutation(jax.random.fold_in(key, 17), N_SHARD).astype(jnp.int32)
    shared = jax.random.randint(jax.random.fold_in(key, 23), (), 1, ATT + 1).astype(jnp.int32)
    glu_part = lax.dynamic_slice_in_dim(order, ATT - shared, BLOCKS)
    return (order[:ATT], glu_part)


def draw_att_owner(key, part):
    return owner_pair(key)[0]


def draw_glu_owner(key, part):
    return owner_pair(key)[1]


def draw_att_stats(key, part):
    return statistic(jax.random.fold_in(key, 101), (N_SHARD, 2, D, D))


def draw_glu_left_stat(key, part):
    return statistic(jax.random.fold_in(key, 102), (N_SHARD, D, D))


def draw_glu_right_stat(key, part):
    return statistic(jax.random.fold_in(key, 103), (N_SHARD, BLK, BLK))


def draw_att_left_root(key, part):
    return inverse_root(jax.random.fold_in(key, 201), (N_SHARD, D, D))


def draw_att_right_root(key, part):
    return inverse_root(jax.random.fold_in(key, 202), (N_SHARD, D, D))


def draw_glu_left_root(key, part):
    return inverse_root(jax.random.fold_in(key, 203), (N_SHARD, D, D))


def draw_glu_right_root(key, part):
    return inverse_root(jax.random.fold_in(key, 204), (N_SHARD, BLK, BLK))


def block_scale(stream_key, dims, cuts, least, high):
    gain, own = 1.0, jax.random.fold_in(stream_key, 6)
    for position, parts in cuts:
        steps = jnp.exp(jax.random.uniform(jax.random.fold_in(own, position), (parts,), jnp.float32, least / len(cuts), high / len(cuts)))
        gain = gain * jnp.repeat(steps, dims[position] // parts).reshape([-1 if axis == position else 1 for axis in range(len(dims))])
    return gain


def scatter_about(stream_key, shape, width, reach, split=(), dtype=jnp.bfloat16):
    level = block_scale(stream_key, shape, split, -0.22, 0.18) if split else 1.0
    entries = jax.random.normal(stream_key, shape, jnp.float32) * width * level
    return jnp.minimum(jnp.maximum(entries, -reach), reach).astype(dtype)


def setup_inputs(seed: int = 0) -> dict:
    arg_keys = jax.random.split(jax.random.key(seed), 18)
    att_grads = scatter_about(arg_keys[0], (MICRO, ATT, D, D), 0.5, 6.0, ((2, 8), (3, 4)), jnp.float32)
    glu_grads = scatter_about(arg_keys[1], (MICRO, BLOCKS, D, BLK), 0.5, 6.0, ((2, 8), (3, 4)), jnp.float32)
    att_weight = scatter_about(arg_keys[2], (ATT, D, D), D ** -0.5, 0.21875, ((1, 8), (2, 4)), jnp.float32)
    att_moment = scatter_about(arg_keys[3], (ATT, D, D), 0.3, 4.0, ((1, 8), (2, 4)), jnp.float32)
    att_second = jnp.clip(jnp.exp(math.log(1.0) - 2.9957323 * jax.random.uniform(arg_keys[4], (ATT, D, D), jnp.float32) ** block_scale(arg_keys[4], (ATT, D, D), ((1, 8), (2, 4)), -0.2, 0.2)), 0.05, 1.0)
    glu_weight = scatter_about(arg_keys[5], (BLOCKS, D, BLK), D ** -0.5, 0.21875, ((1, 8), (2, 4)), jnp.float32)
    glu_moment = scatter_about(arg_keys[6], (BLOCKS, D, BLK), 0.3, 4.0, ((1, 8), (2, 4)), jnp.float32)
    glu_second = jnp.clip(jnp.exp(math.log(1.0) - 2.9957323 * jax.random.uniform(arg_keys[7], (BLOCKS, D, BLK), jnp.float32) ** block_scale(arg_keys[7], (BLOCKS, D, BLK), ((1, 8), (2, 4)), -0.2, 0.2)), 0.05, 1.0)
    att_stats = draw_att_stats(jax.random.fold_in(arg_keys[17], 71), 0)
    att_left_root = draw_att_left_root(jax.random.fold_in(arg_keys[17], 71), 0)
    att_right_root = draw_att_right_root(jax.random.fold_in(arg_keys[17], 71), 0)
    glu_left_stat = draw_glu_left_stat(jax.random.fold_in(arg_keys[17], 71), 0)
    glu_right_stat = draw_glu_right_stat(jax.random.fold_in(arg_keys[17], 71), 0)
    glu_left_root = draw_glu_left_root(jax.random.fold_in(arg_keys[17], 71), 0)
    glu_right_root = draw_glu_right_root(jax.random.fold_in(arg_keys[17], 71), 0)
    att_owner = draw_att_owner(jax.random.fold_in(arg_keys[17], 71), 0)
    glu_owner = draw_glu_owner(jax.random.fold_in(arg_keys[17], 71), 0)
    return {"att_grads": att_grads, "glu_grads": glu_grads, "att_weight": att_weight, "att_moment": att_moment, "att_second": att_second, "glu_weight": glu_weight, "glu_moment": glu_moment, "glu_second": glu_second, "att_stats": att_stats, "att_left_root": att_left_root, "att_right_root": att_right_root, "glu_left_stat": glu_left_stat, "glu_right_stat": glu_right_stat, "glu_left_root": glu_left_root, "glu_right_root": glu_right_root, "att_owner": att_owner, "glu_owner": glu_owner}


beta_one = 0.9
beta_two = 0.999
beta_stat = 0.999
adam_eps = 1e-08
graft_eps = 1e-06
learn_rate = 0.01
top_precision = lax.Precision.HIGHEST

def adam_part(grads, moment, second):
    summed = lax.optimization_barrier(jnp.sum(grads, axis=0))
    moment_new = beta_one * moment + (1.0 - beta_one) * summed
    second_new = beta_two * second + (1.0 - beta_two) * summed * summed
    direction = moment_new / (jnp.sqrt(second_new) + adam_eps)
    adam_sq = lax.optimization_barrier(jnp.sum(direction * direction, axis=(1, 2)))
    return (summed, moment_new, second_new, adam_sq)

def precondition(grad, left_stat, right_stat, left_root, right_root, adam_sq):
    left_new = beta_stat * left_stat + (1.0 - beta_stat) * jnp.dot(grad, grad.T, precision=top_precision)
    right_new = beta_stat * right_stat + (1.0 - beta_stat) * jnp.dot(grad.T, grad, precision=top_precision)
    halfway = jnp.dot(left_root, grad.astype(jnp.bfloat16), preferred_element_type=jnp.float32).astype(jnp.bfloat16)
    shampoo = jnp.dot(halfway, right_root, preferred_element_type=jnp.float32)
    scale = jnp.sqrt(adam_sq / (jnp.sum(shampoo * shampoo) + graft_eps))
    return (left_new, right_new, scale * shampoo)

def reference(att_grads, glu_grads, att_weight, att_moment, att_second, glu_weight, glu_moment, glu_second, att_stats, att_left_root, att_right_root, glu_left_stat, glu_right_stat, glu_left_root, glu_right_root, att_owner, glu_owner):
    att_sum, att_moment_out, att_second_out, att_adam = adam_part(att_grads, att_moment, att_second)
    glu_sum, glu_moment_out, glu_second_out, glu_adam = adam_part(glu_grads, glu_moment, glu_second)

    def att_unit(operands):
        grad, owner, adam_sq = operands
        stats = att_stats[owner]
        left_new, right_new, update = precondition(grad, stats[0], stats[1], att_left_root[owner], att_right_root[owner], adam_sq)
        return (jnp.stack([left_new, right_new]), update)

    def glu_unit(operands):
        grad, owner, adam_sq = operands
        return precondition(grad, glu_left_stat[owner], glu_right_stat[owner], glu_left_root[owner], glu_right_root[owner], adam_sq)
    att_new, att_update = lax.map(att_unit, (att_sum, att_owner, att_adam))
    glu_left_new, glu_right_new, glu_update = lax.map(glu_unit, (glu_sum, glu_owner, glu_adam))
    att_stats_out = att_stats.at[att_owner].set(att_new)
    glu_left_out = glu_left_stat.at[glu_owner].set(glu_left_new)
    glu_right_out = glu_right_stat.at[glu_owner].set(glu_right_new)
    att_weight_out = att_weight - learn_rate * att_update
    glu_weight_out = glu_weight - learn_rate * glu_update
    return (att_weight_out, att_moment_out, att_second_out, glu_weight_out, glu_moment_out, glu_second_out, att_stats_out, glu_left_out, glu_right_out)
```

```python
import functools

import jax
import jax.numpy as jnp
from jax import lax
from jax.experimental import pallas as pl
from jax.experimental.pallas import tpu as pltpu
from jax.sharding import PartitionSpec as P

beta_one = 0.9
beta_two = 0.999
beta_stat = 0.999
adam_eps = 1e-08
graft_eps = 1e-06
learn_rate = 0.01

bf16 = jnp.bfloat16
f32 = jnp.float32
LANES = 128
VMEM = pl.BlockSpec(memory_space=pltpu.VMEM)
SMEM = pl.BlockSpec(memory_space=pltpu.SMEM)


def round_up(value, step):
    return -(-value // step) * step


def packed_shape(rows, cols):
    lanes = round_up(cols, LANES)
    return (rows, lanes) if lanes > cols else (round_up(rows + 3, 8), cols)


def pieces(total, shape):
    full = jnp.full(shape, total, f32)
    high = full.astype(bf16).astype(f32)
    middle = (full - high).astype(bf16).astype(f32)
    low = full - high - middle
    row = lax.broadcasted_iota(jnp.int32, shape, 0)
    column = lax.broadcasted_iota(jnp.int32, shape, 1)
    value = jnp.where(row == 0, high, jnp.where(row == 1, middle, jnp.where(row == 2, low, 0.0)))
    return jnp.where(column == 0, value, 0.0).astype(bf16)


def adam_kernel(owner, grads, moment, second, packed, moment_out, second_out):
    rows, cols = moment.shape[1:]
    packed_rows, packed_cols = packed.shape[1:]
    packed[...] = jnp.zeros_like(packed)

    def unit(u, carry):
        summed = grads[0, u]
        for micro in range(1, grads.shape[0]):
            summed = summed + grads[micro, u]
        moment_new = beta_one * moment[u] + (1.0 - beta_one) * summed
        second_new = beta_two * second[u] + (1.0 - beta_two) * summed * summed
        direction = moment_new / (jnp.sqrt(second_new) + adam_eps)
        moment_out[u] = moment_new
        second_out[u] = second_new
        total = jnp.sum(direction * direction)
        slot = owner[u]
        if packed_cols > cols:
            packed[slot, :, :cols] = summed.astype(bf16)
            packed[slot, :, cols:] = pieces(total, (packed_rows, packed_cols - cols))
        else:
            packed[slot, :rows, :] = summed.astype(bf16)
            packed[slot, rows:, :] = pieces(total, (packed_rows - rows, packed_cols))
        return carry

    lax.fori_loop(0, moment.shape[0], unit, 0, unroll=moment.shape[0] <= 4)


def adam_part(owner, grads, moment, second, owners):
    rows, cols = moment.shape[1:]
    packed = jax.ShapeDtypeStruct((owners, *packed_shape(rows, cols)), bf16)
    return pl.pallas_call(
        adam_kernel,
        out_shape=(
            packed,
            jax.ShapeDtypeStruct(moment.shape, f32),
            jax.ShapeDtypeStruct(second.shape, f32),
        ),
        in_specs=[SMEM, VMEM, VMEM, VMEM],
        out_specs=(VMEM, VMEM, VMEM),
        cost_estimate=pl.CostEstimate(
            flops=20 * moment.size, bytes_accessed=32 * moment.size, transcendentals=moment.size
        ),
    )(owner, grads, moment, second)


def holds(owner):
    me = lax.axis_index("shard")
    found = owner[0] == me
    for unit in range(1, owner.shape[0]):
        found = jnp.logical_or(found, owner[unit] == me)
    return found


def block(ref, rows, cols, start=0, count=None):
    count = ref.shape[0] if count is None else count
    return ref[pl.ds(start, count), :rows, :cols].reshape(count * rows, cols)


def shampoo_kernel(rows, cols, owner, *refs):
    tensor = lax.axis_size("tensor")
    left, grad, (root, out, norm, adam, half) = refs[:tensor], refs[tensor : 2 * tensor], refs[2 * tensor :]
    part = lax.axis_index("tensor")

    @pl.when(holds(owner))
    def _():
        depth = left[0].shape[0]
        total = jnp.zeros(out.shape, f32)
        adam_sq = jnp.zeros((), f32)
        for k in range(tensor):
            columns = block(grad[k], rows, cols)
            for i in range(tensor):
                product = jnp.dot(left[i][...], columns, preferred_element_type=f32)
                place = pl.multiple_of((part ^ i) * depth, depth)
                half[k, pl.ds(place, depth), :] = product.astype(bf16)
            if grad[k].shape[2] > cols:
                extra = grad[k][:, :, cols:]
            else:
                extra = grad[k][:, rows:, :]
            adam_sq = adam_sq + jnp.sum(extra.astype(f32))
        for k in range(tensor):
            place = pl.multiple_of((part ^ k) * cols, cols)
            total = total + jnp.dot(
                half[k], root[0, pl.ds(place, cols), :], preferred_element_type=f32
            )
        out[...] = total
        norm[...] = jnp.full(norm.shape, jnp.sum(total * total), f32)
        adam[...] = jnp.full(adam.shape, adam_sq, f32)

    @pl.when(jnp.logical_not(holds(owner)))
    def _():
        out[...] = jnp.zeros_like(out)
        norm[...] = jnp.zeros_like(norm)
        adam[...] = jnp.zeros_like(adam)


def shampoo_part(owner, left, grad, root, rows):
    cols = root.shape[2]
    depth = left[0].shape[1]
    tensor = len(left)
    small = jax.ShapeDtypeStruct((8, LANES), f32)
    return pl.pallas_call(
        functools.partial(shampoo_kernel, rows, cols),
        out_shape=(jax.ShapeDtypeStruct((depth, cols), f32), small, small),
        in_specs=[SMEM] + [VMEM] * (2 * tensor + 1),
        out_specs=(VMEM, VMEM, VMEM),
        scratch_shapes=[pltpu.VMEM((tensor, depth, cols), bf16)],
        cost_estimate=pl.CostEstimate(
            flops=2 * depth * cols * tensor * (depth + cols),
            bytes_accessed=2 * depth * depth + 2 * depth * cols * tensor + 6 * depth * cols,
            transcendentals=0,
        ),
    )(owner, *left, *grad, root)


def stats_kernel(rows, cols, paired, owner, *refs):
    tensor = lax.axis_size("tensor")
    grad = refs[:tensor]
    if paired:
        stats, stats_out, square = refs[tensor:]
        left, right = stats.at[0, 0], stats.at[0, 1]
        left_out, right_out = stats_out.at[0, 0], stats_out.at[0, 1]
    else:
        left, right, left_out, right_out, square = refs[tensor:]
        left, right, left_out, right_out = left.at[0], right.at[0], left_out.at[0], right_out.at[0]
    part = lax.axis_index("tensor")

    @pl.when(holds(owner))
    def _():
        high = left.shape[0]
        total = jnp.zeros(left.shape, f32)
        mine = block(grad[0], rows, cols)
        for k in range(tensor):
            columns = block(grad[k], rows, cols)
            slots = high // rows
            band = block(grad[k], rows, cols, part * slots, slots)
            total = total + lax.dot_general(
                band, columns, (((1,), (1,)), ((), ())), preferred_element_type=f32
            )
            square[part ^ k] = lax.dot_general(
                mine, columns, (((0,), (0,)), ((), ())), preferred_element_type=f32
            )
        left_out[...] = beta_stat * left[...] + (1.0 - beta_stat) * total
        for k in range(tensor):
            span = slice(k * cols, (k + 1) * cols)
            right_out[:, span] = beta_stat * right[:, span] + (1.0 - beta_stat) * square[k]

    @pl.when(jnp.logical_not(holds(owner)))
    def _():
        left_out[...] = left[...]
        right_out[...] = right[...]


def stats_part(owner, grad, stats, rows, cols):
    tensor = len(grad)
    shapes = tuple(jax.ShapeDtypeStruct(s.shape, f32) for s in stats)
    depth = tensor * cols
    return pl.pallas_call(
        functools.partial(stats_kernel, rows, cols, len(stats) == 1),
        out_shape=shapes,
        in_specs=[SMEM] + [VMEM] * (tensor + len(stats)),
        out_specs=(VMEM,) * len(stats),
        scratch_shapes=[pltpu.VMEM((tensor, cols, cols), f32)],
        cost_estimate=pl.CostEstimate(
            flops=4 * depth * depth * cols,
            bytes_accessed=8 * sum(s.size for s in stats) + 2 * depth * depth,
            transcendentals=0,
        ),
    )(owner, *grad, *stats)


def weight_kernel(owner, weight, back, out):
    def unit(u, carry):
        out[u] = weight[u] - learn_rate * back[owner[u]].astype(f32)
        return carry

    lax.fori_loop(0, weight.shape[0], unit, 0, unroll=weight.shape[0] <= 4)


def weight_part(owner, weight, back):
    return pl.pallas_call(
        weight_kernel,
        out_shape=jax.ShapeDtypeStruct(weight.shape, f32),
        in_specs=[SMEM, VMEM, VMEM],
        out_specs=VMEM,
    )(owner, weight, back)


def flip(value, bits):
    size = lax.axis_size("tensor")
    return lax.ppermute(value, "tensor", [(i, i ^ bits) for i in range(size)])


def spread(value):
    blocks = [value]
    bit = lax.axis_size("tensor") // 2
    held = {0: value}
    while bit:
        for k in sorted(held):
            held[k | bit] = flip(held[k], bit)
        bit //= 2
    return [held[k] for k in range(len(held))]


def over_shard(value):
    return lax.all_to_all(value, "shard", split_axis=0, concat_axis=0, tiled=True)


def grafted(done, norm, adam, owners):
    bit = 1
    while bit < lax.axis_size("tensor"):
        norm = norm + flip(norm, bit)
        bit *= 2
    scale = jnp.sqrt(adam[0, 0] / (norm[0, 0] + graft_eps))
    return (scale * done).astype(bf16).reshape(owners, -1, done.shape[1])


def per_device(
    att_grads,
    glu_grads,
    att_weight,
    att_moment,
    att_second,
    glu_weight,
    glu_moment,
    glu_second,
    att_stats,
    att_left_root,
    att_right_root,
    glu_left_stat,
    glu_right_stat,
    glu_left_root,
    glu_right_root,
    att_owner,
    glu_owner,
):
    owners = lax.axis_size("shard")
    rows = att_weight.shape[1]
    att_packed, att_moment_out, att_second_out = adam_part(
        att_owner, att_grads, att_moment, att_second, owners
    )
    glu_packed, glu_moment_out, glu_second_out = adam_part(
        glu_owner, glu_grads, glu_moment, glu_second, owners
    )
    att_left = spread(att_left_root[0])
    glu_left = spread(glu_left_root[0])
    att_grad = spread(over_shard(att_packed))
    att_done, att_norm, att_adam = shampoo_part(att_owner, att_left, att_grad, att_right_root, rows)
    glu_grad = spread(over_shard(glu_packed))
    glu_done, glu_norm, glu_adam = shampoo_part(glu_owner, glu_left, glu_grad, glu_right_root, rows)
    att_back = over_shard(grafted(att_done, att_norm, att_adam, owners))
    glu_back = over_shard(grafted(glu_done, glu_norm, glu_adam, owners))
    (att_stats_out,) = stats_part(att_owner, att_grad, (att_stats,), rows, att_weight.shape[2])
    glu_left_out, glu_right_out = stats_part(
        glu_owner, glu_grad, (glu_left_stat, glu_right_stat), rows, glu_weight.shape[2]
    )
    att_weight_out = weight_part(att_owner, att_weight, att_back)
    glu_weight_out = weight_part(glu_owner, glu_weight, glu_back)
    return (
        att_weight_out,
        att_moment_out,
        att_second_out,
        glu_weight_out,
        glu_moment_out,
        glu_second_out,
        att_stats_out,
        glu_left_out,
        glu_right_out,
    )


def solution(mesh):
    placed = (
        P(None, None, "shard", "tensor"),
        P(None, None, "shard", "tensor"),
        P(None, "shard", "tensor"),
        P(None, "shard", "tensor"),
        P(None, "shard", "tensor"),
        P(None, "shard", "tensor"),
        P(None, "shard", "tensor"),
        P(None, "shard", "tensor"),
        P("shard", None, "tensor", None),
        P("shard", "tensor", None),
        P("shard", None, "tensor"),
        P("shard", "tensor", None),
        P("shard", "tensor", None),
        P("shard", "tensor", None),
        P("shard", None, "tensor"),
        P(),
        P(),
    )
    return jax.shard_map(
        per_device,
        mesh=mesh,
        in_specs=placed,
        out_specs=(
            P(None, "shard", "tensor"),
            P(None, "shard", "tensor"),
            P(None, "shard", "tensor"),
            P(None, "shard", "tensor"),
            P(None, "shard", "tensor"),
            P(None, "shard", "tensor"),
            P("shard", None, "tensor", None),
            P("shard", "tensor", None),
            P("shard", "tensor", None),
        ),
        check_vma=False,
    )
```

```python
import functools

import jax
import jax.numpy as jnp
from jax import lax
from jax.experimental import pallas as pl
from jax.experimental.pallas import tpu as pltpu
from jax.sharding import PartitionSpec as P

beta_one = 0.9
beta_two = 0.999
beta_stat = 0.999
adam_eps = 1e-08
graft_eps = 1e-06
learn_rate = 0.01

bf16 = jnp.bfloat16
f32 = jnp.float32
LANES = 128
VMEM = pl.BlockSpec(memory_space=pltpu.VMEM)
SMEM = pl.BlockSpec(memory_space=pltpu.SMEM)


def round_up(value, step):
    return -(-value // step) * step


def packed_shape(rows, cols):
    lanes = round_up(cols, LANES)
    return (rows, lanes) if lanes > cols else (round_up(rows + 3, 8), cols)


def pieces(total, shape):
    full = jnp.full(shape, total, f32)
    high = full.astype(bf16).astype(f32)
    middle = (full - high).astype(bf16).astype(f32)
    low = full - high - middle
    row = lax.broadcasted_iota(jnp.int32, shape, 0)
    column = lax.broadcasted_iota(jnp.int32, shape, 1)
    value = jnp.where(row == 0, high, jnp.where(row == 1, middle, jnp.where(row == 2, low, 0.0)))
    return jnp.where(column == 0, value, 0.0).astype(bf16)


def adam_kernel(direct, owner, grads, moment, second, *refs):
    packed, (moment_out, second_out, total) = refs[:-3], refs[-3:]
    units, rows, cols = moment.shape
    packed_rows, packed_cols = packed[0].shape[-2:]

    def block_sum(u):
        summed = grads[0, u]
        for micro in range(1, grads.shape[0]):
            summed = summed + grads[micro, u]
        return summed

    def unit(u, carry):
        summed = block_sum(u)
        moment_new = beta_one * moment[u] + (1.0 - beta_one) * summed
        second_new = beta_two * second[u] + (1.0 - beta_two) * summed * summed
        direction = moment_new / (jnp.sqrt(second_new) + adam_eps)
        moment_out[u] = moment_new
        second_out[u] = second_new
        total[u] = jnp.sum(direction * direction)
        return carry

    lax.fori_loop(0, units, unit, 0, unroll=units <= 4)

    def fill(target, u):
        if packed_cols > cols:
            target[:, :cols] = block_sum(u).astype(bf16)
            target[:, cols:] = pieces(total[u], (packed_rows, packed_cols - cols))
        else:
            target[:rows, :] = block_sum(u).astype(bf16)
            target[rows:, :] = pieces(total[u], (packed_rows - rows, packed_cols))

    if direct:
        me = lax.axis_index("shard")
        for k in range(len(packed)):
            found, index = held_by(owner, me ^ k)

            @pl.when(found)
            def _():
                fill(packed[k], index)

            @pl.when(jnp.logical_not(found))
            def _():
                packed[k][...] = jnp.zeros_like(packed[k])
    else:
        packed[0][...] = jnp.zeros_like(packed[0])

        def place(u, carry):
            fill(packed[0].at[owner[u]], u)
            return carry

        lax.fori_loop(0, units, place, 0)


def adam_part(owner, grads, moment, second, owners):
    rows, cols = moment.shape[1:]
    shape = packed_shape(rows, cols)
    if by_permutes(owners, rows):
        packed = [jax.ShapeDtypeStruct(shape, bf16)] * owners
    else:
        packed = [jax.ShapeDtypeStruct((owners, *shape), bf16)]
    *packed, moment_out, second_out = pl.pallas_call(
        functools.partial(adam_kernel, len(packed) > 1),
        out_shape=(
            *packed,
            jax.ShapeDtypeStruct(moment.shape, f32),
            jax.ShapeDtypeStruct(second.shape, f32),
        ),
        in_specs=[SMEM, VMEM, VMEM, VMEM],
        out_specs=(VMEM,) * (len(packed) + 2),
        scratch_shapes=[pltpu.SMEM((moment.shape[0],), f32)],
        cost_estimate=pl.CostEstimate(
            flops=20 * moment.size, bytes_accessed=32 * moment.size, transcendentals=moment.size
        ),
    )(owner, grads, moment, second)
    return packed, moment_out, second_out


def by_permutes(owners, rows):
    return owners <= 8 and owners & (owners - 1) == 0 and rows % 8 == 0


def cross(value, bits):
    size = lax.axis_size("shard")
    return lax.ppermute(value, "shard", [(i, i ^ bits) for i in range(size)])


def order_kernel(*refs):
    out = refs[-1]
    me = lax.axis_index("shard")
    for k, ref in enumerate(refs[:-1]):
        out[me ^ k] = ref[...]


def after(value, *others):
    return lax.optimization_barrier((value, *others))[0]


def gathered(packed, *others):
    packed = [after(packed[0], *others)] + list(packed[1:])
    if len(packed) == 1:
        return lax.all_to_all(packed[0], "shard", split_axis=0, concat_axis=0, tiled=True)
    arrived = [packed[0]] + [cross(packed[k], k) for k in range(1, len(packed))]
    shape = (len(packed), *packed[0].shape)
    return pl.pallas_call(
        order_kernel,
        out_shape=jax.ShapeDtypeStruct(shape, bf16),
        in_specs=[VMEM] * len(packed),
        out_specs=VMEM,
        cost_estimate=pl.CostEstimate(
            flops=0, bytes_accessed=4 * packed[0].size * len(packed), transcendentals=0
        ),
    )(*arrived)


def held_by(owner, place):
    found = owner[0] == place
    index = jnp.int32(0)
    for unit in range(1, owner.shape[0]):
        here = owner[unit] == place
        found = jnp.logical_or(found, here)
        index = jnp.where(here, unit, index)
    return found, index


def holds(owner):
    return held_by(owner, lax.axis_index("shard"))[0]


def block(ref, rows, cols, start=0, count=None):
    count = ref.shape[0] if count is None else count
    return ref[pl.ds(start, count), :rows, :cols].reshape(count * rows, cols)


def shampoo_kernel(rows, cols, owner, *refs):
    tensor = lax.axis_size("tensor")
    left, grad, (root, out, norm, adam, half) = refs[0], refs[1 : tensor + 1], refs[tensor + 1 :]
    part = lax.axis_index("tensor")

    @pl.when(holds(owner))
    def _():
        total = jnp.zeros(out.shape, f32)
        adam_sq = jnp.zeros((), f32)
        for k in range(tensor):
            columns = block(grad[k], rows, cols)
            half[k] = jnp.dot(left[...], columns, preferred_element_type=f32).astype(bf16)
            if grad[k].shape[2] > cols:
                extra = grad[k][:, :, cols:]
            else:
                extra = grad[k][:, rows:, :]
            adam_sq = adam_sq + jnp.sum(extra.astype(f32))
        for k in range(tensor):
            place = pl.multiple_of((part ^ k) * cols, cols)
            total = total + jnp.dot(
                half[k], root[0, pl.ds(place, cols), :], preferred_element_type=f32
            )
        out[...] = total
        norm[...] = jnp.full(norm.shape, jnp.sum(total * total), f32)
        adam[...] = jnp.full(adam.shape, adam_sq, f32)

    @pl.when(jnp.logical_not(holds(owner)))
    def _():
        out[...] = jnp.zeros_like(out)
        norm[...] = jnp.zeros_like(norm)
        adam[...] = jnp.zeros_like(adam)


def shampoo_part(owner, left, grad, root, rows):
    cols = root.shape[2]
    depth = left.shape[1]
    tensor = len(grad)
    small = jax.ShapeDtypeStruct((8, LANES), f32)
    return pl.pallas_call(
        functools.partial(shampoo_kernel, rows, cols),
        out_shape=(jax.ShapeDtypeStruct((depth, cols), f32), small, small),
        in_specs=[SMEM] + [VMEM] * (tensor + 2),
        out_specs=(VMEM, VMEM, VMEM),
        scratch_shapes=[pltpu.VMEM((tensor, depth, cols), bf16)],
        cost_estimate=pl.CostEstimate(
            flops=2 * depth * cols * tensor * (depth + cols),
            bytes_accessed=2 * depth * depth + 2 * depth * cols * tensor + 6 * depth * cols,
            transcendentals=0,
        ),
    )(owner, left, *grad, root)


def stats_kernel(rows, cols, paired, owner, *refs):
    tensor = lax.axis_size("tensor")
    grad = refs[:tensor]
    if paired:
        stats, stats_out, square = refs[tensor:]
        left, right = stats.at[0, 0], stats.at[0, 1]
        left_out, right_out = stats_out.at[0, 0], stats_out.at[0, 1]
    else:
        left, right, left_out, right_out, square = refs[tensor:]
        left, right, left_out, right_out = left.at[0], right.at[0], left_out.at[0], right_out.at[0]
    part = lax.axis_index("tensor")

    @pl.when(holds(owner))
    def _():
        high = left.shape[0]
        total = jnp.zeros(left.shape, f32)
        mine = block(grad[0], rows, cols)
        for k in range(tensor):
            columns = block(grad[k], rows, cols)
            slots = high // rows
            band = block(grad[k], rows, cols, part * slots, slots)
            total = total + lax.dot_general(
                band, columns, (((1,), (1,)), ((), ())), preferred_element_type=f32
            )
            square[part ^ k] = lax.dot_general(
                mine, columns, (((0,), (0,)), ((), ())), preferred_element_type=f32
            )
        left_out[...] = beta_stat * left[...] + (1.0 - beta_stat) * total
        for k in range(tensor):
            span = slice(k * cols, (k + 1) * cols)
            right_out[:, span] = beta_stat * right[:, span] + (1.0 - beta_stat) * square[k]

    @pl.when(jnp.logical_not(holds(owner)))
    def _():
        left_out[...] = left[...]
        right_out[...] = right[...]


def stats_part(owner, grad, stats, rows, cols):
    tensor = len(grad)
    shapes = tuple(jax.ShapeDtypeStruct(s.shape, f32) for s in stats)
    depth = tensor * cols
    return pl.pallas_call(
        functools.partial(stats_kernel, rows, cols, len(stats) == 1),
        out_shape=shapes,
        in_specs=[SMEM] + [VMEM] * (tensor + len(stats)),
        out_specs=(VMEM,) * len(stats),
        scratch_shapes=[pltpu.VMEM((tensor, cols, cols), f32)],
        cost_estimate=pl.CostEstimate(
            flops=4 * depth * depth * cols,
            bytes_accessed=8 * sum(s.size for s in stats) + 2 * depth * depth,
            transcendentals=0,
        ),
    )(owner, *grad, *stats)


def weight_kernel(owner, weight, *refs):
    back, out = refs[:-1], refs[-1]
    if len(back) == 1:

        def unit(u, carry):
            out[u] = weight[u] - learn_rate * back[0][owner[u]].astype(f32)
            return carry

        lax.fori_loop(0, weight.shape[0], unit, 0)
        return
    me = lax.axis_index("shard")
    for k, ref in enumerate(back):
        found, index = held_by(owner, me ^ k)

        @pl.when(found)
        def _():
            out[index] = weight[index] - learn_rate * ref[...].astype(f32)


def weight_part(owner, weight, back):
    return pl.pallas_call(
        weight_kernel,
        out_shape=jax.ShapeDtypeStruct(weight.shape, f32),
        in_specs=[SMEM] + [VMEM] * (1 + len(back)),
        out_specs=VMEM,
        cost_estimate=pl.CostEstimate(
            flops=2 * weight.size, bytes_accessed=12 * weight.size, transcendentals=0
        ),
    )(owner, weight, *back)


def flip(value, bits):
    size = lax.axis_size("tensor")
    return lax.ppermute(value, "tensor", [(i, i ^ bits) for i in range(size)])


def spread(value):
    return spread_rest(*spread_first(value))


def spread_first(value):
    return value, flip(value, lax.axis_size("tensor") // 2)


def spread_rest(value, far):
    bit = lax.axis_size("tensor") // 2
    held = {0: value, bit: far}
    bit //= 2
    while bit:
        for k in sorted(held):
            held[k | bit] = flip(held[k], bit)
        bit //= 2
    return [held[k] for k in range(len(held))]


def rows_kernel(*refs):
    out, part = refs[-1], lax.axis_index("tensor")
    depth = refs[0].shape[0]
    for k, ref in enumerate(refs[:-1]):
        out[pl.ds(pl.multiple_of((part ^ k) * depth, depth), depth), :] = ref[...]


def whole_root(rows, far):
    parts = spread_rest(rows, far)
    shape = (rows.shape[0] * len(parts), rows.shape[1])
    return pl.pallas_call(
        rows_kernel,
        out_shape=jax.ShapeDtypeStruct(shape, bf16),
        in_specs=[VMEM] * len(parts),
        out_specs=VMEM,
        cost_estimate=pl.CostEstimate(
            flops=0, bytes_accessed=4 * rows.size * len(parts), transcendentals=0
        ),
    )(*parts)


def scale_kernel(direct, done, adam, *refs):
    tensor = lax.axis_size("tensor")
    norm, out = refs[:tensor], refs[tensor:]
    total = norm[0][...]
    for other in norm[1:]:
        total = total + other[...]
    scale = jnp.sqrt(adam[...] / (total + graft_eps))[0, 0]
    if not direct:
        out[0][...] = (scale * done[...]).astype(bf16)
        return
    me = lax.axis_index("shard")
    for k, ref in enumerate(out):
        rows = ref.shape[0]
        ref[...] = (scale * done[pl.ds(pl.multiple_of((me ^ k) * rows, rows), rows), :]).astype(bf16)


def grafted(done, norm, adam, owners):
    depth, cols = done.shape
    rows = depth // owners
    norms = [norm] + [flip(norm, k) for k in range(1, lax.axis_size("tensor"))]
    direct = by_permutes(owners, rows)
    shapes = [(rows, cols)] * owners if direct else [done.shape]
    out = pl.pallas_call(
        functools.partial(scale_kernel, direct),
        out_shape=tuple(jax.ShapeDtypeStruct(shape, bf16) for shape in shapes),
        in_specs=[VMEM] * (2 + len(norms)),
        out_specs=(VMEM,) * len(shapes),
        cost_estimate=pl.CostEstimate(
            flops=done.size, bytes_accessed=6 * done.size, transcendentals=0
        ),
    )(done, adam, *norms)
    return out if direct else [out[0].reshape(owners, rows, cols)]


def returned(out):
    if len(out) > 1:
        return [out[0]] + [cross(out[k], k) for k in range(1, len(out))]
    return [lax.all_to_all(out[0], "shard", split_axis=0, concat_axis=0, tiled=True)]


def per_device(
    att_grads,
    glu_grads,
    att_weight,
    att_moment,
    att_second,
    glu_weight,
    glu_moment,
    glu_second,
    att_stats,
    att_left_root,
    att_right_root,
    glu_left_stat,
    glu_right_stat,
    glu_left_root,
    glu_right_root,
    att_owner,
    glu_owner,
):
    owners = lax.axis_size("shard")
    rows = att_weight.shape[1]
    att_packed, att_moment_out, att_second_out = adam_part(
        att_owner, att_grads, att_moment, att_second, owners
    )
    glu_packed, glu_moment_out, glu_second_out = adam_part(
        glu_owner, glu_grads, glu_moment, glu_second, owners
    )
    att_root, att_root_far = spread_first(att_left_root[0])
    glu_root, glu_root_far = spread_first(glu_left_root[0])
    att_near, att_far = spread_first(gathered(att_packed, att_root_far, glu_root_far))
    att_left = whole_root(att_root, att_root_far)
    att_grad = spread_rest(att_near, att_far)
    att_done, att_norm, att_adam = shampoo_part(att_owner, att_left, att_grad, att_right_root, rows)
    glu_left = whole_root(glu_root, glu_root_far)
    glu_near, glu_far = spread_first(gathered(glu_packed, att_far))
    att_send = grafted(att_done, att_norm, att_adam, owners)
    glu_grad = spread_rest(glu_near, after(glu_far, att_send[0]))
    att_back = returned(att_send)
    glu_done, glu_norm, glu_adam = shampoo_part(glu_owner, glu_left, glu_grad, glu_right_root, rows)
    glu_back = returned(grafted(glu_done, glu_norm, glu_adam, owners))
    (att_stats_out,) = stats_part(att_owner, att_grad, (att_stats,), rows, att_weight.shape[2])
    glu_left_out, glu_right_out = stats_part(
        glu_owner, glu_grad, (glu_left_stat, glu_right_stat), rows, glu_weight.shape[2]
    )
    att_weight_out = weight_part(att_owner, att_weight, att_back)
    glu_weight_out = weight_part(glu_owner, glu_weight, glu_back)
    return (
        att_weight_out,
        att_moment_out,
        att_second_out,
        glu_weight_out,
        glu_moment_out,
        glu_second_out,
        att_stats_out,
        glu_left_out,
        glu_right_out,
    )


def solution(mesh):
    placed = (
        P(None, None, "shard", "tensor"),
        P(None, None, "shard", "tensor"),
        P(None, "shard", "tensor"),
        P(None, "shard", "tensor"),
        P(None, "shard", "tensor"),
        P(None, "shard", "tensor"),
        P(None, "shard", "tensor"),
        P(None, "shard", "tensor"),
        P("shard", None, "tensor", None),
        P("shard", "tensor", None),
        P("shard", None, "tensor"),
        P("shard", "tensor", None),
        P("shard", "tensor", None),
        P("shard", "tensor", None),
        P("shard", None, "tensor"),
        P(),
        P(),
    )
    return jax.shard_map(
        per_device,
        mesh=mesh,
        in_specs=placed,
        out_specs=(
            P(None, "shard", "tensor"),
            P(None, "shard", "tensor"),
            P(None, "shard", "tensor"),
            P(None, "shard", "tensor"),
            P(None, "shard", "tensor"),
            P(None, "shard", "tensor"),
            P("shard", None, "tensor", None),
            P("shard", "tensor", None),
            P("shard", "tensor", None),
        ),
        check_vma=False,
    )
```

```python
import functools

import jax
import jax.numpy as jnp
from jax import lax
from jax.experimental import pallas as pl
from jax.experimental.pallas import tpu as pltpu
from jax.sharding import PartitionSpec as P

beta_one = 0.9
beta_two = 0.999
beta_stat = 0.999
adam_eps = 1e-08
graft_eps = 1e-06
learn_rate = 0.01

bf16 = jnp.bfloat16
f32 = jnp.float32
LANES = 128
VMEM = pl.BlockSpec(memory_space=pltpu.VMEM)
LIMIT = pltpu.CompilerParams(vmem_limit_bytes=16 << 20)
SMEM = pl.BlockSpec(memory_space=pltpu.SMEM)


def round_up(value, step):
    return -(-value // step) * step


def packed_shape(rows, cols):
    lanes = round_up(cols, LANES)
    return (rows, lanes) if lanes > cols else (round_up(rows + 3, 8), cols)


def pieces(total, shape):
    full = jnp.broadcast_to(total, shape)
    high = full.astype(bf16).astype(f32)
    middle = (full - high).astype(bf16).astype(f32)
    low = full - high - middle
    row = lax.broadcasted_iota(jnp.int32, shape, 0)
    column = lax.broadcasted_iota(jnp.int32, shape, 1)
    value = jnp.where(row == 0, high, jnp.where(row == 1, middle, jnp.where(row == 2, low, 0.0)))
    return jnp.where(column == 0, value, 0.0).astype(bf16)


def adam_kernel(owner, grads, moment, second, packed, moment_out, second_out):
    rows, cols = moment.shape[1:]
    packed_rows, packed_cols = packed.shape[1:]
    packed[...] = jnp.zeros_like(packed)

    def unit(u, carry):
        summed = grads[0, u]
        for micro in range(1, grads.shape[0]):
            summed = summed + grads[micro, u]
        moment_new = beta_one * moment[u] + (1.0 - beta_one) * summed
        second_new = beta_two * second[u] + (1.0 - beta_two) * summed * summed
        direction = moment_new / (jnp.sqrt(second_new) + adam_eps)
        moment_out[u] = moment_new
        second_out[u] = second_new
        total = jnp.sum(direction * direction, axis=(0, 1), keepdims=True)
        slot = owner[u]
        if packed_cols > cols:
            packed[slot, :, :cols] = summed.astype(bf16)
            packed[slot, :, cols:] = pieces(total, (packed_rows, packed_cols - cols))
        else:
            packed[slot, :rows, :] = summed.astype(bf16)
            packed[slot, rows:, :] = pieces(total, (packed_rows - rows, packed_cols))
        return carry

    lax.fori_loop(0, moment.shape[0], unit, 0, unroll=moment.shape[0] <= 4)


def adam_part(owner, grads, moment, second, owners):
    rows, cols = moment.shape[1:]
    packed = jax.ShapeDtypeStruct((owners, *packed_shape(rows, cols)), bf16)
    return pl.pallas_call(
        adam_kernel,
        out_shape=(
            packed,
            jax.ShapeDtypeStruct(moment.shape, f32),
            jax.ShapeDtypeStruct(second.shape, f32),
        ),
        in_specs=[SMEM, VMEM, VMEM, VMEM],
        out_specs=(VMEM, VMEM, VMEM),
        compiler_params=LIMIT,
        cost_estimate=pl.CostEstimate(
            flops=20 * moment.size, bytes_accessed=32 * moment.size, transcendentals=moment.size
        ),
    )(owner, grads, moment, second)


def holds(owner):
    me = lax.axis_index("shard")
    found = owner[0] == me
    for unit in range(1, owner.shape[0]):
        found = jnp.logical_or(found, owner[unit] == me)
    return found


def block(ref, rows, cols, start=0, count=None):
    count = ref.shape[0] if count is None else count
    return ref[pl.ds(start, count), :rows, :cols].reshape(count * rows, cols)


def shampoo_kernel(rows, cols, owner, *refs):
    tensor = lax.axis_size("tensor")
    left, grad, (root, out, norm, adam, whole, half) = refs[:tensor], refs[tensor : 2 * tensor], refs[2 * tensor :]
    part = lax.axis_index("tensor")

    @pl.when(holds(owner))
    def _():
        depth = left[0].shape[0]
        for i in range(tensor):
            place = pl.multiple_of((part ^ i) * depth, depth)
            whole[pl.ds(place, depth), :] = left[i][...]
        total = jnp.zeros(out.shape, f32)
        adam_sq = jnp.zeros((), f32)
        for k in range(tensor):
            columns = block(grad[k], rows, cols)
            half[k] = jnp.dot(whole[...], columns, preferred_element_type=f32).astype(bf16)
            if grad[k].shape[2] > cols:
                extra = grad[k][:, :, cols:]
            else:
                extra = grad[k][:, rows:, :]
            adam_sq = adam_sq + jnp.sum(extra.astype(f32))
        for k in range(tensor):
            place = pl.multiple_of((part ^ k) * cols, cols)
            total = total + jnp.dot(
                half[k], root[0, pl.ds(place, cols), :], preferred_element_type=f32
            )
        out[...] = total
        norm[...] = jnp.full(norm.shape, jnp.sum(total * total), f32)
        adam[...] = jnp.full(adam.shape, adam_sq, f32)

    @pl.when(jnp.logical_not(holds(owner)))
    def _():
        out[...] = jnp.zeros_like(out)
        norm[...] = jnp.zeros_like(norm)
        adam[...] = jnp.zeros_like(adam)


def shampoo_part(owner, left, grad, root, rows):
    cols = root.shape[2]
    depth = left[0].shape[1]
    tensor = len(left)
    small = jax.ShapeDtypeStruct((8, LANES), f32)
    return pl.pallas_call(
        functools.partial(shampoo_kernel, rows, cols),
        out_shape=(jax.ShapeDtypeStruct((depth, cols), f32), small, small),
        in_specs=[SMEM] + [VMEM] * (2 * tensor + 1),
        out_specs=(VMEM, VMEM, VMEM),
        scratch_shapes=[pltpu.VMEM((depth, depth), bf16), pltpu.VMEM((tensor, depth, cols), bf16)],
        compiler_params=LIMIT,
        cost_estimate=pl.CostEstimate(
            flops=2 * depth * cols * tensor * (depth + cols),
            bytes_accessed=2 * depth * depth + 2 * depth * cols * tensor + 6 * depth * cols,
            transcendentals=0,
        ),
    )(owner, *left, *grad, root)


def stats_kernel(rows, cols, paired, owner, *refs):
    tensor = lax.axis_size("tensor")
    grad = refs[:tensor]
    if paired:
        stats, stats_out, square = refs[tensor:]
        left, right = stats.at[0, 0], stats.at[0, 1]
        left_out, right_out = stats_out.at[0, 0], stats_out.at[0, 1]
    else:
        left, right, left_out, right_out, square = refs[tensor:]
        left, right, left_out, right_out = left.at[0], right.at[0], left_out.at[0], right_out.at[0]
    part = lax.axis_index("tensor")

    @pl.when(holds(owner))
    def _():
        high = left.shape[0]
        total = jnp.zeros(left.shape, f32)
        mine = block(grad[0], rows, cols)
        for k in range(tensor):
            columns = block(grad[k], rows, cols)
            slots = high // rows
            band = block(grad[k], rows, cols, part * slots, slots)
            total = total + lax.dot_general(
                band, columns, (((1,), (1,)), ((), ())), preferred_element_type=f32
            )
            square[part ^ k] = lax.dot_general(
                mine, columns, (((0,), (0,)), ((), ())), preferred_element_type=f32
            )
        left_out[...] = beta_stat * left[...] + (1.0 - beta_stat) * total
        for k in range(tensor):
            span = slice(k * cols, (k + 1) * cols)
            right_out[:, span] = beta_stat * right[:, span] + (1.0 - beta_stat) * square[k]

    @pl.when(jnp.logical_not(holds(owner)))
    def _():
        left_out[...] = left[...]
        right_out[...] = right[...]


def stats_part(owner, grad, stats, rows, cols):
    tensor = len(grad)
    shapes = tuple(jax.ShapeDtypeStruct(s.shape, f32) for s in stats)
    depth = tensor * cols
    return pl.pallas_call(
        functools.partial(stats_kernel, rows, cols, len(stats) == 1),
        out_shape=shapes,
        in_specs=[SMEM] + [VMEM] * (tensor + len(stats)),
        out_specs=(VMEM,) * len(stats),
        scratch_shapes=[pltpu.VMEM((tensor, cols, cols), f32)],
        compiler_params=LIMIT,
        cost_estimate=pl.CostEstimate(
            flops=4 * depth * depth * cols,
            bytes_accessed=8 * sum(s.size for s in stats) + 2 * depth * depth,
            transcendentals=0,
        ),
    )(owner, *grad, *stats)


def weight_kernel(owner, weight, back, out):
    def unit(u, carry):
        out[u] = weight[u] - learn_rate * back[owner[u]].astype(f32)
        return carry

    lax.fori_loop(0, weight.shape[0], unit, 0, unroll=weight.shape[0] <= 4)


def weight_part(owner, weight, back):
    return pl.pallas_call(
        weight_kernel,
        out_shape=jax.ShapeDtypeStruct(weight.shape, f32),
        in_specs=[SMEM, VMEM, VMEM],
        out_specs=VMEM,
        compiler_params=LIMIT,
        cost_estimate=pl.CostEstimate(
            flops=2 * weight.size, bytes_accessed=12 * weight.size, transcendentals=0
        ),
    )(owner, weight, back)


def flip(value, bits):
    size = lax.axis_size("tensor")
    return lax.ppermute(value, "tensor", [(i, i ^ bits) for i in range(size)])


def spread_first(value):
    return value, flip(value, lax.axis_size("tensor") // 2)


def spread_rest(value, far):
    bit = lax.axis_size("tensor") // 2
    held = {0: value, bit: far}
    bit //= 2
    while bit:
        for k in sorted(held):
            held[k | bit] = flip(held[k], bit)
        bit //= 2
    return [held[k] for k in range(len(held))]


def after(value, *others):
    return lax.optimization_barrier((value, *others))[0]


def over_shard(value):
    return lax.all_to_all(value, "shard", split_axis=0, concat_axis=0, tiled=True)


def scale_kernel(done, adam, *refs):
    norm, out = refs[:-1], refs[-1]
    total = norm[0][...]
    for other in norm[1:]:
        total = total + other[...]
    scale = jnp.sqrt(adam[...] / (total + graft_eps))[:1, :1]
    out[...] = (scale * done[...]).astype(bf16)


def grafted(done, norm, adam, owners):
    norms = [norm] + [flip(norm, k) for k in range(1, lax.axis_size("tensor"))]
    out = pl.pallas_call(
        scale_kernel,
        out_shape=jax.ShapeDtypeStruct(done.shape, bf16),
        in_specs=[VMEM] * (2 + len(norms)),
        out_specs=VMEM,
        compiler_params=LIMIT,
        cost_estimate=pl.CostEstimate(
            flops=done.size, bytes_accessed=6 * done.size, transcendentals=0
        ),
    )(done, adam, *norms)
    return out.reshape(owners, -1, done.shape[1])


def per_device(
    att_grads,
    glu_grads,
    att_weight,
    att_moment,
    att_second,
    glu_weight,
    glu_moment,
    glu_second,
    att_stats,
    att_left_root,
    att_right_root,
    glu_left_stat,
    glu_right_stat,
    glu_left_root,
    glu_right_root,
    att_owner,
    glu_owner,
):
    owners = lax.axis_size("shard")
    rows = att_weight.shape[1]
    att_packed, att_moment_out, att_second_out = adam_part(
        att_owner, att_grads, att_moment, att_second, owners
    )
    glu_packed, glu_moment_out, glu_second_out = adam_part(
        glu_owner, glu_grads, glu_moment, glu_second, owners
    )
    att_root, att_root_far = spread_first(att_left_root[0])
    glu_root, glu_root_far = spread_first(glu_left_root[0])
    att_left = spread_rest(att_root, att_root_far)
    glu_left = spread_rest(glu_root, glu_root_far)
    att_near, att_far = spread_first(
        after(over_shard(att_packed), *att_left[1:], glu_root_far, glu_packed)
    )
    att_grad = spread_rest(att_near, att_far)
    att_done, att_norm, att_adam = shampoo_part(att_owner, att_left, att_grad, att_right_root, rows)
    glu_near, glu_far = spread_first(after(over_shard(glu_packed), att_done, *glu_left[1:]))
    att_send = grafted(att_done, att_norm, att_adam, owners)
    glu_grad = spread_rest(glu_near, after(glu_far, att_send))
    att_back = over_shard(att_send)
    glu_done, glu_norm, glu_adam = shampoo_part(glu_owner, glu_left, glu_grad, glu_right_root, rows)
    glu_back = over_shard(grafted(glu_done, glu_norm, glu_adam, owners))
    (att_stats_out,) = stats_part(att_owner, att_grad, (att_stats,), rows, att_weight.shape[2])
    glu_left_out, glu_right_out = stats_part(
        glu_owner, glu_grad, (glu_left_stat, glu_right_stat), rows, glu_weight.shape[2]
    )
    att_weight_out = weight_part(att_owner, att_weight, att_back)
    glu_weight_out = weight_part(glu_owner, glu_weight, glu_back)
    return (
        att_weight_out,
        att_moment_out,
        att_second_out,
        glu_weight_out,
        glu_moment_out,
        glu_second_out,
        att_stats_out,
        glu_left_out,
        glu_right_out,
    )


def solution(mesh):
    placed = (
        P(None, None, "shard", "tensor"),
        P(None, None, "shard", "tensor"),
        P(None, "shard", "tensor"),
        P(None, "shard", "tensor"),
        P(None, "shard", "tensor"),
        P(None, "shard", "tensor"),
        P(None, "shard", "tensor"),
        P(None, "shard", "tensor"),
        P("shard", None, "tensor", None),
        P("shard", "tensor", None),
        P("shard", None, "tensor"),
        P("shard", "tensor", None),
        P("shard", "tensor", None),
        P("shard", "tensor", None),
        P("shard", None, "tensor"),
        P(),
        P(),
    )
    return jax.shard_map(
        per_device,
        mesh=mesh,
        in_specs=placed,
        out_specs=(
            P(None, "shard", "tensor"),
            P(None, "shard", "tensor"),
            P(None, "shard", "tensor"),
            P(None, "shard", "tensor"),
            P(None, "shard", "tensor"),
            P(None, "shard", "tensor"),
            P("shard", None, "tensor", None),
            P("shard", "tensor", None),
            P("shard", "tensor", None),
        ),
        check_vma=False,
    )
```

```python
import functools

import jax
import jax.numpy as jnp
from jax import lax
from jax.experimental import pallas as pl
from jax.experimental.pallas import tpu as pltpu
from jax.sharding import PartitionSpec as P

beta_one = 0.9
beta_two = 0.999
beta_stat = 0.999
adam_eps = 1e-08
graft_eps = 1e-06
learn_rate = 0.01

bf16 = jnp.bfloat16
f32 = jnp.float32
LANES = 128
VMEM = pl.BlockSpec(memory_space=pltpu.VMEM)
BRIEF = pl.CostEstimate(flops=1024, bytes_accessed=1024, transcendentals=0)
LIMIT = pltpu.CompilerParams(vmem_limit_bytes=16 << 20)
SMEM = pl.BlockSpec(memory_space=pltpu.SMEM)


def round_up(value, step):
    return -(-value // step) * step


def packed_shape(rows, cols):
    lanes = round_up(cols, LANES)
    return (rows, lanes) if lanes > cols else (round_up(rows + 3, 8), cols)


def pieces(total, shape):
    full = jnp.broadcast_to(total, shape)
    high = full.astype(bf16).astype(f32)
    middle = (full - high).astype(bf16).astype(f32)
    low = full - high - middle
    row = lax.broadcasted_iota(jnp.int32, shape, 0)
    column = lax.broadcasted_iota(jnp.int32, shape, 1)
    value = jnp.where(row == 0, high, jnp.where(row == 1, middle, jnp.where(row == 2, low, 0.0)))
    return jnp.where(column == 0, value, 0.0).astype(bf16)


def adam_kernel(owner, grads, moment, second, packed, moment_out, second_out):
    rows, cols = moment.shape[1:]
    packed_rows, packed_cols = packed.shape[1:]
    packed[...] = jnp.zeros_like(packed)

    def unit(u, carry):
        summed = grads[0, u]
        for micro in range(1, grads.shape[0]):
            summed = summed + grads[micro, u]
        moment_new = beta_one * moment[u] + (1.0 - beta_one) * summed
        second_new = beta_two * second[u] + (1.0 - beta_two) * summed * summed
        direction = moment_new / (jnp.sqrt(second_new) + adam_eps)
        moment_out[u] = moment_new
        second_out[u] = second_new
        total = jnp.sum(direction * direction, axis=(0, 1), keepdims=True)
        slot = owner[u]
        if packed_cols > cols:
            packed[slot, :, :cols] = summed.astype(bf16)
            packed[slot, :, cols:] = pieces(total, (packed_rows, packed_cols - cols))
        else:
            packed[slot, :rows, :] = summed.astype(bf16)
            packed[slot, rows:, :] = pieces(total, (packed_rows - rows, packed_cols))
        return carry

    lax.fori_loop(0, moment.shape[0], unit, 0, unroll=moment.shape[0] <= 4)


def adam_part(owner, grads, moment, second, owners, params):
    rows, cols = moment.shape[1:]
    packed = jax.ShapeDtypeStruct((owners, *packed_shape(rows, cols)), bf16)
    return pl.pallas_call(
        adam_kernel,
        out_shape=(
            packed,
            jax.ShapeDtypeStruct(moment.shape, f32),
            jax.ShapeDtypeStruct(second.shape, f32),
        ),
        in_specs=[SMEM, VMEM, VMEM, VMEM],
        out_specs=(VMEM, VMEM, VMEM),
        compiler_params=params,
        cost_estimate=pl.CostEstimate(
            flops=20 * moment.size, bytes_accessed=32 * moment.size, transcendentals=moment.size
        ),
    )(owner, grads, moment, second)


def holds(owner):
    me = lax.axis_index("shard")
    found = owner[0] == me
    for unit in range(1, owner.shape[0]):
        found = jnp.logical_or(found, owner[unit] == me)
    return found


def block(ref, rows, cols, start=0, count=None):
    count = ref.shape[0] if count is None else count
    return ref[pl.ds(start, count), :rows, :cols].reshape(count * rows, cols)


def shampoo_kernel(rows, cols, owner, *refs):
    tensor = lax.axis_size("tensor")
    left, grad, (root, out, norm, adam, whole, half) = refs[:tensor], refs[tensor : 2 * tensor], refs[2 * tensor :]
    part = lax.axis_index("tensor")

    @pl.when(holds(owner))
    def _():
        depth = left[0].shape[0]
        for i in range(tensor):
            place = pl.multiple_of((part ^ i) * depth, depth)
            whole[pl.ds(place, depth), :] = left[i][...]
        total = jnp.zeros(out.shape, f32)
        adam_sq = jnp.zeros((), f32)
        for k in range(tensor):
            columns = block(grad[k], rows, cols)
            half[k] = jnp.dot(whole[...], columns, preferred_element_type=f32).astype(bf16)
            if grad[k].shape[2] > cols:
                extra = grad[k][:, :, cols:]
            else:
                extra = grad[k][:, rows:, :]
            adam_sq = adam_sq + jnp.sum(extra.astype(f32))
        for k in range(tensor):
            place = pl.multiple_of((part ^ k) * cols, cols)
            total = total + jnp.dot(
                half[k], root[0, pl.ds(place, cols), :], preferred_element_type=f32
            )
        out[...] = total
        norm[...] = jnp.full(norm.shape, jnp.sum(total * total), f32)
        adam[...] = jnp.full(adam.shape, adam_sq, f32)

    @pl.when(jnp.logical_not(holds(owner)))
    def _():
        out[...] = jnp.zeros_like(out)
        norm[...] = jnp.zeros_like(norm)
        adam[...] = jnp.zeros_like(adam)


def shampoo_part(owner, left, grad, root, rows):
    cols = root.shape[2]
    depth = left[0].shape[1]
    tensor = len(left)
    small = jax.ShapeDtypeStruct((8, LANES), f32)
    return pl.pallas_call(
        functools.partial(shampoo_kernel, rows, cols),
        out_shape=(jax.ShapeDtypeStruct((depth, cols), f32), small, small),
        in_specs=[SMEM] + [VMEM] * (2 * tensor + 1),
        out_specs=(VMEM, VMEM, VMEM),
        scratch_shapes=[pltpu.VMEM((depth, depth), bf16), pltpu.VMEM((tensor, depth, cols), bf16)],
        compiler_params=LIMIT,
        cost_estimate=BRIEF,
    )(owner, *left, *grad, root)


def stats_kernel(rows, cols, paired, owner, *refs):
    tensor = lax.axis_size("tensor")
    grad = refs[:tensor]
    if paired:
        stats, stats_out, square = refs[tensor:]
        left, right = stats.at[0, 0], stats.at[0, 1]
        left_out, right_out = stats_out.at[0, 0], stats_out.at[0, 1]
    else:
        left, right, left_out, right_out, square = refs[tensor:]
        left, right, left_out, right_out = left.at[0], right.at[0], left_out.at[0], right_out.at[0]
    part = lax.axis_index("tensor")

    @pl.when(holds(owner))
    def _():
        high = left.shape[0]
        total = jnp.zeros(left.shape, f32)
        mine = block(grad[0], rows, cols)
        for k in range(tensor):
            columns = block(grad[k], rows, cols)
            slots = high // rows
            band = block(grad[k], rows, cols, part * slots, slots)
            total = total + lax.dot_general(
                band, columns, (((1,), (1,)), ((), ())), preferred_element_type=f32
            )
            square[part ^ k] = lax.dot_general(
                mine, columns, (((0,), (0,)), ((), ())), preferred_element_type=f32
            )
        left_out[...] = beta_stat * left[...] + (1.0 - beta_stat) * total
        for k in range(tensor):
            span = slice(k * cols, (k + 1) * cols)
            right_out[:, span] = beta_stat * right[:, span] + (1.0 - beta_stat) * square[k]

    @pl.when(jnp.logical_not(holds(owner)))
    def _():
        left_out[...] = left[...]
        right_out[...] = right[...]


def stats_part(owner, grad, stats, rows, cols):
    tensor = len(grad)
    shapes = tuple(jax.ShapeDtypeStruct(s.shape, f32) for s in stats)
    depth = tensor * cols
    return pl.pallas_call(
        functools.partial(stats_kernel, rows, cols, len(stats) == 1),
        out_shape=shapes,
        in_specs=[SMEM] + [VMEM] * (tensor + len(stats)),
        out_specs=(VMEM,) * len(stats),
        scratch_shapes=[pltpu.VMEM((tensor, cols, cols), f32)],
        compiler_params=LIMIT,
        cost_estimate=pl.CostEstimate(
            flops=4 * depth * depth * cols,
            bytes_accessed=8 * sum(s.size for s in stats) + 2 * depth * depth,
            transcendentals=0,
        ),
    )(owner, *grad, *stats)


def weight_kernel(owner, weight, back, out):
    def unit(u, carry):
        out[u] = weight[u] - learn_rate * back[owner[u]].astype(f32)
        return carry

    lax.fori_loop(0, weight.shape[0], unit, 0, unroll=weight.shape[0] <= 4)


def weight_part(owner, weight, back):
    return pl.pallas_call(
        weight_kernel,
        out_shape=jax.ShapeDtypeStruct(weight.shape, f32),
        in_specs=[SMEM, VMEM, VMEM],
        out_specs=VMEM,
        compiler_params=LIMIT,
        cost_estimate=pl.CostEstimate(
            flops=2 * weight.size, bytes_accessed=12 * weight.size, transcendentals=0
        ),
    )(owner, weight, back)


def flip(value, bits):
    size = lax.axis_size("tensor")
    return lax.ppermute(value, "tensor", [(i, i ^ bits) for i in range(size)])


def spread_first(value):
    return value, flip(value, lax.axis_size("tensor") // 2)


def spread_rest(value, far):
    bit = lax.axis_size("tensor") // 2
    held = {0: value, bit: far}
    bit //= 2
    while bit:
        for k in sorted(held):
            held[k | bit] = flip(held[k], bit)
        bit //= 2
    return [held[k] for k in range(len(held))]


def after(value, *others):
    return lax.optimization_barrier((value, *others))[0]


def over_shard(value):
    return lax.all_to_all(value, "shard", split_axis=0, concat_axis=0, tiled=True)


def scale_kernel(done, adam, *refs):
    norm, out = refs[:-1], refs[-1]
    total = norm[0][...]
    for other in norm[1:]:
        total = total + other[...]
    scale = jnp.sqrt(adam[...] / (total + graft_eps))[:1, :1]
    out[...] = (scale * done[...]).astype(bf16)


def grafted(done, norm, adam, owners):
    norms = [norm] + [flip(norm, k) for k in range(1, lax.axis_size("tensor"))]
    out = pl.pallas_call(
        scale_kernel,
        out_shape=jax.ShapeDtypeStruct(done.shape, bf16),
        in_specs=[VMEM] * (2 + len(norms)),
        out_specs=VMEM,
        compiler_params=LIMIT,
        cost_estimate=pl.CostEstimate(
            flops=done.size, bytes_accessed=6 * done.size, transcendentals=0
        ),
    )(done, adam, *norms)
    return out.reshape(owners, -1, done.shape[1])


def per_device(
    att_grads,
    glu_grads,
    att_weight,
    att_moment,
    att_second,
    glu_weight,
    glu_moment,
    glu_second,
    att_stats,
    att_left_root,
    att_right_root,
    glu_left_stat,
    glu_right_stat,
    glu_left_root,
    glu_right_root,
    att_owner,
    glu_owner,
):
    owners = lax.axis_size("shard")
    rows = att_weight.shape[1]
    att_packed, att_moment_out, att_second_out = adam_part(
        att_owner, att_grads, att_moment, att_second, owners, None
    )
    glu_packed, glu_moment_out, glu_second_out = adam_part(
        glu_owner, glu_grads, glu_moment, glu_second, owners, LIMIT
    )
    att_root, att_root_far = spread_first(att_left_root[0])
    att_near, att_far = spread_first(after(over_shard(att_packed), att_root_far, glu_packed))
    att_left = spread_rest(*lax.optimization_barrier((att_root, att_root_far, att_near))[:2])
    glu_root, glu_root_far = spread_first(after(glu_left_root[0], att_far))
    att_grad = spread_rest(att_near, att_far)
    att_done, att_norm, att_adam = shampoo_part(att_owner, att_left, att_grad, att_right_root, rows)
    att_send = grafted(att_done, att_norm, att_adam, owners)
    glu_near, glu_far = spread_first(after(over_shard(glu_packed), att_send, glu_root_far))
    glu_left = spread_rest(*lax.optimization_barrier((glu_root, glu_root_far, glu_near))[:2])
    att_back = over_shard(att_send)
    glu_grad = spread_rest(glu_near, glu_far)
    glu_done, glu_norm, glu_adam = shampoo_part(glu_owner, glu_left, glu_grad, glu_right_root, rows)
    glu_back = over_shard(grafted(glu_done, glu_norm, glu_adam, owners))
    (att_stats_out,) = stats_part(att_owner, att_grad, (att_stats,), rows, att_weight.shape[2])
    glu_left_out, glu_right_out = stats_part(
        glu_owner, glu_grad, (glu_left_stat, glu_right_stat), rows, glu_weight.shape[2]
    )
    att_weight_out = weight_part(att_owner, att_weight, att_back)
    glu_weight_out = weight_part(glu_owner, glu_weight, glu_back)
    return (
        att_weight_out,
        att_moment_out,
        att_second_out,
        glu_weight_out,
        glu_moment_out,
        glu_second_out,
        att_stats_out,
        glu_left_out,
        glu_right_out,
    )


def solution(mesh):
    placed = (
        P(None, None, "shard", "tensor"),
        P(None, None, "shard", "tensor"),
        P(None, "shard", "tensor"),
        P(None, "shard", "tensor"),
        P(None, "shard", "tensor"),
        P(None, "shard", "tensor"),
        P(None, "shard", "tensor"),
        P(None, "shard", "tensor"),
        P("shard", None, "tensor", None),
        P("shard", "tensor", None),
        P("shard", None, "tensor"),
        P("shard", "tensor", None),
        P("shard", "tensor", None),
        P("shard", "tensor", None),
        P("shard", None, "tensor"),
        P(),
        P(),
    )
    return jax.shard_map(
        per_device,
        mesh=mesh,
        in_specs=placed,
        out_specs=(
            P(None, "shard", "tensor"),
            P(None, "shard", "tensor"),
            P(None, "shard", "tensor"),
            P(None, "shard", "tensor"),
            P(None, "shard", "tensor"),
            P(None, "shard", "tensor"),
            P("shard", None, "tensor", None),
            P("shard", "tensor", None),
            P("shard", "tensor", None),
        ),
        check_vma=False,
    )
```

```python
import functools

import jax
import jax.numpy as jnp
from jax import lax
from jax.experimental import pallas as pl
from jax.experimental.pallas import tpu as pltpu
from jax.sharding import PartitionSpec as P

beta_one = 0.9
beta_two = 0.999
beta_stat = 0.999
adam_eps = 1e-08
graft_eps = 1e-06
learn_rate = 0.01

bf16 = jnp.bfloat16
f32 = jnp.float32
LANES = 128
VMEM = pl.BlockSpec(memory_space=pltpu.VMEM)
BRIEF = pl.CostEstimate(flops=1024, bytes_accessed=1024, transcendentals=0)
LIMIT = pltpu.CompilerParams(vmem_limit_bytes=16 << 20)
SMEM = pl.BlockSpec(memory_space=pltpu.SMEM)


def round_up(value, step):
    return -(-value // step) * step


def packed_shape(rows, cols):
    lanes = round_up(cols, LANES)
    return (rows, lanes) if lanes > cols else (round_up(rows + 3, 8), cols)


def pieces(totals, shape):
    row = lax.broadcasted_iota(jnp.int32, shape, 0)
    column = lax.broadcasted_iota(jnp.int32, shape, 1)
    value = jnp.zeros(shape, f32)
    for n, total in enumerate(totals):
        rest = jnp.broadcast_to(total, shape)
        for m in range(3):
            piece = rest.astype(bf16).astype(f32)
            value = jnp.where(row == 3 * n + m, piece, value)
            rest = rest - piece
    return jnp.where(column == 0, value, 0.0).astype(bf16)


def adam_kernel(owner, grads, moment, second, packed, moment_out, second_out):
    rows, cols = moment.shape[1:]
    packed_rows, packed_cols = packed.shape[1:]
    packed[...] = jnp.zeros_like(packed)

    def unit(u, carry):
        summed = grads[0, u]
        for micro in range(1, grads.shape[0]):
            summed = summed + grads[micro, u]
        moment_new = beta_one * moment[u] + (1.0 - beta_one) * summed
        second_new = beta_two * second[u] + (1.0 - beta_two) * summed * summed
        direction = moment_new / (jnp.sqrt(second_new) + adam_eps)
        moment_out[u] = moment_new
        second_out[u] = second_new
        total = jnp.sum(direction * direction, axis=(0, 1), keepdims=True)
        slot = owner[u]
        if packed_cols > cols:
            packed[slot, :, :cols] = summed.astype(bf16)
            packed[slot, :, cols:] = pieces((total,), (packed_rows, packed_cols - cols))
        else:
            packed[slot, :rows, :] = summed.astype(bf16)
            packed[slot, rows:, :] = pieces((total,), (packed_rows - rows, packed_cols))
        return carry

    lax.fori_loop(0, moment.shape[0], unit, 0, unroll=moment.shape[0] <= 4)


def adam_part(owner, grads, moment, second, owners, params):
    rows, cols = moment.shape[1:]
    packed = jax.ShapeDtypeStruct((owners, *packed_shape(rows, cols)), bf16)
    return pl.pallas_call(
        adam_kernel,
        out_shape=(
            packed,
            jax.ShapeDtypeStruct(moment.shape, f32),
            jax.ShapeDtypeStruct(second.shape, f32),
        ),
        in_specs=[SMEM, VMEM, VMEM, VMEM],
        out_specs=(VMEM, VMEM, VMEM),
        compiler_params=params,
        cost_estimate=pl.CostEstimate(
            flops=20 * moment.size, bytes_accessed=32 * moment.size, transcendentals=moment.size
        ),
    )(owner, grads, moment, second)


def holds(owner):
    me = lax.axis_index("shard")
    found = owner[0] == me
    for unit in range(1, owner.shape[0]):
        found = jnp.logical_or(found, owner[unit] == me)
    return found


def block(ref, rows, cols, start=0, count=None):
    count = ref.shape[0] if count is None else count
    return ref[pl.ds(start, count), :rows, :cols].reshape(count * rows, cols)


def shampoo_kernel(rows, cols, owner, *refs):
    tensor = lax.axis_size("tensor")
    left, grad, (root, *outs, whole, half) = refs[:tensor], refs[tensor : 2 * tensor], refs[2 * tensor :]
    part = lax.axis_index("tensor")

    @pl.when(holds(owner))
    def _():
        depth = left[0].shape[0]
        for i in range(tensor):
            place = pl.multiple_of((part ^ i) * depth, depth)
            whole[pl.ds(place, depth), :] = left[i][...]
        total = jnp.zeros((whole.shape[0], cols), f32)
        adam_sq = jnp.zeros((1, 1), f32)
        for k in range(tensor):
            columns = block(grad[k], rows, cols)
            half[k] = jnp.dot(whole[...], columns, preferred_element_type=f32).astype(bf16)
            if grad[k].shape[2] > cols:
                extra = grad[k][:, :, cols:]
            else:
                extra = grad[k][:, rows:, :]
            extra = extra.astype(f32).reshape(-1, extra.shape[-1])
            adam_sq = adam_sq + jnp.sum(extra, axis=(0, 1), keepdims=True)
        for k in range(tensor):
            span = slice(k * cols, (k + 1) * cols)
            if spare(cols):
                sides, right = (((1,), (1,)), ((), ())), root[0, :, span]
            else:
                sides, right = (((1,), (0,)), ((), ())), root[0, span, :]
            total = total + lax.dot_general(
                half[part ^ k], right, sides, preferred_element_type=f32
            )
        norm = jnp.sum(total * total, axis=(0, 1), keepdims=True)
        if len(outs) == 1:
            out = outs[0]
            owners, high, wide = out.shape
            out[:, :, :cols] = total.astype(bf16).reshape(owners, high, cols)
            extra = pieces((norm, adam_sq), (high, wide - cols))
            out[:, :, cols:] = jnp.broadcast_to(extra[None], (owners, *extra.shape))
        else:
            for ref, value in zip(outs, (total, norm, adam_sq)):
                ref[...] = jnp.broadcast_to(value, ref.shape)

    @pl.when(jnp.logical_not(holds(owner)))
    def _():
        for ref in outs:
            ref[...] = jnp.zeros_like(ref)


def spare(cols):
    return round_up(cols, LANES) > cols


def shampoo_part(owner, left, grad, root, rows):
    cols = root.shape[2]
    depth = left[0].shape[1]
    if spare(cols):
        root = jnp.swapaxes(root, 1, 2)
    tensor = len(left)
    small = jax.ShapeDtypeStruct((8, LANES), f32)
    if spare(cols):
        shapes = (jax.ShapeDtypeStruct((depth // rows, rows, round_up(cols, LANES)), bf16),)
    else:
        shapes = (jax.ShapeDtypeStruct((depth, cols), f32), small, small)
    return pl.pallas_call(
        functools.partial(shampoo_kernel, rows, cols),
        out_shape=shapes,
        in_specs=[SMEM] + [VMEM] * (2 * tensor + 1),
        out_specs=(VMEM,) * len(shapes),
        scratch_shapes=[pltpu.VMEM((depth, depth), bf16), pltpu.VMEM((tensor, depth, cols), bf16)],
        compiler_params=LIMIT,
        cost_estimate=BRIEF,
    )(owner, *left, *grad, root)


def stats_kernel(rows, cols, paired, owner, *refs):
    tensor = lax.axis_size("tensor")
    grad = refs[:tensor]
    if paired:
        stats, stats_out, square = refs[tensor:]
        left, right = stats.at[0, 0], stats.at[0, 1]
        left_out, right_out = stats_out.at[0, 0], stats_out.at[0, 1]
    else:
        left, right, left_out, right_out, square = refs[tensor:]
        left, right, left_out, right_out = left.at[0], right.at[0], left_out.at[0], right_out.at[0]
    part = lax.axis_index("tensor")

    @pl.when(holds(owner))
    def _():
        high = left.shape[0]
        total = jnp.zeros(left.shape, f32)
        mine = block(grad[0], rows, cols)
        for k in range(tensor):
            columns = block(grad[k], rows, cols)
            slots = high // rows
            band = block(grad[k], rows, cols, part * slots, slots)
            total = total + lax.dot_general(
                band, columns, (((1,), (1,)), ((), ())), preferred_element_type=f32
            )
            square[part ^ k] = lax.dot_general(
                mine, columns, (((0,), (0,)), ((), ())), preferred_element_type=f32
            )
        left_out[...] = beta_stat * left[...] + (1.0 - beta_stat) * total
        for k in range(tensor):
            span = slice(k * cols, (k + 1) * cols)
            right_out[:, span] = beta_stat * right[:, span] + (1.0 - beta_stat) * square[k]

    @pl.when(jnp.logical_not(holds(owner)))
    def _():
        left_out[...] = left[...]
        right_out[...] = right[...]


def stats_part(owner, grad, stats, rows, cols):
    tensor = len(grad)
    shapes = tuple(jax.ShapeDtypeStruct(s.shape, f32) for s in stats)
    depth = tensor * cols
    return pl.pallas_call(
        functools.partial(stats_kernel, rows, cols, len(stats) == 1),
        out_shape=shapes,
        in_specs=[SMEM] + [VMEM] * (tensor + len(stats)),
        out_specs=(VMEM,) * len(stats),
        scratch_shapes=[pltpu.VMEM((tensor, cols, cols), f32)],
        compiler_params=LIMIT,
        cost_estimate=pl.CostEstimate(
            flops=4 * depth * depth * cols,
            bytes_accessed=8 * sum(s.size for s in stats) + 2 * depth * depth,
            transcendentals=0,
        ),
    )(owner, *grad, *stats)


def weight_kernel(owner, weight, back, *refs):
    *norm, out = refs
    cols = weight.shape[2]

    def unit(u, carry):
        update = back[owner[u], :, :cols].astype(f32)
        if norm:
            adam, *norms = norm
            total = norms[0][u]
            for other in norms[1:]:
                total = total + other[u]
            update = jnp.sqrt(adam[u] / (total + graft_eps))[:1, :1] * update
        out[u] = weight[u] - learn_rate * update
        return carry

    lax.fori_loop(0, weight.shape[0], unit, 0, unroll=weight.shape[0] <= 4)


def weight_part(owner, weight, back, *norm):
    return pl.pallas_call(
        weight_kernel,
        out_shape=jax.ShapeDtypeStruct(weight.shape, f32),
        in_specs=[SMEM] + [VMEM] * (2 + len(norm)),
        out_specs=VMEM,
        compiler_params=LIMIT,
        cost_estimate=pl.CostEstimate(
            flops=2 * weight.size, bytes_accessed=12 * weight.size, transcendentals=0
        ),
    )(owner, weight, back, *norm)


def extra_kernel(cols, owner, back, norm, adam):
    def unit(u, carry):
        extra = back[owner[u], :, cols:].astype(f32)
        row = lax.broadcasted_iota(jnp.int32, extra.shape, 0)
        for ref, first in ((norm, 0), (adam, 3)):
            mine = jnp.where((row >= first) & (row < first + 3), extra, 0.0)
            total = jnp.sum(mine, axis=(0, 1), keepdims=True)
            ref[u] = jnp.broadcast_to(total, ref.shape[1:])
        return carry

    lax.fori_loop(0, norm.shape[0], unit, 0, unroll=norm.shape[0] <= 4)


def extra_part(owner, back, cols):
    small = jax.ShapeDtypeStruct((owner.shape[0], 8, LANES), f32)
    norm, adam = pl.pallas_call(
        functools.partial(extra_kernel, cols),
        out_shape=(small, small),
        in_specs=[SMEM, VMEM],
        out_specs=(VMEM, VMEM),
        compiler_params=LIMIT,
        cost_estimate=BRIEF,
    )(owner, back)
    return adam, *all_norms(norm)


def all_norms(norm):
    return [norm] + [flip(norm, k) for k in range(1, lax.axis_size("tensor"))]


def back_part(owner, weight, done, owners):
    if len(done) == 1:
        back = over_shard(done[0])
        return weight_part(owner, weight, back, *extra_part(owner, back, weight.shape[2]))
    return weight_part(owner, weight, over_shard(grafted(*done, owners)))


def flip(value, bits):
    size = lax.axis_size("tensor")
    return lax.ppermute(value, "tensor", [(i, i ^ bits) for i in range(size)])


def spread_first(value):
    return value, flip(value, lax.axis_size("tensor") // 2)


def spread_rest(value, far):
    bit = lax.axis_size("tensor") // 2
    held = {0: value, bit: far}
    bit //= 2
    while bit:
        for k in sorted(held):
            held[k | bit] = flip(held[k], bit)
        bit //= 2
    return [held[k] for k in range(len(held))]


def after(value, *others):
    return lax.optimization_barrier((value, *others))[0]


def over_shard(value):
    return lax.all_to_all(value, "shard", split_axis=0, concat_axis=0, tiled=True)


def scale_kernel(done, adam, *refs):
    norm, out = refs[:-1], refs[-1]
    total = norm[0][...]
    for other in norm[1:]:
        total = total + other[...]
    scale = jnp.sqrt(adam[...] / (total + graft_eps))[:1, :1]
    out[...] = (scale * done[...]).astype(bf16)


def grafted(done, norm, adam, owners):
    norms = all_norms(norm)
    out = pl.pallas_call(
        scale_kernel,
        out_shape=jax.ShapeDtypeStruct(done.shape, bf16),
        in_specs=[VMEM] * (2 + len(norms)),
        out_specs=VMEM,
        compiler_params=LIMIT,
        cost_estimate=pl.CostEstimate(
            flops=done.size, bytes_accessed=6 * done.size, transcendentals=0
        ),
    )(done, adam, *norms)
    return out.reshape(owners, -1, done.shape[1])


def per_device(
    att_grads,
    glu_grads,
    att_weight,
    att_moment,
    att_second,
    glu_weight,
    glu_moment,
    glu_second,
    att_stats,
    att_left_root,
    att_right_root,
    glu_left_stat,
    glu_right_stat,
    glu_left_root,
    glu_right_root,
    att_owner,
    glu_owner,
):
    owners = lax.axis_size("shard")
    rows = att_weight.shape[1]
    att_packed, att_moment_out, att_second_out = adam_part(
        att_owner, att_grads, att_moment, att_second, owners, None
    )
    glu_packed, glu_moment_out, glu_second_out = adam_part(
        glu_owner, glu_grads, glu_moment, glu_second, owners, LIMIT
    )
    att_root, att_root_far = spread_first(att_left_root[0])
    att_near, att_far = spread_first(after(over_shard(att_packed), att_root_far, glu_packed))
    att_left = spread_rest(*lax.optimization_barrier((att_root, att_root_far, att_near))[:2])
    glu_root, glu_root_far = spread_first(after(glu_left_root[0], att_far))
    att_grad = spread_rest(att_near, att_far)
    att_done = shampoo_part(att_owner, att_left, att_grad, att_right_root, rows)
    glu_near, glu_far = spread_first(after(over_shard(glu_packed), glu_root_far, *att_done))
    glu_left = spread_rest(*lax.optimization_barrier((glu_root, glu_root_far, glu_near))[:2])
    (att_stats_out,) = stats_part(att_owner, att_grad, (att_stats,), rows, att_weight.shape[2])
    glu_grad = spread_rest(glu_near, after(glu_far, att_stats_out, *glu_left[1:]))
    glu_done = shampoo_part(glu_owner, glu_left, glu_grad, glu_right_root, rows)
    glu_left_out, glu_right_out = stats_part(
        glu_owner, glu_grad, (glu_left_stat, glu_right_stat), rows, glu_weight.shape[2]
    )
    att_weight_out = back_part(att_owner, att_weight, att_done, owners)
    glu_weight_out = back_part(glu_owner, glu_weight, glu_done, owners)
    return (
        att_weight_out,
        att_moment_out,
        att_second_out,
        glu_weight_out,
        glu_moment_out,
        glu_second_out,
        att_stats_out,
        glu_left_out,
        glu_right_out,
    )


def solution(mesh):
    placed = (
        P(None, None, "shard", "tensor"),
        P(None, None, "shard", "tensor"),
        P(None, "shard", "tensor"),
        P(None, "shard", "tensor"),
        P(None, "shard", "tensor"),
        P(None, "shard", "tensor"),
        P(None, "shard", "tensor"),
        P(None, "shard", "tensor"),
        P("shard", None, "tensor", None),
        P("shard", "tensor", None),
        P("shard", None, "tensor"),
        P("shard", "tensor", None),
        P("shard", "tensor", None),
        P("shard", "tensor", None),
        P("shard", None, "tensor"),
        P(),
        P(),
    )
    return jax.shard_map(
        per_device,
        mesh=mesh,
        in_specs=placed,
        out_specs=(
            P(None, "shard", "tensor"),
            P(None, "shard", "tensor"),
            P(None, "shard", "tensor"),
            P(None, "shard", "tensor"),
            P(None, "shard", "tensor"),
            P(None, "shard", "tensor"),
            P("shard", None, "tensor", None),
            P("shard", "tensor", None),
            P("shard", "tensor", None),
        ),
        check_vma=False,
    )
```

```python
import functools

import jax
import jax.numpy as jnp
from jax import lax
from jax.experimental import pallas as pl
from jax.experimental.pallas import tpu as pltpu
from jax.sharding import PartitionSpec as P

beta_one = 0.9
beta_two = 0.999
beta_stat = 0.999
adam_eps = 1e-08
graft_eps = 1e-06
learn_rate = 0.01

bf16 = jnp.bfloat16
f32 = jnp.float32
LANES = 128
VMEM = pl.BlockSpec(memory_space=pltpu.VMEM)
BRIEF = pl.CostEstimate(flops=1024, bytes_accessed=1024, transcendentals=0)
LIMIT = pltpu.CompilerParams(vmem_limit_bytes=16 << 20)
SMEM = pl.BlockSpec(memory_space=pltpu.SMEM)


def round_up(value, step):
    return -(-value // step) * step


def folds(rows, cols):
    return cols == LANES + LANES // 2 and rows % 32 == 0


def packed_shape(rows, cols, totals):
    lanes = round_up(cols, LANES)
    if folds(rows, cols):
        return (rows + rows // 2 + round_up(3 * totals, 8), LANES)
    return (rows, lanes) if lanes > cols else (round_up(rows + 3 * totals, 8), cols)


def pieces(totals, shape):
    row = lax.broadcasted_iota(jnp.int32, shape, 0)
    column = lax.broadcasted_iota(jnp.int32, shape, 1)
    value = jnp.zeros(shape, f32)
    for n, total in enumerate(totals):
        rest = jnp.broadcast_to(total, shape)
        for m in range(3):
            piece = rest.astype(bf16).astype(f32)
            value = jnp.where(row == 3 * n + m, piece, value)
            rest = rest - piece
    return jnp.where(column == 0, value, 0.0).astype(bf16)


def pack(ref, value, totals):
    rows, cols = value.shape
    high, wide = ref.shape
    if folds(rows, cols):
        half, side = rows // 2, value[:, LANES:]
        ref[:rows, :] = value[:, :LANES].astype(bf16)
        ref[rows : rows + half, :] = jnp.concatenate([side[:half], side[half:]], axis=1).astype(bf16)
        if totals:
            ref[rows + half :, :] = pieces(totals, (high - rows - half, wide))
    elif wide > cols:
        ref[:, :cols] = value.astype(bf16)
        ref[:, cols:] = pieces(totals, (high, wide - cols))
    else:
        ref[:rows, :] = value.astype(bf16)
        if totals:
            ref[rows:, :] = pieces(totals, (high - rows, wide))


def unpack(ref, rows, cols, start=0, count=None):
    count = ref.shape[0] if count is None else count
    span = pl.ds(start, count)
    if not folds(rows, cols):
        return ref[span, :rows, :cols].reshape(count * rows, cols)
    side = ref[span, rows : rows + rows // 2, :]
    side = jnp.concatenate([side[:, :, : LANES // 2], side[:, :, LANES // 2 :]], axis=1)
    return jnp.concatenate([ref[span, :rows, :], side], axis=2).reshape(count * rows, cols)


def unpack_total(ref, rows, cols, n, start=0, count=None):
    count = ref.shape[0] if count is None else count
    span = pl.ds(start, count)
    if folds(rows, cols):
        extra = ref[span, rows + rows // 2 :, :]
    elif ref.shape[2] > cols:
        extra = ref[span, :, cols:]
    else:
        extra = ref[span, rows:, :]
    row = lax.broadcasted_iota(jnp.int32, extra.shape, 1)
    mine = jnp.where((row >= 3 * n) & (row < 3 * n + 3), extra.astype(f32), 0.0)
    return jnp.sum(jnp.sum(mine, axis=0), axis=(0, 1), keepdims=True)


def adam_kernel(owner, grads, moment, second, packed, moment_out, second_out):
    packed[...] = jnp.zeros_like(packed)

    def unit(u, carry):
        summed = grads[0, u]
        for micro in range(1, grads.shape[0]):
            summed = summed + grads[micro, u]
        moment_new = beta_one * moment[u] + (1.0 - beta_one) * summed
        second_new = beta_two * second[u] + (1.0 - beta_two) * summed * summed
        direction = moment_new / (jnp.sqrt(second_new) + adam_eps)
        moment_out[u] = moment_new
        second_out[u] = second_new
        total = jnp.sum(direction * direction, axis=(0, 1), keepdims=True)
        pack(packed.at[owner[u]], summed, (total,))
        return carry

    lax.fori_loop(0, moment.shape[0], unit, 0, unroll=moment.shape[0] <= 4)


def adam_part(owner, grads, moment, second, owners, params):
    rows, cols = moment.shape[1:]
    return pl.pallas_call(
        adam_kernel,
        out_shape=(
            jax.ShapeDtypeStruct((owners, *packed_shape(rows, cols, 1)), bf16),
            jax.ShapeDtypeStruct(moment.shape, f32),
            jax.ShapeDtypeStruct(second.shape, f32),
        ),
        in_specs=[SMEM, VMEM, VMEM, VMEM],
        out_specs=(VMEM, VMEM, VMEM),
        compiler_params=params,
        cost_estimate=pl.CostEstimate(
            flops=20 * moment.size, bytes_accessed=32 * moment.size, transcendentals=moment.size
        ),
    )(owner, grads, moment, second)


def holds(owner):
    me = lax.axis_index("shard")
    found = owner[0] == me
    for unit in range(1, owner.shape[0]):
        found = jnp.logical_or(found, owner[unit] == me)
    return found


def shampoo_kernel(rows, cols, turned, embed, owner, *refs):
    tensor = lax.axis_size("tensor")
    left, grad = refs[:tensor], refs[tensor : 2 * tensor]
    root, *outs, whole, blocks, done = refs[2 * tensor :]
    part = lax.axis_index("tensor")

    @pl.when(holds(owner))
    def _():
        depth = left[0].shape[0]
        adam_sq = jnp.zeros((1, 1), f32)
        for k in range(tensor):
            whole[pl.ds(pl.multiple_of((part ^ k) * depth, depth), depth), :] = left[k][...]
            blocks[part ^ k] = unpack(grad[k], rows, cols)
            adam_sq = adam_sq + unpack_total(grad[k], rows, cols, 0)
        half = jnp.zeros((whole.shape[0], cols), f32)
        for k in range(tensor):
            span = slice(k * cols, (k + 1) * cols)
            if turned:
                sides, right = (((1,), (1,)), ((), ())), root[0, :, span]
            else:
                sides, right = (((1,), (0,)), ((), ())), root[0, span, :]
            half = half + lax.dot_general(blocks[k], right, sides, preferred_element_type=f32)
        total = jnp.dot(whole[...], half.astype(bf16), preferred_element_type=f32)
        norm = jnp.sum(total * total, axis=(0, 1), keepdims=True)
        if embed:
            done[...] = total
            for slot in range(outs[0].shape[0]):
                value = done[slot * rows : (slot + 1) * rows, :]
                pack(outs[0].at[slot], value, (norm, adam_sq))
        else:
            for ref, value in zip(outs, (total, norm, adam_sq)):
                ref[...] = jnp.broadcast_to(value, ref.shape)

    @pl.when(jnp.logical_not(holds(owner)))
    def _():
        for ref in outs:
            ref[...] = jnp.zeros_like(ref)


def shampoo_part(owner, left, grad, root, rows, embed):
    cols = root.shape[2]
    depth = left[0].shape[1]
    tensor = len(left)
    turned = cols % LANES != 0
    if turned:
        root = jnp.swapaxes(root, 1, 2)
    if embed:
        shapes = (jax.ShapeDtypeStruct((depth // rows, *packed_shape(rows, cols, 2)), bf16),)
    else:
        small = jax.ShapeDtypeStruct((8, LANES), f32)
        shapes = (jax.ShapeDtypeStruct((depth, cols), f32), small, small)
    return pl.pallas_call(
        functools.partial(shampoo_kernel, rows, cols, turned, embed),
        out_shape=shapes,
        in_specs=[SMEM] + [VMEM] * (2 * tensor + 1),
        out_specs=(VMEM,) * len(shapes),
        scratch_shapes=[
            pltpu.VMEM((depth, depth), bf16),
            pltpu.VMEM((tensor, depth, cols), bf16),
            pltpu.VMEM((depth, cols) if embed else (8, LANES), f32),
        ],
        compiler_params=LIMIT,
        cost_estimate=BRIEF,
    )(owner, *left, *grad, root)


def stats_kernel(rows, cols, paired, owner, *refs):
    tensor = lax.axis_size("tensor")
    grad = refs[:tensor]
    if paired:
        stats, stats_out, square = refs[tensor:]
        left, right = stats.at[0, 0], stats.at[0, 1]
        left_out, right_out = stats_out.at[0, 0], stats_out.at[0, 1]
    else:
        left, right, left_out, right_out, square = refs[tensor:]
        left, right, left_out, right_out = left.at[0], right.at[0], left_out.at[0], right_out.at[0]
    part = lax.axis_index("tensor")

    @pl.when(holds(owner))
    def _():
        high = left.shape[0]
        total = jnp.zeros(left.shape, f32)
        mine = unpack(grad[0], rows, cols)
        for k in range(tensor):
            columns = unpack(grad[k], rows, cols)
            slots = high // rows
            band = unpack(grad[k], rows, cols, part * slots, slots)
            total = total + lax.dot_general(
                band, columns, (((1,), (1,)), ((), ())), preferred_element_type=f32
            )
            square[part ^ k] = lax.dot_general(
                mine, columns, (((0,), (0,)), ((), ())), preferred_element_type=f32
            )
        left_out[...] = beta_stat * left[...] + (1.0 - beta_stat) * total
        for k in range(tensor):
            span = slice(k * cols, (k + 1) * cols)
            right_out[:, span] = beta_stat * right[:, span] + (1.0 - beta_stat) * square[k]

    @pl.when(jnp.logical_not(holds(owner)))
    def _():
        left_out[...] = left[...]
        right_out[...] = right[...]


def stats_part(owner, grad, stats, rows, cols):
    tensor = len(grad)
    shapes = tuple(jax.ShapeDtypeStruct(s.shape, f32) for s in stats)
    depth = tensor * cols
    return pl.pallas_call(
        functools.partial(stats_kernel, rows, cols, len(stats) == 1),
        out_shape=shapes,
        in_specs=[SMEM] + [VMEM] * (tensor + len(stats)),
        out_specs=(VMEM,) * len(stats),
        scratch_shapes=[pltpu.VMEM((tensor, cols, cols), f32)],
        compiler_params=LIMIT,
        cost_estimate=pl.CostEstimate(
            flops=4 * depth * depth * cols,
            bytes_accessed=8 * sum(s.size for s in stats) + 2 * depth * depth,
            transcendentals=0,
        ),
    )(owner, *grad, *stats)


def weight_kernel(owner, weight, back, *refs):
    *norm, out = refs
    rows, cols = weight.shape[1:]

    def unit(u, carry):
        update = unpack(back, rows, cols, owner[u], 1).astype(f32)
        if norm:
            adam, *norms = norm
            total = norms[0][u]
            for other in norms[1:]:
                total = total + other[u]
            update = jnp.sqrt(adam[u] / (total + graft_eps))[:1, :1] * update
        out[u] = weight[u] - learn_rate * update
        return carry

    lax.fori_loop(0, weight.shape[0], unit, 0, unroll=weight.shape[0] <= 4)


def weight_part(owner, weight, back, *norm):
    return pl.pallas_call(
        weight_kernel,
        out_shape=jax.ShapeDtypeStruct(weight.shape, f32),
        in_specs=[SMEM] + [VMEM] * (2 + len(norm)),
        out_specs=VMEM,
        compiler_params=LIMIT,
        cost_estimate=pl.CostEstimate(
            flops=2 * weight.size, bytes_accessed=12 * weight.size, transcendentals=0
        ),
    )(owner, weight, back, *norm)


def totals_kernel(rows, cols, owner, back, norm, adam):
    def unit(u, carry):
        for n, ref in enumerate((norm, adam)):
            total = unpack_total(back, rows, cols, n, owner[u], 1)
            ref[u] = jnp.broadcast_to(total, ref.shape[1:])
        return carry

    lax.fori_loop(0, norm.shape[0], unit, 0, unroll=norm.shape[0] <= 4)


def totals_part(owner, back, rows, cols):
    small = jax.ShapeDtypeStruct((owner.shape[0], 8, LANES), f32)
    norm, adam = pl.pallas_call(
        functools.partial(totals_kernel, rows, cols),
        out_shape=(small, small),
        in_specs=[SMEM, VMEM],
        out_specs=(VMEM, VMEM),
        compiler_params=LIMIT,
        cost_estimate=BRIEF,
    )(owner, back)
    return adam, *all_norms(norm)


def all_norms(norm):
    return [norm] + [flip(norm, k) for k in range(1, lax.axis_size("tensor"))]


def flip(value, bits):
    size = lax.axis_size("tensor")
    return lax.ppermute(value, "tensor", [(i, i ^ bits) for i in range(size)])


def spread_first(value):
    return value, flip(value, lax.axis_size("tensor") // 2)


def spread_rest(value, far):
    bit = lax.axis_size("tensor") // 2
    held = {0: value, bit: far}
    bit //= 2
    while bit:
        for k in sorted(held):
            held[k | bit] = flip(held[k], bit)
        bit //= 2
    return [held[k] for k in range(len(held))]


def after(value, *others):
    return lax.optimization_barrier((value, *others))[0]


def over_shard(value):
    return lax.all_to_all(value, "shard", split_axis=0, concat_axis=0, tiled=True)


def scale_kernel(done, adam, *refs):
    norm, out = refs[:-1], refs[-1]
    total = norm[0][...]
    for other in norm[1:]:
        total = total + other[...]
    scale = jnp.sqrt(adam[...] / (total + graft_eps))[:1, :1]
    rows = done.shape[0] // out.shape[0]
    for slot in range(out.shape[0]):
        pack(out.at[slot], scale * done[slot * rows : (slot + 1) * rows, :], ())


def grafted(done, norm, adam, owners):
    depth, cols = done.shape
    norms = all_norms(norm)
    return pl.pallas_call(
        scale_kernel,
        out_shape=jax.ShapeDtypeStruct((owners, *packed_shape(depth // owners, cols, 0)), bf16),
        in_specs=[VMEM] * (2 + len(norms)),
        out_specs=VMEM,
        compiler_params=LIMIT,
        cost_estimate=pl.CostEstimate(
            flops=done.size, bytes_accessed=6 * done.size, transcendentals=0
        ),
    )(done, adam, *norms)


def per_device(
    att_grads,
    glu_grads,
    att_weight,
    att_moment,
    att_second,
    glu_weight,
    glu_moment,
    glu_second,
    att_stats,
    att_left_root,
    att_right_root,
    glu_left_stat,
    glu_right_stat,
    glu_left_root,
    glu_right_root,
    att_owner,
    glu_owner,
):
    owners = lax.axis_size("shard")
    rows = att_weight.shape[1]
    att_packed, att_moment_out, att_second_out = adam_part(
        att_owner, att_grads, att_moment, att_second, owners, LIMIT
    )
    glu_packed, glu_moment_out, glu_second_out = adam_part(
        glu_owner, glu_grads, glu_moment, glu_second, owners, None
    )
    glu_root, glu_root_far = spread_first(glu_left_root[0])
    glu_near, glu_far = spread_first(after(over_shard(glu_packed), glu_root_far, att_packed))
    glu_left = spread_rest(*lax.optimization_barrier((glu_root, glu_root_far, glu_near))[:2])
    att_root, att_root_far = spread_first(after(att_left_root[0], glu_far))
    glu_grad = spread_rest(glu_near, glu_far)
    (glu_done,) = shampoo_part(glu_owner, glu_left, glu_grad, glu_right_root, rows, True)
    att_near, att_far = spread_first(after(over_shard(att_packed), glu_done))
    att_left = spread_rest(*lax.optimization_barrier((att_root, att_root_far, att_near))[:2])
    glu_left_out, glu_right_out = stats_part(
        glu_owner, glu_grad, (glu_left_stat, glu_right_stat), rows, glu_weight.shape[2]
    )
    glu_back = over_shard(glu_done)
    att_grad = spread_rest(att_near, after(att_far, glu_left_out, *att_left[1:]))
    att_done = shampoo_part(att_owner, att_left, att_grad, att_right_root, rows, False)
    (att_stats_out,) = stats_part(att_owner, att_grad, (att_stats,), rows, att_weight.shape[2])
    att_back = over_shard(grafted(*att_done, owners))
    glu_totals = totals_part(glu_owner, glu_back, rows, glu_weight.shape[2])
    glu_weight_out = weight_part(glu_owner, glu_weight, glu_back, *glu_totals)
    att_weight_out = weight_part(att_owner, att_weight, att_back)
    return (
        att_weight_out,
        att_moment_out,
        att_second_out,
        glu_weight_out,
        glu_moment_out,
        glu_second_out,
        att_stats_out,
        glu_left_out,
        glu_right_out,
    )


def solution(mesh):
    placed = (
        P(None, None, "shard", "tensor"),
        P(None, None, "shard", "tensor"),
        P(None, "shard", "tensor"),
        P(None, "shard", "tensor"),
        P(None, "shard", "tensor"),
        P(None, "shard", "tensor"),
        P(None, "shard", "tensor"),
        P(None, "shard", "tensor"),
        P("shard", None, "tensor", None),
        P("shard", "tensor", None),
        P("shard", None, "tensor"),
        P("shard", "tensor", None),
        P("shard", "tensor", None),
        P("shard", "tensor", None),
        P("shard", None, "tensor"),
        P(),
        P(),
    )
    return jax.shard_map(
        per_device,
        mesh=mesh,
        in_specs=placed,
        out_specs=(
            P(None, "shard", "tensor"),
            P(None, "shard", "tensor"),
            P(None, "shard", "tensor"),
            P(None, "shard", "tensor"),
            P(None, "shard", "tensor"),
            P(None, "shard", "tensor"),
            P("shard", None, "tensor", None),
            P("shard", "tensor", None),
            P("shard", "tensor", None),
        ),
        check_vma=False,
    )
```

```python
import functools

import jax
import jax.numpy as jnp
from jax import lax
from jax.experimental import pallas as pl
from jax.experimental.pallas import tpu as pltpu
from jax.sharding import PartitionSpec as P

beta_one = 0.9
beta_two = 0.999
beta_stat = 0.999
adam_eps = 1e-08
graft_eps = 1e-06
learn_rate = 0.01

bf16 = jnp.bfloat16
f32 = jnp.float32
LANES = 128
VMEM = pl.BlockSpec(memory_space=pltpu.VMEM)
BRIEF = pl.CostEstimate(flops=1_000_000_000, bytes_accessed=1024, transcendentals=0)
LIMIT = pltpu.CompilerParams(vmem_limit_bytes=16 << 20)
SMEM = pl.BlockSpec(memory_space=pltpu.SMEM)
HBM = pl.BlockSpec(memory_space=pltpu.HBM)


def in_hbm(value):
    return pltpu.with_memory_space_constraint(value, pltpu.HBM)


def round_up(value, step):
    return -(-value // step) * step


def folds(rows, cols):
    return cols == LANES + LANES // 2 and rows % 32 == 0


def packed_shape(rows, cols, totals):
    lanes = round_up(cols, LANES)
    if folds(rows, cols):
        return (rows + rows // 2 + round_up(3 * totals, 8), LANES)
    return (rows, lanes) if lanes > cols else (round_up(rows + 3 * totals, 8), cols)


def pieces(totals, shape):
    row = lax.broadcasted_iota(jnp.int32, shape, 0)
    column = lax.broadcasted_iota(jnp.int32, shape, 1)
    value = jnp.zeros(shape, f32)
    for n, total in enumerate(totals):
        rest = jnp.broadcast_to(total, shape)
        for m in range(3):
            piece = rest.astype(bf16).astype(f32)
            value = jnp.where(row == 3 * n + m, piece, value)
            rest = rest - piece
    return jnp.where(column == 0, value, 0.0).astype(bf16)


def pack(ref, value, totals):
    rows, cols = value.shape
    high, wide = ref.shape
    if folds(rows, cols):
        half, side = rows // 2, value[:, LANES:]
        ref[:rows, :] = value[:, :LANES].astype(bf16)
        ref[rows : rows + half, :] = jnp.concatenate([side[:half], side[half:]], axis=1).astype(bf16)
        if totals:
            ref[rows + half :, :] = pieces(totals, (high - rows - half, wide))
    elif wide > cols:
        ref[:, :cols] = value.astype(bf16)
        ref[:, cols:] = pieces(totals, (high, wide - cols))
    else:
        ref[:rows, :] = value.astype(bf16)
        if totals:
            ref[rows:, :] = pieces(totals, (high - rows, wide))


def unpack(ref, rows, cols, start=0, count=None):
    count = ref.shape[0] if count is None else count
    span = pl.ds(start, count)
    if not folds(rows, cols):
        return ref[span, :rows, :cols].reshape(count * rows, cols)
    side = ref[span, rows : rows + rows // 2, :]
    side = jnp.concatenate([side[:, :, : LANES // 2], side[:, :, LANES // 2 :]], axis=1)
    return jnp.concatenate([ref[span, :rows, :], side], axis=2).reshape(count * rows, cols)


def unpack_total(ref, rows, cols, n, start=0, count=None):
    count = ref.shape[0] if count is None else count
    span = pl.ds(start, count)
    if folds(rows, cols):
        extra = ref[span, rows + rows // 2 :, :]
    elif ref.shape[2] > cols:
        extra = ref[span, :, cols:]
    else:
        extra = ref[span, rows:, :]
    row = lax.broadcasted_iota(jnp.int32, extra.shape, 1)
    mine = jnp.where((row >= 3 * n) & (row < 3 * n + 3), extra.astype(f32), 0.0)
    return jnp.sum(jnp.sum(mine, axis=0), axis=(0, 1), keepdims=True)


def adam_kernel(owner, grads, moment, second, packed, moment_out, second_out):
    packed[...] = jnp.zeros_like(packed)

    def unit(u, carry):
        summed = grads[0, u]
        for micro in range(1, grads.shape[0]):
            summed = summed + grads[micro, u]
        moment_new = beta_one * moment[u] + (1.0 - beta_one) * summed
        second_new = beta_two * second[u] + (1.0 - beta_two) * summed * summed
        direction = moment_new / (jnp.sqrt(second_new) + adam_eps)
        moment_out[u] = moment_new
        second_out[u] = second_new
        total = jnp.sum(direction * direction, axis=(0, 1), keepdims=True)
        pack(packed.at[owner[u]], summed, (total,))
        return carry

    lax.fori_loop(0, moment.shape[0], unit, 0, unroll=moment.shape[0] <= 4)


def adam_part(owner, grads, moment, second, owners, params):
    rows, cols = moment.shape[1:]
    return pl.pallas_call(
        adam_kernel,
        out_shape=(
            jax.ShapeDtypeStruct((owners, *packed_shape(rows, cols, 1)), bf16),
            jax.ShapeDtypeStruct(moment.shape, f32),
            jax.ShapeDtypeStruct(second.shape, f32),
        ),
        in_specs=[SMEM, VMEM, VMEM, VMEM],
        out_specs=(VMEM, VMEM, VMEM),
        compiler_params=params,
        cost_estimate=pl.CostEstimate(
            flops=10_000_000_000, bytes_accessed=32 * moment.size, transcendentals=moment.size
        ),
    )(owner, grads, moment, second)


def holds(owner):
    me = lax.axis_index("shard")
    found = owner[0] == me
    for unit in range(1, owner.shape[0]):
        found = jnp.logical_or(found, owner[unit] == me)
    return found


def shampoo_kernel(rows, cols, turned, embed, owner, *refs):
    tensor = lax.axis_size("tensor")
    left, grad = refs[:tensor], refs[tensor : 2 * tensor]
    root_hbm, *outs, whole, blocks, done, root, arrived = refs[2 * tensor :]
    part = lax.axis_index("tensor")

    @pl.when(holds(owner))
    def _():
        depth = left[0].shape[0]
        fetches = [pltpu.make_async_copy(root_hbm, root, arrived.at[tensor])]
        for k in range(tensor):
            band = pl.ds(pl.multiple_of((part ^ k) * depth, depth), depth)
            fetches.append(pltpu.make_async_copy(left[k], whole.at[band, :], arrived.at[k]))
        for fetch in fetches:
            fetch.start()
        adam_sq = jnp.zeros((1, 1), f32)
        for k in range(tensor):
            blocks[part ^ k] = unpack(grad[k], rows, cols)
            adam_sq = adam_sq + unpack_total(grad[k], rows, cols, 0)
        half = jnp.zeros((whole.shape[0], cols), f32)
        fetches[0].wait()
        for k in range(tensor):
            span = slice(k * cols, (k + 1) * cols)
            if turned:
                sides, right = (((1,), (1,)), ((), ())), root[0, :, span]
            else:
                sides, right = (((1,), (0,)), ((), ())), root[0, span, :]
            half = half + lax.dot_general(blocks[k], right, sides, preferred_element_type=f32)
        for fetch in fetches[1:]:
            fetch.wait()
        total = jnp.dot(whole[...], half.astype(bf16), preferred_element_type=f32)
        norm = jnp.sum(total * total, axis=(0, 1), keepdims=True)
        if embed:
            done[...] = total
            for slot in range(outs[0].shape[0]):
                value = done[slot * rows : (slot + 1) * rows, :]
                pack(outs[0].at[slot], value, (norm, adam_sq))
        else:
            for ref, value in zip(outs, (total, norm, adam_sq)):
                ref[...] = jnp.broadcast_to(value, ref.shape)

    @pl.when(jnp.logical_not(holds(owner)))
    def _():
        for ref in outs:
            ref[...] = jnp.zeros_like(ref)


def shampoo_part(owner, left, grad, root, rows, embed):
    cols = root.shape[2]
    depth = left[0].shape[1]
    tensor = len(left)
    turned = cols % LANES != 0
    if turned:
        root = jnp.swapaxes(root, 1, 2)
    if embed:
        shapes = (jax.ShapeDtypeStruct((depth // rows, *packed_shape(rows, cols, 2)), bf16),)
    else:
        small = jax.ShapeDtypeStruct((8, LANES), f32)
        shapes = (jax.ShapeDtypeStruct((depth, cols), f32), small, small)
    return pl.pallas_call(
        functools.partial(shampoo_kernel, rows, cols, turned, embed),
        out_shape=shapes,
        in_specs=[SMEM] + [HBM] * tensor + [VMEM] * tensor + [HBM],
        out_specs=(VMEM,) * len(shapes),
        scratch_shapes=[
            pltpu.VMEM((depth, depth), bf16),
            pltpu.VMEM((tensor, depth, cols), bf16),
            pltpu.VMEM((depth, cols) if embed else (8, LANES), f32),
            pltpu.VMEM(root.shape, bf16),
            pltpu.SemaphoreType.DMA((tensor + 1,)),
        ],
        compiler_params=LIMIT,
        cost_estimate=BRIEF,
    )(owner, *[in_hbm(value) for value in left], *grad, in_hbm(root))


def stats_kernel(rows, cols, paired, owner, *refs):
    tensor = lax.axis_size("tensor")
    grad, count = refs[:tensor], 1 if paired else 2
    stats, outs = refs[tensor : tensor + count], refs[tensor + count : tensor + 2 * count]
    square, held, arrived = refs[tensor + 2 * count], refs[-count - 1 : -1], refs[-1]
    if paired:
        left, right = held[0].at[0, 0], held[0].at[0, 1]
        left_out, right_out = outs[0].at[0, 0], outs[0].at[0, 1]
    else:
        left, right = held[0].at[0], held[1].at[0]
        left_out, right_out = outs[0].at[0], outs[1].at[0]
    part = lax.axis_index("tensor")
    fetches = [pltpu.make_async_copy(stats[i], held[i], arrived.at[i]) for i in range(count)]
    for fetch in fetches:
        fetch.start()

    @pl.when(holds(owner))
    def _():
        high = left.shape[0]
        total = jnp.zeros(left.shape, f32)
        mine = unpack(grad[0], rows, cols)
        for k in range(tensor):
            columns = unpack(grad[k], rows, cols)
            slots = high // rows
            band = unpack(grad[k], rows, cols, part * slots, slots)
            total = total + lax.dot_general(
                band, columns, (((1,), (1,)), ((), ())), preferred_element_type=f32
            )
            square[part ^ k] = lax.dot_general(
                mine, columns, (((0,), (0,)), ((), ())), preferred_element_type=f32
            )
        for fetch in fetches:
            fetch.wait()
        left_out[...] = beta_stat * left[...] + (1.0 - beta_stat) * total
        for k in range(tensor):
            span = slice(k * cols, (k + 1) * cols)
            right_out[:, span] = beta_stat * right[:, span] + (1.0 - beta_stat) * square[k]

    @pl.when(jnp.logical_not(holds(owner)))
    def _():
        for fetch in fetches:
            fetch.wait()
        left_out[...] = left[...]
        right_out[...] = right[...]


def stats_part(owner, grad, stats, rows, cols):
    tensor = len(grad)
    depth = tensor * cols
    return pl.pallas_call(
        functools.partial(stats_kernel, rows, cols, len(stats) == 1),
        out_shape=tuple(jax.ShapeDtypeStruct(value.shape, f32) for value in stats),
        in_specs=[SMEM] + [VMEM] * tensor + [HBM] * len(stats),
        out_specs=(VMEM,) * len(stats),
        scratch_shapes=[pltpu.VMEM((tensor, cols, cols), f32)]
        + [pltpu.VMEM(value.shape, f32) for value in stats]
        + [pltpu.SemaphoreType.DMA((len(stats),))],
        compiler_params=LIMIT,
        cost_estimate=pl.CostEstimate(
            flops=4 * depth * depth * cols,
            bytes_accessed=8 * sum(value.size for value in stats) + 2 * depth * depth,
            transcendentals=0,
        ),
    )(owner, *grad, *[in_hbm(value) for value in stats])


def weight_kernel(owner, weight, back, *refs):
    *norm, out = refs
    rows, cols = weight.shape[1:]

    def unit(u, carry):
        update = unpack(back, rows, cols, owner[u], 1).astype(f32)
        if norm:
            adam, *norms = norm
            total = norms[0][u]
            for other in norms[1:]:
                total = total + other[u]
            update = jnp.sqrt(adam[u] / (total + graft_eps))[:1, :1] * update
        out[u] = weight[u] - learn_rate * update
        return carry

    lax.fori_loop(0, weight.shape[0], unit, 0, unroll=weight.shape[0] <= 4)


def weight_part(owner, weight, back, *norm):
    return pl.pallas_call(
        weight_kernel,
        out_shape=jax.ShapeDtypeStruct(weight.shape, f32),
        in_specs=[SMEM] + [VMEM] * (2 + len(norm)),
        out_specs=VMEM,
        compiler_params=LIMIT,
        cost_estimate=pl.CostEstimate(
            flops=2 * weight.size, bytes_accessed=12 * weight.size, transcendentals=0
        ),
    )(owner, weight, back, *norm)


def totals_kernel(rows, cols, owner, back, norm, adam):
    def unit(u, carry):
        for n, ref in enumerate((norm, adam)):
            total = unpack_total(back, rows, cols, n, owner[u], 1)
            ref[u] = jnp.broadcast_to(total, ref.shape[1:])
        return carry

    lax.fori_loop(0, norm.shape[0], unit, 0, unroll=norm.shape[0] <= 4)


def totals_part(owner, back, rows, cols):
    small = jax.ShapeDtypeStruct((owner.shape[0], 8, LANES), f32)
    norm, adam = pl.pallas_call(
        functools.partial(totals_kernel, rows, cols),
        out_shape=(small, small),
        in_specs=[SMEM, VMEM],
        out_specs=(VMEM, VMEM),
        compiler_params=LIMIT,
        cost_estimate=BRIEF,
    )(owner, back)
    return adam, *all_norms(norm)


def all_norms(norm):
    return [norm] + [flip(norm, k) for k in range(1, lax.axis_size("tensor"))]


def flip(value, bits):
    size = lax.axis_size("tensor")
    return lax.ppermute(value, "tensor", [(i, i ^ bits) for i in range(size)])


def spread_first(value):
    return value, flip(value, lax.axis_size("tensor") // 2)


def spread_rest(value, far):
    bit = lax.axis_size("tensor") // 2
    held = {0: value, bit: far}
    bit //= 2
    while bit:
        for k in sorted(held):
            held[k | bit] = flip(held[k], bit)
        bit //= 2
    return [held[k] for k in range(len(held))]


def after(value, *others):
    return lax.optimization_barrier((value, *others))[0]


def over_shard(value):
    return lax.all_to_all(value, "shard", split_axis=0, concat_axis=0, tiled=True)


def scale_kernel(done, adam, *refs):
    norm, out = refs[:-1], refs[-1]
    total = norm[0][...]
    for other in norm[1:]:
        total = total + other[...]
    scale = jnp.sqrt(adam[...] / (total + graft_eps))[:1, :1]
    rows = done.shape[0] // out.shape[0]
    for slot in range(out.shape[0]):
        pack(out.at[slot], scale * done[slot * rows : (slot + 1) * rows, :], ())


def grafted(done, norm, adam, owners):
    depth, cols = done.shape
    norms = all_norms(norm)
    return pl.pallas_call(
        scale_kernel,
        out_shape=jax.ShapeDtypeStruct((owners, *packed_shape(depth // owners, cols, 0)), bf16),
        in_specs=[VMEM] * (2 + len(norms)),
        out_specs=VMEM,
        compiler_params=LIMIT,
        cost_estimate=pl.CostEstimate(
            flops=done.size, bytes_accessed=6 * done.size, transcendentals=0
        ),
    )(done, adam, *norms)


def per_device(
    att_grads,
    glu_grads,
    att_weight,
    att_moment,
    att_second,
    glu_weight,
    glu_moment,
    glu_second,
    att_stats,
    att_left_root,
    att_right_root,
    glu_left_stat,
    glu_right_stat,
    glu_left_root,
    glu_right_root,
    att_owner,
    glu_owner,
):
    owners = lax.axis_size("shard")
    rows = att_weight.shape[1]
    glu_packed, glu_moment_out, glu_second_out = adam_part(
        glu_owner, glu_grads, glu_moment, glu_second, owners, None
    )
    glu_root, glu_root_far = spread_first(glu_left_root[0])
    att_root, att_root_far = spread_first(att_left_root[0])
    att_packed, att_moment_out, att_second_out = adam_part(
        att_owner,
        after(att_grads, glu_root_far, att_root_far),
        att_moment,
        att_second,
        owners,
        LIMIT,
    )
    glu_left = spread_rest(glu_root, glu_root_far)
    att_left = spread_rest(att_root, att_root_far)
    glu_near, glu_far = spread_first(
        after(over_shard(glu_packed), att_packed, *glu_left[1:], *att_left[1:])
    )
    glu_grad = spread_rest(glu_near, glu_far)
    (glu_done,) = shampoo_part(glu_owner, glu_left, glu_grad, glu_right_root, rows, True)
    att_near, att_far = spread_first(after(over_shard(att_packed), glu_done))
    att_grad = spread_rest(att_near, att_far)
    glu_back = over_shard(after(glu_done, att_grad[1]))
    att_done = shampoo_part(att_owner, att_left, att_grad, att_right_root, rows, False)
    glu_left_out, glu_right_out = stats_part(
        glu_owner,
        [after(glu_grad[0], att_done[0]), *glu_grad[1:]],
        (glu_left_stat, glu_right_stat),
        rows,
        glu_weight.shape[2],
    )
    att_done = (after(att_done[0], glu_left_out), *att_done[1:])
    (att_stats_out,) = stats_part(att_owner, att_grad, (att_stats,), rows, att_weight.shape[2])
    att_back = over_shard(grafted(*att_done, owners))
    glu_totals = totals_part(glu_owner, glu_back, rows, glu_weight.shape[2])
    glu_weight_out = weight_part(glu_owner, glu_weight, glu_back, *glu_totals)
    att_weight_out = weight_part(att_owner, att_weight, att_back)
    return (
        att_weight_out,
        att_moment_out,
        att_second_out,
        glu_weight_out,
        glu_moment_out,
        glu_second_out,
        att_stats_out,
        glu_left_out,
        glu_right_out,
    )


def solution(mesh):
    placed = (
        P(None, None, "shard", "tensor"),
        P(None, None, "shard", "tensor"),
        P(None, "shard", "tensor"),
        P(None, "shard", "tensor"),
        P(None, "shard", "tensor"),
        P(None, "shard", "tensor"),
        P(None, "shard", "tensor"),
        P(None, "shard", "tensor"),
        P("shard", None, "tensor", None),
        P("shard", "tensor", None),
        P("shard", None, "tensor"),
        P("shard", "tensor", None),
        P("shard", "tensor", None),
        P("shard", "tensor", None),
        P("shard", None, "tensor"),
        P(),
        P(),
    )
    return jax.shard_map(
        per_device,
        mesh=mesh,
        in_specs=placed,
        out_specs=(
            P(None, "shard", "tensor"),
            P(None, "shard", "tensor"),
            P(None, "shard", "tensor"),
            P(None, "shard", "tensor"),
            P(None, "shard", "tensor"),
            P(None, "shard", "tensor"),
            P("shard", None, "tensor", None),
            P("shard", "tensor", None),
            P("shard", "tensor", None),
        ),
        check_vma=False,
    )
```

```python
import functools

import jax
import jax.numpy as jnp
from jax import lax
from jax.experimental import pallas as pl
from jax.experimental.pallas import tpu as pltpu
from jax.sharding import PartitionSpec as P

beta_one = 0.9
beta_two = 0.999
beta_stat = 0.999
adam_eps = 1e-08
graft_eps = 1e-06
learn_rate = 0.01

bf16 = jnp.bfloat16
f32 = jnp.float32
LANES = 128
VMEM = pl.BlockSpec(memory_space=pltpu.VMEM)
BRIEF = pl.CostEstimate(flops=1_000_000_000, bytes_accessed=1024, transcendentals=0)
LIMIT = pltpu.CompilerParams(vmem_limit_bytes=16 << 20)
SMEM = pl.BlockSpec(memory_space=pltpu.SMEM)
HBM = pl.BlockSpec(memory_space=pltpu.HBM)


def in_hbm(value):
    return pltpu.with_memory_space_constraint(value, pltpu.HBM)


def round_up(value, step):
    return -(-value // step) * step


def folds(rows, cols):
    return cols == LANES + LANES // 2 and rows % 32 == 0


def packed_shape(rows, cols, totals):
    lanes = round_up(cols, LANES)
    if folds(rows, cols):
        return (rows + rows // 2 + round_up(3 * totals, 8), LANES)
    return (rows, lanes) if lanes > cols else (round_up(rows + 3 * totals, 8), cols)


def pieces(totals, shape):
    row = lax.broadcasted_iota(jnp.int32, shape, 0)
    column = lax.broadcasted_iota(jnp.int32, shape, 1)
    value = jnp.zeros(shape, f32)
    for n, total in enumerate(totals):
        rest = jnp.broadcast_to(total, shape)
        for m in range(3):
            piece = rest.astype(bf16).astype(f32)
            value = jnp.where(row == 3 * n + m, piece, value)
            rest = rest - piece
    return jnp.where(column == 0, value, 0.0).astype(bf16)


def pack(ref, value, totals):
    rows, cols = value.shape
    high, wide = ref.shape
    if folds(rows, cols):
        half, side = rows // 2, value[:, LANES:]
        ref[:rows, :] = value[:, :LANES].astype(bf16)
        ref[rows : rows + half, :] = jnp.concatenate([side[:half], side[half:]], axis=1).astype(bf16)
        if totals:
            ref[rows + half :, :] = pieces(totals, (high - rows - half, wide))
    elif wide > cols:
        ref[:, :cols] = value.astype(bf16)
        ref[:, cols:] = pieces(totals, (high, wide - cols))
    else:
        ref[:rows, :] = value.astype(bf16)
        if totals:
            ref[rows:, :] = pieces(totals, (high - rows, wide))


def unpack(ref, rows, cols, start=0, count=None):
    count = ref.shape[0] if count is None else count
    span = pl.ds(start, count)
    if not folds(rows, cols):
        return ref[span, :rows, :cols].reshape(count * rows, cols)
    side = ref[span, rows : rows + rows // 2, :]
    side = jnp.concatenate([side[:, :, : LANES // 2], side[:, :, LANES // 2 :]], axis=1)
    return jnp.concatenate([ref[span, :rows, :], side], axis=2).reshape(count * rows, cols)


def unpack_total(ref, rows, cols, n, start=0, count=None):
    count = ref.shape[0] if count is None else count
    span = pl.ds(start, count)
    if folds(rows, cols):
        extra = ref[span, rows + rows // 2 :, :]
    elif ref.shape[2] > cols:
        extra = ref[span, :, cols:]
    else:
        extra = ref[span, rows:, :]
    row = lax.broadcasted_iota(jnp.int32, extra.shape, 1)
    mine = jnp.where((row >= 3 * n) & (row < 3 * n + 3), extra.astype(f32), 0.0)
    return jnp.sum(jnp.sum(mine, axis=0), axis=(0, 1), keepdims=True)


def adam_kernel(owner, grads, moment, second, packed, moment_out, second_out):
    packed[...] = jnp.zeros_like(packed)

    def unit(u, carry):
        summed = grads[0, u]
        for micro in range(1, grads.shape[0]):
            summed = summed + grads[micro, u]
        moment_new = beta_one * moment[u] + (1.0 - beta_one) * summed
        second_new = beta_two * second[u] + (1.0 - beta_two) * summed * summed
        direction = moment_new / (jnp.sqrt(second_new) + adam_eps)
        moment_out[u] = moment_new
        second_out[u] = second_new
        total = jnp.sum(direction * direction, axis=(0, 1), keepdims=True)
        pack(packed.at[owner[u]], summed, (total,))
        return carry

    lax.fori_loop(0, moment.shape[0], unit, 0, unroll=moment.shape[0] <= 4)


def adam_part(owner, grads, moment, second, owners, params):
    rows, cols = moment.shape[1:]
    return pl.pallas_call(
        adam_kernel,
        out_shape=(
            jax.ShapeDtypeStruct((owners, *packed_shape(rows, cols, 1)), bf16),
            jax.ShapeDtypeStruct(moment.shape, f32),
            jax.ShapeDtypeStruct(second.shape, f32),
        ),
        in_specs=[SMEM, VMEM, VMEM, VMEM],
        out_specs=(VMEM, VMEM, VMEM),
        compiler_params=params,
        cost_estimate=pl.CostEstimate(
            flops=10_000_000_000, bytes_accessed=32 * moment.size, transcendentals=moment.size
        ),
    )(owner, grads, moment, second)


def holds(owner):
    me = lax.axis_index("shard")
    found = owner[0] == me
    for unit in range(1, owner.shape[0]):
        found = jnp.logical_or(found, owner[unit] == me)
    return found


def shampoo_kernel(rows, cols, turned, embed, owner, *refs):
    tensor = lax.axis_size("tensor")
    left, grad = refs[:tensor], refs[tensor : 2 * tensor]
    root_hbm, *outs, whole, blocks, done, root, arrived = refs[2 * tensor :]
    part = lax.axis_index("tensor")

    @pl.when(holds(owner))
    def _():
        depth = left[0].shape[0]
        fetch = pltpu.make_async_copy(root_hbm, root, arrived)
        fetch.start()
        adam_sq = jnp.zeros((1, 1), f32)
        for k in range(tensor):
            band = pl.ds(pl.multiple_of((part ^ k) * depth, depth), depth)
            whole[band, :] = left[k][...]
            blocks[part ^ k] = unpack(grad[k], rows, cols)
            adam_sq = adam_sq + unpack_total(grad[k], rows, cols, 0)
        half = jnp.zeros((whole.shape[0], cols), f32)
        fetch.wait()
        for k in range(tensor):
            span = slice(k * cols, (k + 1) * cols)
            if turned:
                sides, right = (((1,), (1,)), ((), ())), root[0, :, span]
            else:
                sides, right = (((1,), (0,)), ((), ())), root[0, span, :]
            half = half + lax.dot_general(blocks[k], right, sides, preferred_element_type=f32)
        total = jnp.dot(whole[...], half.astype(bf16), preferred_element_type=f32)
        norm = jnp.sum(total * total, axis=(0, 1), keepdims=True)
        if embed:
            done[...] = total
            for slot in range(outs[0].shape[0]):
                value = done[slot * rows : (slot + 1) * rows, :]
                pack(outs[0].at[slot], value, (norm, adam_sq))
        else:
            for ref, value in zip(outs, (total, norm, adam_sq)):
                ref[...] = jnp.broadcast_to(value, ref.shape)

    @pl.when(jnp.logical_not(holds(owner)))
    def _():
        for ref in outs:
            ref[...] = jnp.zeros_like(ref)


def shampoo_part(owner, left, grad, root, rows, embed):
    cols = root.shape[2]
    depth = left[0].shape[1]
    tensor = len(left)
    turned = cols % LANES != 0
    if turned:
        root = jnp.swapaxes(root, 1, 2)
    if embed:
        shapes = (jax.ShapeDtypeStruct((depth // rows, *packed_shape(rows, cols, 2)), bf16),)
    else:
        small = jax.ShapeDtypeStruct((8, LANES), f32)
        shapes = (jax.ShapeDtypeStruct((depth, cols), f32), small, small)
    return pl.pallas_call(
        functools.partial(shampoo_kernel, rows, cols, turned, embed),
        out_shape=shapes,
        in_specs=[SMEM] + [VMEM] * (2 * tensor) + [HBM],
        out_specs=(VMEM,) * len(shapes),
        scratch_shapes=[
            pltpu.VMEM((depth, depth), bf16),
            pltpu.VMEM((tensor, depth, cols), bf16),
            pltpu.VMEM((depth, cols) if embed else (8, LANES), f32),
            pltpu.VMEM(root.shape, bf16),
            pltpu.SemaphoreType.DMA(()),
        ],
        compiler_params=LIMIT,
        cost_estimate=BRIEF,
    )(owner, *left, *grad, in_hbm(root))


def stats_kernel(rows, cols, paired, owner, *refs):
    tensor = lax.axis_size("tensor")
    grad, count = refs[:tensor], 1 if paired else 2
    stats, outs = refs[tensor : tensor + count], refs[tensor + count : tensor + 2 * count]
    square, held, (arrived, sent) = refs[tensor + 2 * count], refs[-count - 2 : -2], refs[-2:]

    def sides(group):
        return [group[0].at[0, 0], group[0].at[0, 1]] if paired else [ref.at[0] for ref in group]

    left, right = sides(held)
    fetches, stores = [], []
    for i, (source, slot, target) in enumerate(zip(sides(stats), (left, right), sides(outs))):
        fetches.append(pltpu.make_async_copy(source, slot, arrived.at[i]))
        stores.append(pltpu.make_async_copy(slot, target, sent.at[i]))
        fetches[-1].start()
    part = lax.axis_index("tensor")

    @pl.when(holds(owner))
    def _():
        high = left.shape[0]
        total = jnp.zeros(left.shape, f32)
        mine = unpack(grad[0], rows, cols)
        for k in range(tensor):
            columns = unpack(grad[k], rows, cols)
            slots = high // rows
            band = unpack(grad[k], rows, cols, part * slots, slots)
            total = total + lax.dot_general(
                band, columns, (((1,), (1,)), ((), ())), preferred_element_type=f32
            )
            square[part ^ k] = lax.dot_general(
                mine, columns, (((0,), (0,)), ((), ())), preferred_element_type=f32
            )
        fetches[0].wait()
        left[...] = beta_stat * left[...] + (1.0 - beta_stat) * total
        stores[0].start()
        fetches[1].wait()
        for k in range(tensor):
            span = slice(k * cols, (k + 1) * cols)
            right[:, span] = beta_stat * right[:, span] + (1.0 - beta_stat) * square[k]
        stores[1].start()
        for store in stores:
            store.wait()

    @pl.when(jnp.logical_not(holds(owner)))
    def _():
        for fetch, store in zip(fetches, stores):
            fetch.wait()
            store.start()
        for store in stores:
            store.wait()


def stats_part(owner, grad, stats, rows, cols):
    tensor = len(grad)
    depth = tensor * cols
    return pl.pallas_call(
        functools.partial(stats_kernel, rows, cols, len(stats) == 1),
        out_shape=tuple(jax.ShapeDtypeStruct(value.shape, f32) for value in stats),
        in_specs=[SMEM] + [VMEM] * tensor + [HBM] * len(stats),
        out_specs=(HBM,) * len(stats),
        scratch_shapes=[pltpu.VMEM((tensor, cols, cols), f32)]
        + [pltpu.VMEM(value.shape, f32) for value in stats]
        + [pltpu.SemaphoreType.DMA((2,)), pltpu.SemaphoreType.DMA((2,))],
        compiler_params=LIMIT,
        cost_estimate=pl.CostEstimate(
            flops=4 * depth * depth * cols,
            bytes_accessed=8 * sum(value.size for value in stats) + 2 * depth * depth,
            transcendentals=0,
        ),
    )(owner, *grad, *[in_hbm(value) for value in stats])


def weight_kernel(owner, weight, back, *refs):
    *norm, out = refs
    rows, cols = weight.shape[1:]

    def unit(u, carry):
        update = unpack(back, rows, cols, owner[u], 1).astype(f32)
        if norm:
            adam, *norms = norm
            total = norms[0][u]
            for other in norms[1:]:
                total = total + other[u]
            update = jnp.sqrt(adam[u] / (total + graft_eps))[:1, :1] * update
        out[u] = weight[u] - learn_rate * update
        return carry

    lax.fori_loop(0, weight.shape[0], unit, 0, unroll=weight.shape[0] <= 4)


def weight_part(owner, weight, back, *norm):
    return pl.pallas_call(
        weight_kernel,
        out_shape=jax.ShapeDtypeStruct(weight.shape, f32),
        in_specs=[SMEM] + [VMEM] * (2 + len(norm)),
        out_specs=VMEM,
        compiler_params=LIMIT,
        cost_estimate=pl.CostEstimate(
            flops=2 * weight.size, bytes_accessed=12 * weight.size, transcendentals=0
        ),
    )(owner, weight, back, *norm)


def totals_kernel(rows, cols, owner, back, norm, adam):
    def unit(u, carry):
        for n, ref in enumerate((norm, adam)):
            total = unpack_total(back, rows, cols, n, owner[u], 1)
            ref[u] = jnp.broadcast_to(total, ref.shape[1:])
        return carry

    lax.fori_loop(0, norm.shape[0], unit, 0, unroll=norm.shape[0] <= 4)


def totals_part(owner, back, rows, cols):
    small = jax.ShapeDtypeStruct((owner.shape[0], 8, LANES), f32)
    norm, adam = pl.pallas_call(
        functools.partial(totals_kernel, rows, cols),
        out_shape=(small, small),
        in_specs=[SMEM, VMEM],
        out_specs=(VMEM, VMEM),
        compiler_params=LIMIT,
        cost_estimate=BRIEF,
    )(owner, back)
    return adam, *all_norms(norm)


def all_norms(norm):
    return [norm] + [flip(norm, k) for k in range(1, lax.axis_size("tensor"))]


def flip(value, bits):
    size = lax.axis_size("tensor")
    return lax.ppermute(value, "tensor", [(i, i ^ bits) for i in range(size)])


def spread_first(value):
    return value, flip(value, lax.axis_size("tensor") // 2)


def spread_rest(value, far):
    bit = lax.axis_size("tensor") // 2
    held = {0: value, bit: far}
    bit //= 2
    while bit:
        for k in sorted(held):
            held[k | bit] = flip(held[k], bit)
        bit //= 2
    return [held[k] for k in range(len(held))]


def after(value, *others):
    return lax.optimization_barrier((value, *others))[0]


def over_shard(value):
    return lax.all_to_all(value, "shard", split_axis=0, concat_axis=0, tiled=True)


def scale_kernel(done, adam, *refs):
    norm, out = refs[:-1], refs[-1]
    total = norm[0][...]
    for other in norm[1:]:
        total = total + other[...]
    scale = jnp.sqrt(adam[...] / (total + graft_eps))[:1, :1]
    rows = done.shape[0] // out.shape[0]
    for slot in range(out.shape[0]):
        pack(out.at[slot], scale * done[slot * rows : (slot + 1) * rows, :], ())


def grafted(done, norm, adam, owners):
    depth, cols = done.shape
    norms = all_norms(norm)
    return pl.pallas_call(
        scale_kernel,
        out_shape=jax.ShapeDtypeStruct((owners, *packed_shape(depth // owners, cols, 0)), bf16),
        in_specs=[VMEM] * (2 + len(norms)),
        out_specs=VMEM,
        compiler_params=LIMIT,
        cost_estimate=pl.CostEstimate(
            flops=done.size, bytes_accessed=6 * done.size, transcendentals=0
        ),
    )(done, adam, *norms)


def per_device(
    att_grads,
    glu_grads,
    att_weight,
    att_moment,
    att_second,
    glu_weight,
    glu_moment,
    glu_second,
    att_stats,
    att_left_root,
    att_right_root,
    glu_left_stat,
    glu_right_stat,
    glu_left_root,
    glu_right_root,
    att_owner,
    glu_owner,
):
    owners = lax.axis_size("shard")
    rows = att_weight.shape[1]
    glu_packed, glu_moment_out, glu_second_out = adam_part(
        glu_owner, glu_grads, glu_moment, glu_second, owners, None
    )
    glu_root, glu_root_far = spread_first(glu_left_root[0])
    att_root, att_root_far = spread_first(att_left_root[0])
    att_packed, att_moment_out, att_second_out = adam_part(
        att_owner,
        after(att_grads, glu_root_far, att_root_far),
        att_moment,
        att_second,
        owners,
        LIMIT,
    )
    glu_near, glu_far = spread_first(after(over_shard(glu_packed), att_packed))
    glu_beside = flip(glu_near, 1)
    glu_root, glu_root_far, _ = lax.optimization_barrier((glu_root, glu_root_far, glu_beside))
    glu_left = spread_rest(glu_root, glu_root_far)
    glu_grad = spread_rest(glu_near, glu_far)
    (glu_done,) = shampoo_part(glu_owner, glu_left, glu_grad, glu_right_root, rows, True)
    att_near, att_far = spread_first(after(over_shard(att_packed), glu_done))
    att_left = spread_rest(*lax.optimization_barrier((att_root, att_root_far, att_near))[:2])
    att_grad = spread_rest(att_near, att_far)
    glu_back = over_shard(after(glu_done, att_grad[1]))
    att_done = shampoo_part(att_owner, att_left, att_grad, att_right_root, rows, False)
    glu_left_out, glu_right_out = stats_part(
        glu_owner,
        [after(glu_grad[0], att_done[0]), *glu_grad[1:]],
        (glu_left_stat, glu_right_stat),
        rows,
        glu_weight.shape[2],
    )
    att_done = (after(att_done[0], glu_left_out), *att_done[1:])
    (att_stats_out,) = stats_part(att_owner, att_grad, (att_stats,), rows, att_weight.shape[2])
    att_back = over_shard(grafted(*att_done, owners))
    glu_totals = totals_part(glu_owner, glu_back, rows, glu_weight.shape[2])
    glu_weight_out = weight_part(glu_owner, glu_weight, glu_back, *glu_totals)
    att_weight_out = weight_part(att_owner, att_weight, att_back)
    return (
        att_weight_out,
        att_moment_out,
        att_second_out,
        glu_weight_out,
        glu_moment_out,
        glu_second_out,
        att_stats_out,
        glu_left_out,
        glu_right_out,
    )


def solution(mesh):
    placed = (
        P(None, None, "shard", "tensor"),
        P(None, None, "shard", "tensor"),
        P(None, "shard", "tensor"),
        P(None, "shard", "tensor"),
        P(None, "shard", "tensor"),
        P(None, "shard", "tensor"),
        P(None, "shard", "tensor"),
        P(None, "shard", "tensor"),
        P("shard", None, "tensor", None),
        P("shard", "tensor", None),
        P("shard", None, "tensor"),
        P("shard", "tensor", None),
        P("shard", "tensor", None),
        P("shard", "tensor", None),
        P("shard", None, "tensor"),
        P(),
        P(),
    )
    return jax.shard_map(
        per_device,
        mesh=mesh,
        in_specs=placed,
        out_specs=(
            P(None, "shard", "tensor"),
            P(None, "shard", "tensor"),
            P(None, "shard", "tensor"),
            P(None, "shard", "tensor"),
            P(None, "shard", "tensor"),
            P(None, "shard", "tensor"),
            P("shard", None, "tensor", None),
            P("shard", "tensor", None),
            P("shard", "tensor", None),
        ),
        check_vma=False,
    )
```

```python
import functools

import jax
import jax.numpy as jnp
from jax import lax
from jax.experimental import pallas as pl
from jax.experimental.pallas import tpu as pltpu
from jax.sharding import PartitionSpec as P

beta_one = 0.9
beta_two = 0.999
beta_stat = 0.999
adam_eps = 1e-08
graft_eps = 1e-06
learn_rate = 0.01

bf16 = jnp.bfloat16
f32 = jnp.float32
LANES = 128
VMEM = pl.BlockSpec(memory_space=pltpu.VMEM)
BRIEF = pl.CostEstimate(flops=1_000_000_000, bytes_accessed=1024, transcendentals=0)
LIMIT = pltpu.CompilerParams(vmem_limit_bytes=16 << 20)
SMEM = pl.BlockSpec(memory_space=pltpu.SMEM)
HBM = pl.BlockSpec(memory_space=pltpu.HBM)


def in_hbm(value):
    return pltpu.with_memory_space_constraint(value, pltpu.HBM)


def round_up(value, step):
    return -(-value // step) * step


def folds(rows, cols):
    return cols == LANES + LANES // 2 and rows % 32 == 0


def packed_shape(rows, cols, totals):
    lanes = round_up(cols, LANES)
    if folds(rows, cols):
        return (rows + rows // 2 + round_up(3 * totals, 8), LANES)
    return (rows, lanes) if lanes > cols else (round_up(rows + 3 * totals, 8), cols)


def pieces(totals, shape):
    row = lax.broadcasted_iota(jnp.int32, shape, 0)
    column = lax.broadcasted_iota(jnp.int32, shape, 1)
    value = jnp.zeros(shape, f32)
    for n, total in enumerate(totals):
        rest = jnp.broadcast_to(total, shape)
        for m in range(3):
            piece = rest.astype(bf16).astype(f32)
            value = jnp.where(row == 3 * n + m, piece, value)
            rest = rest - piece
    return jnp.where(column == 0, value, 0.0).astype(bf16)


def pack(ref, value, totals):
    rows, cols = value.shape
    high, wide = ref.shape
    if folds(rows, cols):
        half, side = rows // 2, value[:, LANES:]
        ref[:rows, :] = value[:, :LANES].astype(bf16)
        ref[rows : rows + half, :] = jnp.concatenate([side[:half], side[half:]], axis=1).astype(bf16)
        if totals:
            ref[rows + half :, :] = pieces(totals, (high - rows - half, wide))
    elif wide > cols:
        ref[:, :cols] = value.astype(bf16)
        ref[:, cols:] = pieces(totals, (high, wide - cols))
    else:
        ref[:rows, :] = value.astype(bf16)
        if totals:
            ref[rows:, :] = pieces(totals, (high - rows, wide))


def unpack(ref, rows, cols, start=0, count=None):
    count = ref.shape[0] if count is None else count
    span = pl.ds(start, count)
    if not folds(rows, cols):
        return ref[span, :rows, :cols].reshape(count * rows, cols)
    side = ref[span, rows : rows + rows // 2, :]
    side = jnp.concatenate([side[:, :, : LANES // 2], side[:, :, LANES // 2 :]], axis=1)
    return jnp.concatenate([ref[span, :rows, :], side], axis=2).reshape(count * rows, cols)


def unpack_total(ref, rows, cols, n, start=0, count=None):
    count = ref.shape[0] if count is None else count
    span = pl.ds(start, count)
    if folds(rows, cols):
        extra = ref[span, rows + rows // 2 :, :]
    elif ref.shape[2] > cols:
        extra = ref[span, :, cols:]
    else:
        extra = ref[span, rows:, :]
    row = lax.broadcasted_iota(jnp.int32, extra.shape, 1)
    mine = jnp.where((row >= 3 * n) & (row < 3 * n + 3), extra.astype(f32), 0.0)
    return jnp.sum(jnp.sum(mine, axis=0), axis=(0, 1), keepdims=True)


def adam_kernel(owner, grads, moment, second, packed, moment_out, second_out):
    packed[...] = jnp.zeros_like(packed)

    def unit(u, carry):
        summed = grads[0, u]
        for micro in range(1, grads.shape[0]):
            summed = summed + grads[micro, u]
        moment_new = beta_one * moment[u] + (1.0 - beta_one) * summed
        second_new = beta_two * second[u] + (1.0 - beta_two) * summed * summed
        direction = moment_new / (jnp.sqrt(second_new) + adam_eps)
        moment_out[u] = moment_new
        second_out[u] = second_new
        total = jnp.sum(direction * direction, axis=(0, 1), keepdims=True)
        pack(packed.at[owner[u]], summed, (total,))
        return carry

    lax.fori_loop(0, moment.shape[0], unit, 0, unroll=moment.shape[0] <= 4)


def adam_part(owner, grads, moment, second, owners, params):
    rows, cols = moment.shape[1:]
    return pl.pallas_call(
        adam_kernel,
        out_shape=(
            jax.ShapeDtypeStruct((owners, *packed_shape(rows, cols, 1)), bf16),
            jax.ShapeDtypeStruct(moment.shape, f32),
            jax.ShapeDtypeStruct(second.shape, f32),
        ),
        in_specs=[SMEM, VMEM, VMEM, VMEM],
        out_specs=(VMEM, VMEM, VMEM),
        compiler_params=params,
        cost_estimate=pl.CostEstimate(
            flops=10_000_000_000, bytes_accessed=32 * moment.size, transcendentals=moment.size
        ),
    )(owner, grads, moment, second)


def holds(owner):
    me = lax.axis_index("shard")
    found = owner[0] == me
    for unit in range(1, owner.shape[0]):
        found = jnp.logical_or(found, owner[unit] == me)
    return found


def shampoo_kernel(rows, cols, turned, embed, owner, *refs):
    tensor = lax.axis_size("tensor")
    left, grad = refs[:tensor], refs[tensor : 2 * tensor]
    root, *outs, whole, blocks, done = refs[2 * tensor :]
    part = lax.axis_index("tensor")

    @pl.when(holds(owner))
    def _():
        depth = left[0].shape[0]
        adam_sq = jnp.zeros((1, 1), f32)
        for k in range(tensor):
            band = pl.ds(pl.multiple_of((part ^ k) * depth, depth), depth)
            whole[band, :] = left[k][...]
            blocks[part ^ k] = unpack(grad[k], rows, cols)
            adam_sq = adam_sq + unpack_total(grad[k], rows, cols, 0)
        half = jnp.zeros((whole.shape[0], cols), f32)
        for k in range(tensor):
            span = slice(k * cols, (k + 1) * cols)
            if turned:
                sides, right = (((1,), (1,)), ((), ())), root[0, :, span]
            else:
                sides, right = (((1,), (0,)), ((), ())), root[0, span, :]
            half = half + lax.dot_general(blocks[k], right, sides, preferred_element_type=f32)
        total = jnp.dot(whole[...], half.astype(bf16), preferred_element_type=f32)
        norm = jnp.sum(total * total, axis=(0, 1), keepdims=True)
        if embed:
            done[...] = total
            for slot in range(outs[0].shape[0]):
                value = done[slot * rows : (slot + 1) * rows, :]
                pack(outs[0].at[slot], value, (norm, adam_sq))
        else:
            for ref, value in zip(outs, (total, norm, adam_sq)):
                ref[...] = jnp.broadcast_to(value, ref.shape)

    @pl.when(jnp.logical_not(holds(owner)))
    def _():
        for ref in outs:
            ref[...] = jnp.zeros_like(ref)


def shampoo_part(owner, left, grad, root, rows, embed):
    cols = root.shape[2]
    depth = left[0].shape[1]
    tensor = len(left)
    turned = cols % LANES != 0
    if turned:
        root = jnp.swapaxes(root, 1, 2)
    if embed:
        shapes = (jax.ShapeDtypeStruct((depth // rows, *packed_shape(rows, cols, 2)), bf16),)
    else:
        small = jax.ShapeDtypeStruct((8, LANES), f32)
        shapes = (jax.ShapeDtypeStruct((depth, cols), f32), small, small)
    return pl.pallas_call(
        functools.partial(shampoo_kernel, rows, cols, turned, embed),
        out_shape=shapes,
        in_specs=[SMEM] + [VMEM] * (2 * tensor + 1),
        out_specs=(VMEM,) * len(shapes),
        scratch_shapes=[
            pltpu.VMEM((depth, depth), bf16),
            pltpu.VMEM((tensor, depth, cols), bf16),
            pltpu.VMEM((depth, cols) if embed else (8, LANES), f32),
        ],
        compiler_params=LIMIT,
        cost_estimate=pl.CostEstimate(
            flops=1_000_000_000 if embed else 2_000_000_000, bytes_accessed=1024, transcendentals=0
        ),
    )(owner, *left, *grad, root)


def stats_kernel(rows, cols, paired, owner, *refs):
    tensor = lax.axis_size("tensor")
    grad, count = refs[:tensor], 1 if paired else 2
    stats, outs = refs[tensor : tensor + count], refs[tensor + count : tensor + 2 * count]
    square, held, (arrived, sent) = refs[tensor + 2 * count], refs[-count - 2 : -2], refs[-2:]

    def sides(group):
        return [group[0].at[0, 0], group[0].at[0, 1]] if paired else [ref.at[0] for ref in group]

    left, right = sides(held)
    fetches, stores = [], []
    for i, (source, slot, target) in enumerate(zip(sides(stats), (left, right), sides(outs))):
        fetches.append(pltpu.make_async_copy(source, slot, arrived.at[i]))
        stores.append(pltpu.make_async_copy(slot, target, sent.at[i]))
        fetches[-1].start()
    part = lax.axis_index("tensor")

    @pl.when(holds(owner))
    def _():
        high = left.shape[0]
        total = jnp.zeros(left.shape, f32)
        mine = unpack(grad[0], rows, cols)
        for k in range(tensor):
            columns = unpack(grad[k], rows, cols)
            slots = high // rows
            band = unpack(grad[k], rows, cols, part * slots, slots)
            total = total + lax.dot_general(
                band, columns, (((1,), (1,)), ((), ())), preferred_element_type=f32
            )
            square[part ^ k] = lax.dot_general(
                mine, columns, (((0,), (0,)), ((), ())), preferred_element_type=f32
            )
        fetches[0].wait()
        left[...] = beta_stat * left[...] + (1.0 - beta_stat) * total
        stores[0].start()
        fetches[1].wait()
        for k in range(tensor):
            span = slice(k * cols, (k + 1) * cols)
            right[:, span] = beta_stat * right[:, span] + (1.0 - beta_stat) * square[k]
        stores[1].start()
        for store in stores:
            store.wait()

    @pl.when(jnp.logical_not(holds(owner)))
    def _():
        for fetch, store in zip(fetches, stores):
            fetch.wait()
            store.start()
        for store in stores:
            store.wait()


def stats_part(owner, grad, stats, rows, cols):
    tensor = len(grad)
    depth = tensor * cols
    return pl.pallas_call(
        functools.partial(stats_kernel, rows, cols, len(stats) == 1),
        out_shape=tuple(jax.ShapeDtypeStruct(value.shape, f32) for value in stats),
        in_specs=[SMEM] + [VMEM] * tensor + [HBM] * len(stats),
        out_specs=(HBM,) * len(stats),
        scratch_shapes=[pltpu.VMEM((tensor, cols, cols), f32)]
        + [pltpu.VMEM(value.shape, f32) for value in stats]
        + [pltpu.SemaphoreType.DMA((2,)), pltpu.SemaphoreType.DMA((2,))],
        compiler_params=LIMIT,
        cost_estimate=pl.CostEstimate(
            flops=1_000_000_000,
            bytes_accessed=1024,
            transcendentals=0,
        ),
    )(owner, *grad, *[in_hbm(value) for value in stats])


def weight_kernel(owner, weight, back, *refs):
    *norm, out = refs
    rows, cols = weight.shape[1:]

    def unit(u, carry):
        update = unpack(back, rows, cols, owner[u], 1).astype(f32)
        if norm:
            adam, *norms = norm
            total = norms[0][u]
            for other in norms[1:]:
                total = total + other[u]
            update = jnp.sqrt(adam[u] / (total + graft_eps))[:1, :1] * update
        out[u] = weight[u] - learn_rate * update
        return carry

    lax.fori_loop(0, weight.shape[0], unit, 0, unroll=weight.shape[0] <= 4)


def weight_part(owner, weight, back, *norm):
    return pl.pallas_call(
        weight_kernel,
        out_shape=jax.ShapeDtypeStruct(weight.shape, f32),
        in_specs=[SMEM] + [VMEM] * (2 + len(norm)),
        out_specs=VMEM,
        compiler_params=LIMIT,
        cost_estimate=pl.CostEstimate(
            flops=2 * weight.size, bytes_accessed=12 * weight.size, transcendentals=0
        ),
    )(owner, weight, back, *norm)


def totals_kernel(rows, cols, owner, back, norm, adam):
    def unit(u, carry):
        for n, ref in enumerate((norm, adam)):
            total = unpack_total(back, rows, cols, n, owner[u], 1)
            ref[u] = jnp.broadcast_to(total, ref.shape[1:])
        return carry

    lax.fori_loop(0, norm.shape[0], unit, 0, unroll=norm.shape[0] <= 4)


def totals_part(owner, back, rows, cols):
    small = jax.ShapeDtypeStruct((owner.shape[0], 8, LANES), f32)
    norm, adam = pl.pallas_call(
        functools.partial(totals_kernel, rows, cols),
        out_shape=(small, small),
        in_specs=[SMEM, VMEM],
        out_specs=(VMEM, VMEM),
        compiler_params=LIMIT,
        cost_estimate=BRIEF,
    )(owner, back)
    return adam, *all_norms(norm)


def all_norms(norm):
    return [norm] + [flip(norm, k) for k in range(1, lax.axis_size("tensor"))]


def flip(value, bits):
    size = lax.axis_size("tensor")
    return lax.ppermute(value, "tensor", [(i, i ^ bits) for i in range(size)])


def spread_first(value):
    return value, flip(value, lax.axis_size("tensor") // 2)


def spread_rest(value, far):
    bit = lax.axis_size("tensor") // 2
    held = {0: value, bit: far}
    bit //= 2
    while bit:
        for k in sorted(held):
            held[k | bit] = flip(held[k], bit)
        bit //= 2
    return [held[k] for k in range(len(held))]


def after(value, *others):
    return lax.optimization_barrier((value, *others))[0]


def over_shard(value):
    return lax.all_to_all(value, "shard", split_axis=0, concat_axis=0, tiled=True)


def scale_kernel(done, adam, *refs):
    norm, out = refs[:-1], refs[-1]
    total = norm[0][...]
    for other in norm[1:]:
        total = total + other[...]
    scale = jnp.sqrt(adam[...] / (total + graft_eps))[:1, :1]
    rows = done.shape[0] // out.shape[0]
    for slot in range(out.shape[0]):
        pack(out.at[slot], scale * done[slot * rows : (slot + 1) * rows, :], ())


def grafted(done, norm, adam, owners):
    depth, cols = done.shape
    norms = all_norms(norm)
    return pl.pallas_call(
        scale_kernel,
        out_shape=jax.ShapeDtypeStruct((owners, *packed_shape(depth // owners, cols, 0)), bf16),
        in_specs=[VMEM] * (2 + len(norms)),
        out_specs=VMEM,
        compiler_params=LIMIT,
        cost_estimate=pl.CostEstimate(
            flops=done.size, bytes_accessed=6 * done.size, transcendentals=0
        ),
    )(done, adam, *norms)


def per_device(
    att_grads,
    glu_grads,
    att_weight,
    att_moment,
    att_second,
    glu_weight,
    glu_moment,
    glu_second,
    att_stats,
    att_left_root,
    att_right_root,
    glu_left_stat,
    glu_right_stat,
    glu_left_root,
    glu_right_root,
    att_owner,
    glu_owner,
):
    owners = lax.axis_size("shard")
    rows = att_weight.shape[1]
    glu_packed, glu_moment_out, glu_second_out = adam_part(
        glu_owner, glu_grads, glu_moment, glu_second, owners, None
    )
    glu_root, glu_root_far = spread_first(glu_left_root[0])
    att_root, att_root_far = spread_first(att_left_root[0])
    att_packed, att_moment_out, att_second_out = adam_part(
        att_owner,
        after(att_grads, glu_root_far, att_root_far),
        att_moment,
        att_second,
        owners,
        LIMIT,
    )
    glu_near, glu_far = spread_first(after(over_shard(glu_packed), att_packed))
    glu_beside = flip(glu_near, 1)
    glu_root, glu_root_far, _ = lax.optimization_barrier((glu_root, glu_root_far, glu_beside))
    glu_left = spread_rest(glu_root, glu_root_far)
    glu_grad = spread_rest(glu_near, glu_far)
    (glu_done,) = shampoo_part(glu_owner, glu_left, glu_grad, glu_right_root, rows, True)
    att_near, att_far = spread_first(after(over_shard(att_packed), glu_done))
    att_left = spread_rest(*lax.optimization_barrier((att_root, att_root_far, att_near))[:2])
    att_beside = flip(att_near, 1)
    glu_back = over_shard(after(glu_done, att_beside))
    glu_left_out, glu_right_out = stats_part(
        glu_owner,
        [after(glu_grad[0], att_beside), *glu_grad[1:]],
        (glu_left_stat, glu_right_stat),
        rows,
        glu_weight.shape[2],
    )
    att_grad = spread_rest(att_near, after(att_far, glu_left_out, *att_left[1:]))
    att_done = shampoo_part(att_owner, att_left, att_grad, att_right_root, rows, False)
    (att_stats_out,) = stats_part(att_owner, att_grad, (att_stats,), rows, att_weight.shape[2])
    att_back = over_shard(grafted(*att_done, owners))
    glu_totals = totals_part(glu_owner, glu_back, rows, glu_weight.shape[2])
    glu_weight_out = weight_part(glu_owner, glu_weight, glu_back, *glu_totals)
    att_weight_out = weight_part(att_owner, att_weight, att_back)
    return (
        att_weight_out,
        att_moment_out,
        att_second_out,
        glu_weight_out,
        glu_moment_out,
        glu_second_out,
        att_stats_out,
        glu_left_out,
        glu_right_out,
    )


def solution(mesh):
    placed = (
        P(None, None, "shard", "tensor"),
        P(None, None, "shard", "tensor"),
        P(None, "shard", "tensor"),
        P(None, "shard", "tensor"),
        P(None, "shard", "tensor"),
        P(None, "shard", "tensor"),
        P(None, "shard", "tensor"),
        P(None, "shard", "tensor"),
        P("shard", None, "tensor", None),
        P("shard", "tensor", None),
        P("shard", None, "tensor"),
        P("shard", "tensor", None),
        P("shard", "tensor", None),
        P("shard", "tensor", None),
        P("shard", None, "tensor"),
        P(),
        P(),
    )
    return jax.shard_map(
        per_device,
        mesh=mesh,
        in_specs=placed,
        out_specs=(
            P(None, "shard", "tensor"),
            P(None, "shard", "tensor"),
            P(None, "shard", "tensor"),
            P(None, "shard", "tensor"),
            P(None, "shard", "tensor"),
            P(None, "shard", "tensor"),
            P("shard", None, "tensor", None),
            P("shard", "tensor", None),
            P("shard", "tensor", None),
        ),
        check_vma=False,
    )
```

```python
import functools

import jax
import jax.numpy as jnp
from jax import lax
from jax.experimental import pallas as pl
from jax.experimental.pallas import tpu as pltpu
from jax.sharding import PartitionSpec as P

beta_one = 0.9
beta_two = 0.999
beta_stat = 0.999
adam_eps = 1e-08
graft_eps = 1e-06
learn_rate = 0.01

bf16 = jnp.bfloat16
f32 = jnp.float32
LANES = 128
VMEM = pl.BlockSpec(memory_space=pltpu.VMEM)
BRIEF = pl.CostEstimate(flops=1_000_000_000, bytes_accessed=1024, transcendentals=0)
LIMIT = pltpu.CompilerParams(vmem_limit_bytes=16 << 20)
SMEM = pl.BlockSpec(memory_space=pltpu.SMEM)
HBM = pl.BlockSpec(memory_space=pltpu.HBM)


def in_hbm(value):
    return pltpu.with_memory_space_constraint(value, pltpu.HBM)


def round_up(value, step):
    return -(-value // step) * step


def folds(rows, cols):
    return cols == LANES + LANES // 2 and rows % 32 == 0


def packed_shape(rows, cols, totals):
    lanes = round_up(cols, LANES)
    if folds(rows, cols):
        return (rows + rows // 2 + round_up(3 * totals, 8), LANES)
    return (rows, lanes) if lanes > cols else (round_up(rows + 3 * totals, 8), cols)


def pieces(totals, shape):
    row = lax.broadcasted_iota(jnp.int32, shape, 0)
    column = lax.broadcasted_iota(jnp.int32, shape, 1)
    value = jnp.zeros(shape, f32)
    for n, total in enumerate(totals):
        rest = jnp.broadcast_to(total, shape)
        for m in range(3):
            piece = rest.astype(bf16).astype(f32)
            value = jnp.where(row == 3 * n + m, piece, value)
            rest = rest - piece
    return jnp.where(column == 0, value, 0.0).astype(bf16)


def pack(ref, value, totals):
    rows, cols = value.shape
    high, wide = ref.shape
    if folds(rows, cols):
        half, side = rows // 2, value[:, LANES:]
        ref[:rows, :] = value[:, :LANES].astype(bf16)
        ref[rows : rows + half, :] = jnp.concatenate([side[:half], side[half:]], axis=1).astype(bf16)
        if totals:
            ref[rows + half :, :] = pieces(totals, (high - rows - half, wide))
    elif wide > cols:
        ref[:, :cols] = value.astype(bf16)
        ref[:, cols:] = pieces(totals, (high, wide - cols))
    else:
        ref[:rows, :] = value.astype(bf16)
        if totals:
            ref[rows:, :] = pieces(totals, (high - rows, wide))


def unpack(ref, rows, cols, start=0, count=None):
    count = ref.shape[0] if count is None else count
    span = pl.ds(start, count)
    if not folds(rows, cols):
        return ref[span, :rows, :cols].reshape(count * rows, cols)
    side = ref[span, rows : rows + rows // 2, :]
    side = jnp.concatenate([side[:, :, : LANES // 2], side[:, :, LANES // 2 :]], axis=1)
    return jnp.concatenate([ref[span, :rows, :], side], axis=2).reshape(count * rows, cols)


def unpack_total(ref, rows, cols, n, start=0, count=None):
    count = ref.shape[0] if count is None else count
    span = pl.ds(start, count)
    if folds(rows, cols):
        extra = ref[span, rows + rows // 2 :, :]
    elif ref.shape[2] > cols:
        extra = ref[span, :, cols:]
    else:
        extra = ref[span, rows:, :]
    row = lax.broadcasted_iota(jnp.int32, extra.shape, 1)
    mine = jnp.where((row >= 3 * n) & (row < 3 * n + 3), extra.astype(f32), 0.0)
    return jnp.sum(jnp.sum(mine, axis=0), axis=(0, 1), keepdims=True)


def adam_kernel(owner, grads, moment, second, packed, moment_out, second_out):
    packed[...] = jnp.zeros_like(packed)

    def unit(u, carry):
        summed = grads[0, u]
        for micro in range(1, grads.shape[0]):
            summed = summed + grads[micro, u]
        moment_new = beta_one * moment[u] + (1.0 - beta_one) * summed
        second_new = beta_two * second[u] + (1.0 - beta_two) * summed * summed
        direction = moment_new / (jnp.sqrt(second_new) + adam_eps)
        moment_out[u] = moment_new
        second_out[u] = second_new
        total = jnp.sum(direction * direction, axis=(0, 1), keepdims=True)
        pack(packed.at[owner[u]], summed, (total,))
        return carry

    lax.fori_loop(0, moment.shape[0], unit, 0, unroll=moment.shape[0] <= 4)


def adam_part(owner, grads, moment, second, owners, params):
    rows, cols = moment.shape[1:]
    return pl.pallas_call(
        adam_kernel,
        out_shape=(
            jax.ShapeDtypeStruct((owners, *packed_shape(rows, cols, 1)), bf16),
            jax.ShapeDtypeStruct(moment.shape, f32),
            jax.ShapeDtypeStruct(second.shape, f32),
        ),
        in_specs=[SMEM, VMEM, VMEM, VMEM],
        out_specs=(VMEM, VMEM, VMEM),
        compiler_params=params,
        cost_estimate=pl.CostEstimate(
            flops=10_000_000_000, bytes_accessed=32 * moment.size, transcendentals=moment.size
        ),
    )(owner, grads, moment, second)


def send_kernel(owner, grads, moment, second, packed, grad, first, square, arrived):
    packed[...] = jnp.zeros_like(packed)

    def copies(u):
        return [
            pltpu.make_async_copy(grads.at[:, u], grad.at[:, u], arrived.at[0, u]),
            pltpu.make_async_copy(moment.at[u], first.at[u], arrived.at[1, u]),
            pltpu.make_async_copy(second.at[u], square.at[u], arrived.at[2, u]),
        ]

    def fetch(u, carry):
        for copy in copies(u):
            copy.start()
        return carry

    def unit(u, carry):
        for copy in copies(u):
            copy.wait()
        summed = grad[0, u]
        for micro in range(1, grad.shape[0]):
            summed = summed + grad[micro, u]
        moment_new = beta_one * first[u] + (1.0 - beta_one) * summed
        second_new = beta_two * square[u] + (1.0 - beta_two) * summed * summed
        direction = moment_new / (jnp.sqrt(second_new) + adam_eps)
        total = jnp.sum(direction * direction, axis=(0, 1), keepdims=True)
        pack(packed.at[owner[u]], summed, (total,))
        return carry

    units = first.shape[0]
    lax.fori_loop(0, units, fetch, 0, unroll=units <= 4)
    lax.fori_loop(0, units, unit, 0, unroll=units <= 4)


def send_part(owner, grads, moment, second, owners):
    rows, cols = moment.shape[1:]
    return pl.pallas_call(
        send_kernel,
        out_shape=jax.ShapeDtypeStruct((owners, *packed_shape(rows, cols, 1)), bf16),
        in_specs=[SMEM, HBM, HBM, HBM],
        out_specs=VMEM,
        scratch_shapes=[
            pltpu.VMEM(grads.shape, f32),
            pltpu.VMEM(moment.shape, f32),
            pltpu.VMEM(second.shape, f32),
            pltpu.SemaphoreType.DMA((3, moment.shape[0])),
        ],
        cost_estimate=pl.CostEstimate(
            flops=10_000_000_000, bytes_accessed=32 * moment.size, transcendentals=moment.size
        ),
    )(owner, in_hbm(grads), in_hbm(moment), in_hbm(second))


def moments_kernel(grads, moment, second, moment_out, second_out):
    summed = grads[0]
    for micro in range(1, grads.shape[0]):
        summed = summed + grads[micro]
    moment_out[...] = beta_one * moment[...] + (1.0 - beta_one) * summed
    second_out[...] = beta_two * second[...] + (1.0 - beta_two) * summed * summed


def moments_part(grads, moment, second):
    return pl.pallas_call(
        moments_kernel,
        out_shape=(
            jax.ShapeDtypeStruct(moment.shape, f32),
            jax.ShapeDtypeStruct(second.shape, f32),
        ),
        in_specs=[VMEM, VMEM, VMEM],
        out_specs=(VMEM, VMEM),
        compiler_params=LIMIT,
        cost_estimate=BRIEF,
    )(grads, moment, second)


def holds(owner):
    me = lax.axis_index("shard")
    found = owner[0] == me
    for unit in range(1, owner.shape[0]):
        found = jnp.logical_or(found, owner[unit] == me)
    return found


def shampoo_kernel(rows, cols, turned, embed, owner, *refs):
    tensor = lax.axis_size("tensor")
    left, grad = refs[:tensor], refs[tensor : 2 * tensor]
    root, *outs, whole, blocks, done = refs[2 * tensor :]
    part = lax.axis_index("tensor")

    @pl.when(holds(owner))
    def _():
        depth = left[0].shape[0]
        adam_sq = jnp.zeros((1, 1), f32)
        for k in range(tensor):
            band = pl.ds(pl.multiple_of((part ^ k) * depth, depth), depth)
            whole[band, :] = left[k][...]
            blocks[part ^ k] = unpack(grad[k], rows, cols)
            adam_sq = adam_sq + unpack_total(grad[k], rows, cols, 0)
        half = jnp.zeros((whole.shape[0], cols), f32)
        for k in range(tensor):
            span = slice(k * cols, (k + 1) * cols)
            if turned:
                sides, right = (((1,), (1,)), ((), ())), root[0, :, span]
            else:
                sides, right = (((1,), (0,)), ((), ())), root[0, span, :]
            half = half + lax.dot_general(blocks[k], right, sides, preferred_element_type=f32)
        total = jnp.dot(whole[...], half.astype(bf16), preferred_element_type=f32)
        norm = jnp.sum(total * total, axis=(0, 1), keepdims=True)
        if embed:
            done[...] = total
            for slot in range(outs[0].shape[0]):
                value = done[slot * rows : (slot + 1) * rows, :]
                pack(outs[0].at[slot], value, (norm, adam_sq))
        else:
            for ref, value in zip(outs, (total, norm, adam_sq)):
                ref[...] = jnp.broadcast_to(value, ref.shape)

    @pl.when(jnp.logical_not(holds(owner)))
    def _():
        for ref in outs:
            ref[...] = jnp.zeros_like(ref)


def shampoo_part(owner, left, grad, root, rows, embed):
    cols = root.shape[2]
    depth = left[0].shape[1]
    tensor = len(left)
    turned = cols % LANES != 0
    if turned:
        root = jnp.swapaxes(root, 1, 2)
    if embed:
        shapes = (jax.ShapeDtypeStruct((depth // rows, *packed_shape(rows, cols, 2)), bf16),)
    else:
        small = jax.ShapeDtypeStruct((8, LANES), f32)
        shapes = (jax.ShapeDtypeStruct((depth, cols), f32), small, small)
    return pl.pallas_call(
        functools.partial(shampoo_kernel, rows, cols, turned, embed),
        out_shape=shapes,
        in_specs=[SMEM] + [VMEM] * (2 * tensor + 1),
        out_specs=(VMEM,) * len(shapes),
        scratch_shapes=[
            pltpu.VMEM((depth, depth), bf16),
            pltpu.VMEM((tensor, depth, cols), bf16),
            pltpu.VMEM((depth, cols) if embed else (8, LANES), f32),
        ],
        compiler_params=LIMIT,
        cost_estimate=pl.CostEstimate(
            flops=1_000_000_000 if embed else 2_000_000_000, bytes_accessed=1024, transcendentals=0
        ),
    )(owner, *left, *grad, root)


def stats_kernel(rows, cols, paired, owner, *refs):
    tensor = lax.axis_size("tensor")
    grad, count = refs[:tensor], 1 if paired else 2
    stats, outs = refs[tensor : tensor + count], refs[tensor + count : tensor + 2 * count]
    square, held, (arrived, sent) = refs[tensor + 2 * count], refs[-count - 2 : -2], refs[-2:]

    def sides(group):
        return [group[0].at[0, 0], group[0].at[0, 1]] if paired else [ref.at[0] for ref in group]

    left, right = sides(held)
    fetches, stores = [], []
    for i, (source, slot, target) in enumerate(zip(sides(stats), (left, right), sides(outs))):
        fetches.append(pltpu.make_async_copy(source, slot, arrived.at[i]))
        stores.append(pltpu.make_async_copy(slot, target, sent.at[i]))
        fetches[-1].start()
    part = lax.axis_index("tensor")

    @pl.when(holds(owner))
    def _():
        high = left.shape[0]
        total = jnp.zeros(left.shape, f32)
        mine = unpack(grad[0], rows, cols)
        for k in range(tensor):
            columns = unpack(grad[k], rows, cols)
            slots = high // rows
            band = unpack(grad[k], rows, cols, part * slots, slots)
            total = total + lax.dot_general(
                band, columns, (((1,), (1,)), ((), ())), preferred_element_type=f32
            )
            square[part ^ k] = lax.dot_general(
                mine, columns, (((0,), (0,)), ((), ())), preferred_element_type=f32
            )
        fetches[0].wait()
        left[...] = beta_stat * left[...] + (1.0 - beta_stat) * total
        stores[0].start()
        fetches[1].wait()
        for k in range(tensor):
            span = slice(k * cols, (k + 1) * cols)
            right[:, span] = beta_stat * right[:, span] + (1.0 - beta_stat) * square[k]
        stores[1].start()
        for store in stores:
            store.wait()

    @pl.when(jnp.logical_not(holds(owner)))
    def _():
        for fetch, store in zip(fetches, stores):
            fetch.wait()
            store.start()
        for store in stores:
            store.wait()


def stats_part(owner, grad, stats, rows, cols):
    tensor = len(grad)
    depth = tensor * cols
    return pl.pallas_call(
        functools.partial(stats_kernel, rows, cols, len(stats) == 1),
        out_shape=tuple(jax.ShapeDtypeStruct(value.shape, f32) for value in stats),
        in_specs=[SMEM] + [VMEM] * tensor + [HBM] * len(stats),
        out_specs=(HBM,) * len(stats),
        scratch_shapes=[pltpu.VMEM((tensor, cols, cols), f32)]
        + [pltpu.VMEM(value.shape, f32) for value in stats]
        + [pltpu.SemaphoreType.DMA((2,)), pltpu.SemaphoreType.DMA((2,))],
        compiler_params=LIMIT,
        cost_estimate=pl.CostEstimate(
            flops=1_000_000_000,
            bytes_accessed=1024,
            transcendentals=0,
        ),
    )(owner, *grad, *[in_hbm(value) for value in stats])


def weight_kernel(owner, weight, back, *refs):
    *norm, out = refs
    rows, cols = weight.shape[1:]

    def unit(u, carry):
        update = unpack(back, rows, cols, owner[u], 1).astype(f32)
        if norm:
            adam, *norms = norm
            total = norms[0][u]
            for other in norms[1:]:
                total = total + other[u]
            update = jnp.sqrt(adam[u] / (total + graft_eps))[:1, :1] * update
        out[u] = weight[u] - learn_rate * update
        return carry

    lax.fori_loop(0, weight.shape[0], unit, 0, unroll=weight.shape[0] <= 4)


def weight_part(owner, weight, back, *norm):
    return pl.pallas_call(
        weight_kernel,
        out_shape=jax.ShapeDtypeStruct(weight.shape, f32),
        in_specs=[SMEM] + [VMEM] * (2 + len(norm)),
        out_specs=VMEM,
        compiler_params=LIMIT,
        cost_estimate=pl.CostEstimate(
            flops=2 * weight.size, bytes_accessed=12 * weight.size, transcendentals=0
        ),
    )(owner, weight, back, *norm)


def totals_kernel(rows, cols, owner, back, norm, adam):
    def unit(u, carry):
        for n, ref in enumerate((norm, adam)):
            total = unpack_total(back, rows, cols, n, owner[u], 1)
            ref[u] = jnp.broadcast_to(total, ref.shape[1:])
        return carry

    lax.fori_loop(0, norm.shape[0], unit, 0, unroll=norm.shape[0] <= 4)


def totals_part(owner, back, rows, cols):
    small = jax.ShapeDtypeStruct((owner.shape[0], 8, LANES), f32)
    norm, adam = pl.pallas_call(
        functools.partial(totals_kernel, rows, cols),
        out_shape=(small, small),
        in_specs=[SMEM, VMEM],
        out_specs=(VMEM, VMEM),
        compiler_params=LIMIT,
        cost_estimate=BRIEF,
    )(owner, back)
    return adam, *all_norms(norm)


def all_norms(norm):
    return [norm] + [flip(norm, k) for k in range(1, lax.axis_size("tensor"))]


def flip(value, bits):
    size = lax.axis_size("tensor")
    return lax.ppermute(value, "tensor", [(i, i ^ bits) for i in range(size)])


def spread_first(value):
    return value, flip(value, lax.axis_size("tensor") // 2)


def spread_rest(value, far):
    bit = lax.axis_size("tensor") // 2
    held = {0: value, bit: far}
    bit //= 2
    while bit:
        for k in sorted(held):
            held[k | bit] = flip(held[k], bit)
        bit //= 2
    return [held[k] for k in range(len(held))]


def after(value, *others):
    return lax.optimization_barrier((value, *others))[0]


def over_shard(value):
    return lax.all_to_all(value, "shard", split_axis=0, concat_axis=0, tiled=True)


def scale_kernel(done, adam, *refs):
    norm, out = refs[:-1], refs[-1]
    total = norm[0][...]
    for other in norm[1:]:
        total = total + other[...]
    scale = jnp.sqrt(adam[...] / (total + graft_eps))[:1, :1]
    rows = done.shape[0] // out.shape[0]
    for slot in range(out.shape[0]):
        pack(out.at[slot], scale * done[slot * rows : (slot + 1) * rows, :], ())


def grafted(done, norm, adam, owners):
    depth, cols = done.shape
    norms = all_norms(norm)
    return pl.pallas_call(
        scale_kernel,
        out_shape=jax.ShapeDtypeStruct((owners, *packed_shape(depth // owners, cols, 0)), bf16),
        in_specs=[VMEM] * (2 + len(norms)),
        out_specs=VMEM,
        compiler_params=LIMIT,
        cost_estimate=pl.CostEstimate(
            flops=done.size, bytes_accessed=6 * done.size, transcendentals=0
        ),
    )(done, adam, *norms)


def per_device(
    att_grads,
    glu_grads,
    att_weight,
    att_moment,
    att_second,
    glu_weight,
    glu_moment,
    glu_second,
    att_stats,
    att_left_root,
    att_right_root,
    glu_left_stat,
    glu_right_stat,
    glu_left_root,
    glu_right_root,
    att_owner,
    glu_owner,
):
    owners = lax.axis_size("shard")
    rows = att_weight.shape[1]
    glu_packed = send_part(glu_owner, glu_grads, glu_moment, glu_second, owners)
    glu_root, glu_root_far = spread_first(glu_left_root[0])
    att_root, att_root_far = spread_first(att_left_root[0])
    glu_moment_out, glu_second_out = moments_part(
        after(glu_grads, glu_root_far), glu_moment, glu_second
    )
    att_packed, att_moment_out, att_second_out = adam_part(
        att_owner,
        after(att_grads, glu_moment_out, att_root_far),
        att_moment,
        att_second,
        owners,
        LIMIT,
    )
    glu_near, glu_far = spread_first(after(over_shard(glu_packed), att_packed))
    glu_beside = flip(glu_near, 1)
    glu_root, glu_root_far, _ = lax.optimization_barrier((glu_root, glu_root_far, glu_beside))
    glu_left = spread_rest(glu_root, glu_root_far)
    glu_grad = spread_rest(glu_near, glu_far)
    (glu_done,) = shampoo_part(glu_owner, glu_left, glu_grad, glu_right_root, rows, True)
    att_near, att_far = spread_first(after(over_shard(att_packed), glu_done))
    att_left = spread_rest(*lax.optimization_barrier((att_root, att_root_far, att_near))[:2])
    att_beside = flip(att_near, 1)
    glu_back = over_shard(after(glu_done, att_beside))
    glu_left_out, glu_right_out = stats_part(
        glu_owner,
        [after(glu_grad[0], att_beside), *glu_grad[1:]],
        (glu_left_stat, glu_right_stat),
        rows,
        glu_weight.shape[2],
    )
    att_grad = spread_rest(att_near, after(att_far, glu_left_out, *att_left[1:]))
    att_done = shampoo_part(att_owner, att_left, att_grad, att_right_root, rows, False)
    (att_stats_out,) = stats_part(att_owner, att_grad, (att_stats,), rows, att_weight.shape[2])
    att_back = over_shard(grafted(*att_done, owners))
    glu_totals = totals_part(glu_owner, glu_back, rows, glu_weight.shape[2])
    glu_weight_out = weight_part(glu_owner, glu_weight, glu_back, *glu_totals)
    att_weight_out = weight_part(att_owner, att_weight, att_back)
    return (
        att_weight_out,
        att_moment_out,
        att_second_out,
        glu_weight_out,
        glu_moment_out,
        glu_second_out,
        att_stats_out,
        glu_left_out,
        glu_right_out,
    )


def solution(mesh):
    placed = (
        P(None, None, "shard", "tensor"),
        P(None, None, "shard", "tensor"),
        P(None, "shard", "tensor"),
        P(None, "shard", "tensor"),
        P(None, "shard", "tensor"),
        P(None, "shard", "tensor"),
        P(None, "shard", "tensor"),
        P(None, "shard", "tensor"),
        P("shard", None, "tensor", None),
        P("shard", "tensor", None),
        P("shard", None, "tensor"),
        P("shard", "tensor", None),
        P("shard", "tensor", None),
        P("shard", "tensor", None),
        P("shard", None, "tensor"),
        P(),
        P(),
    )
    return jax.shard_map(
        per_device,
        mesh=mesh,
        in_specs=placed,
        out_specs=(
            P(None, "shard", "tensor"),
            P(None, "shard", "tensor"),
            P(None, "shard", "tensor"),
            P(None, "shard", "tensor"),
            P(None, "shard", "tensor"),
            P(None, "shard", "tensor"),
            P("shard", None, "tensor", None),
            P("shard", "tensor", None),
            P("shard", "tensor", None),
        ),
        check_vma=False,
    )
```

```python
import functools

import jax
import jax.numpy as jnp
from jax import lax
from jax.experimental import pallas as pl
from jax.experimental.pallas import tpu as pltpu
from jax.sharding import PartitionSpec as P

beta_one = 0.9
beta_two = 0.999
beta_stat = 0.999
adam_eps = 1e-08
graft_eps = 1e-06
learn_rate = 0.01

bf16 = jnp.bfloat16
f32 = jnp.float32
LANES = 128
VMEM = pl.BlockSpec(memory_space=pltpu.VMEM)
BRIEF = pl.CostEstimate(flops=1_000_000_000, bytes_accessed=1024, transcendentals=0)
LIMIT = pltpu.CompilerParams(vmem_limit_bytes=16 << 20)
SMEM = pl.BlockSpec(memory_space=pltpu.SMEM)
HBM = pl.BlockSpec(memory_space=pltpu.HBM)


def in_hbm(value):
    return pltpu.with_memory_space_constraint(value, pltpu.HBM)


def round_up(value, step):
    return -(-value // step) * step


def folds(rows, cols):
    return cols == LANES + LANES // 2 and rows % 32 == 0


def packed_shape(rows, cols, totals):
    lanes = round_up(cols, LANES)
    if folds(rows, cols):
        return (rows + rows // 2 + round_up(3 * totals, 8), LANES)
    return (rows, lanes) if lanes > cols else (round_up(rows + 3 * totals, 8), cols)


def pieces(totals, shape):
    row = lax.broadcasted_iota(jnp.int32, shape, 0)
    column = lax.broadcasted_iota(jnp.int32, shape, 1)
    value = jnp.zeros(shape, f32)
    for n, total in enumerate(totals):
        rest = jnp.broadcast_to(total, shape)
        for m in range(3):
            piece = rest.astype(bf16).astype(f32)
            value = jnp.where(row == 3 * n + m, piece, value)
            rest = rest - piece
    return jnp.where(column == 0, value, 0.0).astype(bf16)


def pack(ref, value, totals):
    rows, cols = value.shape
    high, wide = ref.shape
    if folds(rows, cols):
        half, side = rows // 2, value[:, LANES:]
        ref[:rows, :] = value[:, :LANES].astype(bf16)
        ref[rows : rows + half, :] = jnp.concatenate([side[:half], side[half:]], axis=1).astype(bf16)
        if totals:
            ref[rows + half :, :] = pieces(totals, (high - rows - half, wide))
    elif wide > cols:
        ref[:, :cols] = value.astype(bf16)
        ref[:, cols:] = pieces(totals, (high, wide - cols))
    else:
        ref[:rows, :] = value.astype(bf16)
        if totals:
            ref[rows:, :] = pieces(totals, (high - rows, wide))


def unpack(ref, rows, cols, start=0, count=None):
    count = ref.shape[0] if count is None else count
    span = pl.ds(start, count)
    if not folds(rows, cols):
        return ref[span, :rows, :cols].reshape(count * rows, cols)
    side = ref[span, rows : rows + rows // 2, :]
    side = jnp.concatenate([side[:, :, : LANES // 2], side[:, :, LANES // 2 :]], axis=1)
    return jnp.concatenate([ref[span, :rows, :], side], axis=2).reshape(count * rows, cols)


def unpack_total(ref, rows, cols, n, start=0, count=None):
    count = ref.shape[0] if count is None else count
    span = pl.ds(start, count)
    if folds(rows, cols):
        extra = ref[span, rows + rows // 2 :, :]
    elif ref.shape[2] > cols:
        extra = ref[span, :, cols:]
    else:
        extra = ref[span, rows:, :]
    row = lax.broadcasted_iota(jnp.int32, extra.shape, 1)
    mine = jnp.where((row >= 3 * n) & (row < 3 * n + 3), extra.astype(f32), 0.0)
    return jnp.sum(jnp.sum(mine, axis=0), axis=(0, 1), keepdims=True)


def adam_kernel(owner, grads, moment, second, packed, moment_out, second_out):
    packed[...] = jnp.zeros_like(packed)

    def unit(u, carry):
        summed = grads[0, u]
        for micro in range(1, grads.shape[0]):
            summed = summed + grads[micro, u]
        moment_new = beta_one * moment[u] + (1.0 - beta_one) * summed
        second_new = beta_two * second[u] + (1.0 - beta_two) * summed * summed
        direction = moment_new / (jnp.sqrt(second_new) + adam_eps)
        moment_out[u] = moment_new
        second_out[u] = second_new
        total = jnp.sum(direction * direction, axis=(0, 1), keepdims=True)
        pack(packed.at[owner[u]], summed, (total,))
        return carry

    lax.fori_loop(0, moment.shape[0], unit, 0, unroll=moment.shape[0] <= 4)


def adam_part(owner, grads, moment, second, owners, params):
    rows, cols = moment.shape[1:]
    return pl.pallas_call(
        adam_kernel,
        out_shape=(
            jax.ShapeDtypeStruct((owners, *packed_shape(rows, cols, 1)), bf16),
            jax.ShapeDtypeStruct(moment.shape, f32),
            jax.ShapeDtypeStruct(second.shape, f32),
        ),
        in_specs=[SMEM, VMEM, VMEM, VMEM],
        out_specs=(VMEM, VMEM, VMEM),
        compiler_params=params,
        cost_estimate=pl.CostEstimate(
            flops=10_000_000_000, bytes_accessed=32 * moment.size, transcendentals=moment.size
        ),
    )(owner, grads, moment, second)


def send_kernel(owner, grads, moment, second, packed):
    packed[...] = jnp.zeros_like(packed)

    def unit(u, carry):
        summed = grads[0, u]
        for micro in range(1, grads.shape[0]):
            summed = summed + grads[micro, u]
        moment_new = beta_one * moment[u] + (1.0 - beta_one) * summed
        second_new = beta_two * second[u] + (1.0 - beta_two) * summed * summed
        direction = moment_new / (jnp.sqrt(second_new) + adam_eps)
        total = jnp.sum(direction * direction, axis=(0, 1), keepdims=True)
        pack(packed.at[owner[u]], summed, (total,))
        return carry

    lax.fori_loop(0, moment.shape[0], unit, 0, unroll=moment.shape[0] <= 4)


def send_part(owner, grads, moment, second, owners):
    rows, cols = moment.shape[1:]
    return pl.pallas_call(
        send_kernel,
        out_shape=jax.ShapeDtypeStruct((owners, *packed_shape(rows, cols, 1)), bf16),
        in_specs=[SMEM, VMEM, VMEM, VMEM],
        out_specs=VMEM,
        cost_estimate=pl.CostEstimate(
            flops=10_000_000_000, bytes_accessed=32 * moment.size, transcendentals=moment.size
        ),
    )(owner, grads, moment, second)


def moments_kernel(grads, moment, second, moment_out, second_out):
    summed = grads[0]
    for micro in range(1, grads.shape[0]):
        summed = summed + grads[micro]
    moment_out[...] = beta_one * moment[...] + (1.0 - beta_one) * summed
    second_out[...] = beta_two * second[...] + (1.0 - beta_two) * summed * summed


def moments_part(grads, moment, second):
    return pl.pallas_call(
        moments_kernel,
        out_shape=(
            jax.ShapeDtypeStruct(moment.shape, f32),
            jax.ShapeDtypeStruct(second.shape, f32),
        ),
        in_specs=[VMEM, VMEM, VMEM],
        out_specs=(VMEM, VMEM),
        compiler_params=LIMIT,
        cost_estimate=BRIEF,
    )(grads, moment, second)


def holds(owner):
    me = lax.axis_index("shard")
    found = owner[0] == me
    for unit in range(1, owner.shape[0]):
        found = jnp.logical_or(found, owner[unit] == me)
    return found


def shampoo_kernel(rows, cols, turned, embed, owner, *refs):
    tensor = lax.axis_size("tensor")
    left, grad = refs[:tensor], refs[tensor : 2 * tensor]
    root, *outs, whole, blocks, done = refs[2 * tensor :]
    part = lax.axis_index("tensor")

    @pl.when(holds(owner))
    def _():
        depth = left[0].shape[0]
        adam_sq = jnp.zeros((1, 1), f32)
        for k in range(tensor):
            band = pl.ds(pl.multiple_of((part ^ k) * depth, depth), depth)
            whole[band, :] = left[k][...]
            blocks[part ^ k] = unpack(grad[k], rows, cols)
            adam_sq = adam_sq + unpack_total(grad[k], rows, cols, 0)
        half = jnp.zeros((whole.shape[0], cols), f32)
        for k in range(tensor):
            span = slice(k * cols, (k + 1) * cols)
            if turned:
                sides, right = (((1,), (1,)), ((), ())), root[0, :, span]
            else:
                sides, right = (((1,), (0,)), ((), ())), root[0, span, :]
            half = half + lax.dot_general(blocks[k], right, sides, preferred_element_type=f32)
        total = jnp.dot(whole[...], half.astype(bf16), preferred_element_type=f32)
        norm = jnp.sum(total * total, axis=(0, 1), keepdims=True)
        if embed:
            done[...] = total
            for slot in range(outs[0].shape[0]):
                value = done[slot * rows : (slot + 1) * rows, :]
                pack(outs[0].at[slot], value, (norm, adam_sq))
        else:
            for ref, value in zip(outs, (total, norm, adam_sq)):
                ref[...] = jnp.broadcast_to(value, ref.shape)

    @pl.when(jnp.logical_not(holds(owner)))
    def _():
        for ref in outs:
            ref[...] = jnp.zeros_like(ref)


def shampoo_part(owner, left, grad, root, rows, embed):
    cols = root.shape[2]
    depth = left[0].shape[1]
    tensor = len(left)
    turned = cols % LANES != 0
    if turned:
        root = jnp.swapaxes(root, 1, 2)
    if embed:
        shapes = (jax.ShapeDtypeStruct((depth // rows, *packed_shape(rows, cols, 2)), bf16),)
    else:
        small = jax.ShapeDtypeStruct((8, LANES), f32)
        shapes = (jax.ShapeDtypeStruct((depth, cols), f32), small, small)
    return pl.pallas_call(
        functools.partial(shampoo_kernel, rows, cols, turned, embed),
        out_shape=shapes,
        in_specs=[SMEM] + [VMEM] * (2 * tensor + 1),
        out_specs=(VMEM,) * len(shapes),
        scratch_shapes=[
            pltpu.VMEM((depth, depth), bf16),
            pltpu.VMEM((tensor, depth, cols), bf16),
            pltpu.VMEM((depth, cols) if embed else (8, LANES), f32),
        ],
        compiler_params=LIMIT,
        cost_estimate=pl.CostEstimate(
            flops=1_000_000_000 if embed else 2_000_000_000, bytes_accessed=1024, transcendentals=0
        ),
    )(owner, *left, *grad, root)


def stats_kernel(rows, cols, paired, owner, *refs):
    tensor = lax.axis_size("tensor")
    grad, count = refs[:tensor], 1 if paired else 2
    stats, outs = refs[tensor : tensor + count], refs[tensor + count : tensor + 2 * count]
    square, held, (arrived, sent) = refs[tensor + 2 * count], refs[-count - 2 : -2], refs[-2:]

    def sides(group):
        return [group[0].at[0, 0], group[0].at[0, 1]] if paired else [ref.at[0] for ref in group]

    left, right = sides(held)
    fetches, stores = [], []
    for i, (source, slot, target) in enumerate(zip(sides(stats), (left, right), sides(outs))):
        fetches.append(pltpu.make_async_copy(source, slot, arrived.at[i]))
        stores.append(pltpu.make_async_copy(slot, target, sent.at[i]))
        fetches[-1].start()
    part = lax.axis_index("tensor")

    @pl.when(holds(owner))
    def _():
        high = left.shape[0]
        total = jnp.zeros(left.shape, f32)
        mine = unpack(grad[0], rows, cols)
        for k in range(tensor):
            columns = unpack(grad[k], rows, cols)
            slots = high // rows
            band = unpack(grad[k], rows, cols, part * slots, slots)
            total = total + lax.dot_general(
                band, columns, (((1,), (1,)), ((), ())), preferred_element_type=f32
            )
            square[part ^ k] = lax.dot_general(
                mine, columns, (((0,), (0,)), ((), ())), preferred_element_type=f32
            )
        fetches[0].wait()
        left[...] = beta_stat * left[...] + (1.0 - beta_stat) * total
        stores[0].start()
        fetches[1].wait()
        for k in range(tensor):
            span = slice(k * cols, (k + 1) * cols)
            right[:, span] = beta_stat * right[:, span] + (1.0 - beta_stat) * square[k]
        stores[1].start()
        for store in stores:
            store.wait()

    @pl.when(jnp.logical_not(holds(owner)))
    def _():
        for fetch, store in zip(fetches, stores):
            fetch.wait()
            store.start()
        for store in stores:
            store.wait()


def stats_part(owner, grad, stats, rows, cols):
    tensor = len(grad)
    depth = tensor * cols
    return pl.pallas_call(
        functools.partial(stats_kernel, rows, cols, len(stats) == 1),
        out_shape=tuple(jax.ShapeDtypeStruct(value.shape, f32) for value in stats),
        in_specs=[SMEM] + [VMEM] * tensor + [HBM] * len(stats),
        out_specs=(HBM,) * len(stats),
        scratch_shapes=[pltpu.VMEM((tensor, cols, cols), f32)]
        + [pltpu.VMEM(value.shape, f32) for value in stats]
        + [pltpu.SemaphoreType.DMA((2,)), pltpu.SemaphoreType.DMA((2,))],
        compiler_params=LIMIT,
        cost_estimate=pl.CostEstimate(
            flops=1_000_000_000,
            bytes_accessed=1024,
            transcendentals=0,
        ),
    )(owner, *grad, *[in_hbm(value) for value in stats])


def weight_kernel(owner, weight, back, *refs):
    *norm, out = refs
    rows, cols = weight.shape[1:]

    def unit(u, carry):
        update = unpack(back, rows, cols, owner[u], 1).astype(f32)
        if norm:
            adam, *norms = norm
            total = norms[0][u]
            for other in norms[1:]:
                total = total + other[u]
            update = jnp.sqrt(adam[u] / (total + graft_eps))[:1, :1] * update
        out[u] = weight[u] - learn_rate * update
        return carry

    lax.fori_loop(0, weight.shape[0], unit, 0, unroll=weight.shape[0] <= 4)


def weight_part(owner, weight, back, *norm):
    return pl.pallas_call(
        weight_kernel,
        out_shape=jax.ShapeDtypeStruct(weight.shape, f32),
        in_specs=[SMEM] + [VMEM] * (2 + len(norm)),
        out_specs=VMEM,
        compiler_params=LIMIT,
        cost_estimate=pl.CostEstimate(
            flops=2 * weight.size, bytes_accessed=12 * weight.size, transcendentals=0
        ),
    )(owner, weight, back, *norm)


def totals_kernel(rows, cols, owner, back, norm, adam):
    def unit(u, carry):
        for n, ref in enumerate((norm, adam)):
            total = unpack_total(back, rows, cols, n, owner[u], 1)
            ref[u] = jnp.broadcast_to(total, ref.shape[1:])
        return carry

    lax.fori_loop(0, norm.shape[0], unit, 0, unroll=norm.shape[0] <= 4)


def totals_part(owner, back, rows, cols):
    small = jax.ShapeDtypeStruct((owner.shape[0], 8, LANES), f32)
    norm, adam = pl.pallas_call(
        functools.partial(totals_kernel, rows, cols),
        out_shape=(small, small),
        in_specs=[SMEM, VMEM],
        out_specs=(VMEM, VMEM),
        compiler_params=LIMIT,
        cost_estimate=BRIEF,
    )(owner, back)
    return adam, *all_norms(norm)


def all_norms(norm):
    return [norm] + [flip(norm, k) for k in range(1, lax.axis_size("tensor"))]


def flip(value, bits):
    size = lax.axis_size("tensor")
    return lax.ppermute(value, "tensor", [(i, i ^ bits) for i in range(size)])


def spread_first(value):
    return value, flip(value, lax.axis_size("tensor") // 2)


def spread_rest(value, far):
    bit = lax.axis_size("tensor") // 2
    held = {0: value, bit: far}
    bit //= 2
    while bit:
        for k in sorted(held):
            held[k | bit] = flip(held[k], bit)
        bit //= 2
    return [held[k] for k in range(len(held))]


def after(value, *others):
    return lax.optimization_barrier((value, *others))[0]


def over_shard(value):
    return lax.all_to_all(value, "shard", split_axis=0, concat_axis=0, tiled=True)


def scale_kernel(done, adam, *refs):
    norm, out = refs[:-1], refs[-1]
    total = norm[0][...]
    for other in norm[1:]:
        total = total + other[...]
    scale = jnp.sqrt(adam[...] / (total + graft_eps))[:1, :1]
    rows = done.shape[0] // out.shape[0]
    for slot in range(out.shape[0]):
        pack(out.at[slot], scale * done[slot * rows : (slot + 1) * rows, :], ())


def grafted(done, norm, adam, owners):
    depth, cols = done.shape
    norms = all_norms(norm)
    return pl.pallas_call(
        scale_kernel,
        out_shape=jax.ShapeDtypeStruct((owners, *packed_shape(depth // owners, cols, 0)), bf16),
        in_specs=[VMEM] * (2 + len(norms)),
        out_specs=VMEM,
        compiler_params=LIMIT,
        cost_estimate=pl.CostEstimate(
            flops=done.size, bytes_accessed=6 * done.size, transcendentals=0
        ),
    )(done, adam, *norms)


def per_device(
    att_grads,
    glu_grads,
    att_weight,
    att_moment,
    att_second,
    glu_weight,
    glu_moment,
    glu_second,
    att_stats,
    att_left_root,
    att_right_root,
    glu_left_stat,
    glu_right_stat,
    glu_left_root,
    glu_right_root,
    att_owner,
    glu_owner,
):
    owners = lax.axis_size("shard")
    rows = att_weight.shape[1]
    glu_packed = send_part(glu_owner, glu_grads, glu_moment, glu_second, owners)
    glu_root, glu_root_far = spread_first(glu_left_root[0])
    att_root, att_root_far = spread_first(att_left_root[0])
    glu_moment_out, glu_second_out = moments_part(
        after(glu_grads, glu_root_far), glu_moment, glu_second
    )
    att_packed, att_moment_out, att_second_out = adam_part(
        att_owner,
        after(att_grads, glu_moment_out, att_root_far),
        att_moment,
        att_second,
        owners,
        LIMIT,
    )
    glu_near, glu_far = spread_first(after(over_shard(glu_packed), att_packed))
    glu_beside = flip(glu_near, 1)
    glu_root, glu_root_far, _ = lax.optimization_barrier((glu_root, glu_root_far, glu_beside))
    glu_left = spread_rest(glu_root, glu_root_far)
    glu_grad = spread_rest(glu_near, glu_far)
    (glu_done,) = shampoo_part(glu_owner, glu_left, glu_grad, glu_right_root, rows, True)
    att_near, att_far = spread_first(after(over_shard(att_packed), glu_done))
    att_left = spread_rest(*lax.optimization_barrier((att_root, att_root_far, att_near))[:2])
    att_beside = flip(att_near, 1)
    glu_back = over_shard(after(glu_done, att_beside))
    glu_left_out, glu_right_out = stats_part(
        glu_owner,
        [after(glu_grad[0], att_beside), *glu_grad[1:]],
        (glu_left_stat, glu_right_stat),
        rows,
        glu_weight.shape[2],
    )
    att_grad = spread_rest(att_near, after(att_far, glu_left_out, *att_left[1:]))
    att_done = shampoo_part(att_owner, att_left, att_grad, att_right_root, rows, False)
    (att_stats_out,) = stats_part(att_owner, att_grad, (att_stats,), rows, att_weight.shape[2])
    att_back = over_shard(grafted(*att_done, owners))
    glu_totals = totals_part(glu_owner, glu_back, rows, glu_weight.shape[2])
    glu_weight_out = weight_part(glu_owner, glu_weight, glu_back, *glu_totals)
    att_weight_out = weight_part(att_owner, att_weight, att_back)
    return (
        att_weight_out,
        att_moment_out,
        att_second_out,
        glu_weight_out,
        glu_moment_out,
        glu_second_out,
        att_stats_out,
        glu_left_out,
        glu_right_out,
    )


def solution(mesh):
    placed = (
        P(None, None, "shard", "tensor"),
        P(None, None, "shard", "tensor"),
        P(None, "shard", "tensor"),
        P(None, "shard", "tensor"),
        P(None, "shard", "tensor"),
        P(None, "shard", "tensor"),
        P(None, "shard", "tensor"),
        P(None, "shard", "tensor"),
        P("shard", None, "tensor", None),
        P("shard", "tensor", None),
        P("shard", None, "tensor"),
        P("shard", "tensor", None),
        P("shard", "tensor", None),
        P("shard", "tensor", None),
        P("shard", None, "tensor"),
        P(),
        P(),
    )
    return jax.shard_map(
        per_device,
        mesh=mesh,
        in_specs=placed,
        out_specs=(
            P(None, "shard", "tensor"),
            P(None, "shard", "tensor"),
            P(None, "shard", "tensor"),
            P(None, "shard", "tensor"),
            P(None, "shard", "tensor"),
            P(None, "shard", "tensor"),
            P("shard", None, "tensor", None),
            P("shard", "tensor", None),
            P("shard", "tensor", None),
        ),
        check_vma=False,
    )
```

```python
import functools

import jax
import jax.numpy as jnp
from jax import lax
from jax.experimental import pallas as pl
from jax.experimental.pallas import tpu as pltpu
from jax.sharding import PartitionSpec as P

beta_one = 0.9
beta_two = 0.999
beta_stat = 0.999
adam_eps = 1e-08
graft_eps = 1e-06
learn_rate = 0.01

bf16 = jnp.bfloat16
f32 = jnp.float32
LANES = 128
VMEM = pl.BlockSpec(memory_space=pltpu.VMEM)
BRIEF = pl.CostEstimate(flops=1_000_000_000, bytes_accessed=1024, transcendentals=0)
LIMIT = pltpu.CompilerParams(vmem_limit_bytes=16 << 20)
SMEM = pl.BlockSpec(memory_space=pltpu.SMEM)
HBM = pl.BlockSpec(memory_space=pltpu.HBM)


def in_hbm(value):
    return pltpu.with_memory_space_constraint(value, pltpu.HBM)


def round_up(value, step):
    return -(-value // step) * step


def folds(rows, cols):
    return cols == LANES + LANES // 2 and rows % 32 == 0


def packed_shape(rows, cols, totals):
    lanes = round_up(cols, LANES)
    if folds(rows, cols):
        return (rows + rows // 2 + round_up(3 * totals, 8), LANES)
    return (rows, lanes) if lanes > cols else (round_up(rows + 3 * totals, 8), cols)


def pieces(totals, shape):
    row = lax.broadcasted_iota(jnp.int32, shape, 0)
    column = lax.broadcasted_iota(jnp.int32, shape, 1)
    value = jnp.zeros(shape, f32)
    for n, total in enumerate(totals):
        rest = jnp.broadcast_to(total, shape)
        for m in range(3):
            piece = rest.astype(bf16).astype(f32)
            value = jnp.where(row == 3 * n + m, piece, value)
            rest = rest - piece
    return jnp.where(column == 0, value, 0.0).astype(bf16)


def pack(ref, value, totals):
    rows, cols = value.shape
    high, wide = ref.shape
    if folds(rows, cols):
        half, side = rows // 2, value[:, LANES:]
        ref[:rows, :] = value[:, :LANES].astype(bf16)
        ref[rows : rows + half, :] = jnp.concatenate([side[:half], side[half:]], axis=1).astype(bf16)
        if totals:
            ref[rows + half :, :] = pieces(totals, (high - rows - half, wide))
    elif wide > cols:
        ref[:, :cols] = value.astype(bf16)
        ref[:, cols:] = pieces(totals, (high, wide - cols))
    else:
        ref[:rows, :] = value.astype(bf16)
        if totals:
            ref[rows:, :] = pieces(totals, (high - rows, wide))


def unpack(ref, rows, cols, start=0, count=None):
    count = ref.shape[0] if count is None else count
    span = pl.ds(start, count)
    if not folds(rows, cols):
        return ref[span, :rows, :cols].reshape(count * rows, cols)
    side = ref[span, rows : rows + rows // 2, :]
    side = jnp.concatenate([side[:, :, : LANES // 2], side[:, :, LANES // 2 :]], axis=1)
    return jnp.concatenate([ref[span, :rows, :], side], axis=2).reshape(count * rows, cols)


def unpack_total(ref, rows, cols, n, start=0, count=None):
    count = ref.shape[0] if count is None else count
    span = pl.ds(start, count)
    if folds(rows, cols):
        extra = ref[span, rows + rows // 2 :, :]
    elif ref.shape[2] > cols:
        extra = ref[span, :, cols:]
    else:
        extra = ref[span, rows:, :]
    row = lax.broadcasted_iota(jnp.int32, extra.shape, 1)
    mine = jnp.where((row >= 3 * n) & (row < 3 * n + 3), extra.astype(f32), 0.0)
    return jnp.sum(jnp.sum(mine, axis=0), axis=(0, 1), keepdims=True)


def adam_kernel(owner, grads, moment, second, packed, moment_out, second_out):
    packed[...] = jnp.zeros_like(packed)

    def unit(u, carry):
        summed = grads[0, u]
        for micro in range(1, grads.shape[0]):
            summed = summed + grads[micro, u]
        moment_new = beta_one * moment[u] + (1.0 - beta_one) * summed
        second_new = beta_two * second[u] + (1.0 - beta_two) * summed * summed
        direction = moment_new / (jnp.sqrt(second_new) + adam_eps)
        moment_out[u] = moment_new
        second_out[u] = second_new
        total = jnp.sum(direction * direction, axis=(0, 1), keepdims=True)
        pack(packed.at[owner[u]], summed, (total,))
        return carry

    lax.fori_loop(0, moment.shape[0], unit, 0, unroll=moment.shape[0] <= 4)


def adam_part(owner, grads, moment, second, owners, params):
    rows, cols = moment.shape[1:]
    return pl.pallas_call(
        adam_kernel,
        out_shape=(
            jax.ShapeDtypeStruct((owners, *packed_shape(rows, cols, 1)), bf16),
            jax.ShapeDtypeStruct(moment.shape, f32),
            jax.ShapeDtypeStruct(second.shape, f32),
        ),
        in_specs=[SMEM, VMEM, VMEM, VMEM],
        out_specs=(VMEM, VMEM, VMEM),
        compiler_params=params,
        cost_estimate=pl.CostEstimate(
            flops=20 * moment.size, bytes_accessed=32 * moment.size, transcendentals=moment.size
        ),
    )(owner, grads, moment, second)


def send_kernel(owner, grads, moment, second, packed):
    packed[...] = jnp.zeros_like(packed)

    def unit(u, carry):
        summed = grads[0, u]
        for micro in range(1, grads.shape[0]):
            summed = summed + grads[micro, u]
        moment_new = beta_one * moment[u] + (1.0 - beta_one) * summed
        second_new = beta_two * second[u] + (1.0 - beta_two) * summed * summed
        direction = moment_new / (jnp.sqrt(second_new) + adam_eps)
        total = jnp.sum(direction * direction, axis=(0, 1), keepdims=True)
        pack(packed.at[owner[u]], summed, (total,))
        return carry

    lax.fori_loop(0, moment.shape[0], unit, 0, unroll=moment.shape[0] <= 4)


def send_part(owner, grads, moment, second, owners):
    rows, cols = moment.shape[1:]
    return pl.pallas_call(
        send_kernel,
        out_shape=jax.ShapeDtypeStruct((owners, *packed_shape(rows, cols, 1)), bf16),
        in_specs=[SMEM, VMEM, VMEM, VMEM],
        out_specs=VMEM,
        cost_estimate=pl.CostEstimate(
            flops=10_000_000_000, bytes_accessed=32 * moment.size, transcendentals=moment.size
        ),
    )(owner, grads, moment, second)


def moments_kernel(grads, moment, second, moment_out, second_out):
    summed = grads[0]
    for micro in range(1, grads.shape[0]):
        summed = summed + grads[micro]
    moment_out[...] = beta_one * moment[...] + (1.0 - beta_one) * summed
    second_out[...] = beta_two * second[...] + (1.0 - beta_two) * summed * summed


def moments_part(grads, moment, second):
    return pl.pallas_call(
        moments_kernel,
        out_shape=(
            jax.ShapeDtypeStruct(moment.shape, f32),
            jax.ShapeDtypeStruct(second.shape, f32),
        ),
        in_specs=[VMEM, VMEM, VMEM],
        out_specs=(VMEM, VMEM),
        compiler_params=LIMIT,
        cost_estimate=BRIEF,
    )(grads, moment, second)


def holds(owner):
    me = lax.axis_index("shard")
    found = owner[0] == me
    for unit in range(1, owner.shape[0]):
        found = jnp.logical_or(found, owner[unit] == me)
    return found


def shampoo_kernel(rows, cols, turned, embed, owner, *refs):
    tensor = lax.axis_size("tensor")
    left, grad = refs[:tensor], refs[tensor : 2 * tensor]
    root, *outs, whole, blocks, done = refs[2 * tensor :]
    part = lax.axis_index("tensor")

    @pl.when(holds(owner))
    def _():
        depth = left[0].shape[0]
        adam_sq = jnp.zeros((1, 1), f32)
        for k in range(tensor):
            band = pl.ds(pl.multiple_of((part ^ k) * depth, depth), depth)
            whole[band, :] = left[k][...]
            blocks[part ^ k] = unpack(grad[k], rows, cols)
            adam_sq = adam_sq + unpack_total(grad[k], rows, cols, 0)
        half = jnp.zeros((whole.shape[0], cols), f32)
        for k in range(tensor):
            span = slice(k * cols, (k + 1) * cols)
            if turned:
                sides, right = (((1,), (1,)), ((), ())), root[0, :, span]
            else:
                sides, right = (((1,), (0,)), ((), ())), root[0, span, :]
            half = half + lax.dot_general(blocks[k], right, sides, preferred_element_type=f32)
        total = jnp.dot(whole[...], half.astype(bf16), preferred_element_type=f32)
        norm = jnp.sum(total * total, axis=(0, 1), keepdims=True)
        if embed:
            done[...] = total
            for slot in range(outs[0].shape[0]):
                value = done[slot * rows : (slot + 1) * rows, :]
                pack(outs[0].at[slot], value, (norm, adam_sq))
        else:
            for ref, value in zip(outs, (total, norm, adam_sq)):
                ref[...] = jnp.broadcast_to(value, ref.shape)

    @pl.when(jnp.logical_not(holds(owner)))
    def _():
        for ref in outs:
            ref[...] = jnp.zeros_like(ref)


def shampoo_part(owner, left, grad, root, rows, embed):
    cols = root.shape[2]
    depth = left[0].shape[1]
    tensor = len(left)
    turned = cols % LANES != 0
    if turned:
        root = jnp.swapaxes(root, 1, 2)
    if embed:
        shapes = (jax.ShapeDtypeStruct((depth // rows, *packed_shape(rows, cols, 2)), bf16),)
    else:
        small = jax.ShapeDtypeStruct((8, LANES), f32)
        shapes = (jax.ShapeDtypeStruct((depth, cols), f32), small, small)
    return pl.pallas_call(
        functools.partial(shampoo_kernel, rows, cols, turned, embed),
        out_shape=shapes,
        in_specs=[SMEM] + [VMEM] * (2 * tensor + 1),
        out_specs=(VMEM,) * len(shapes),
        scratch_shapes=[
            pltpu.VMEM((depth, depth), bf16),
            pltpu.VMEM((tensor, depth, cols), bf16),
            pltpu.VMEM((depth, cols) if embed else (8, LANES), f32),
        ],
        compiler_params=LIMIT,
        cost_estimate=pl.CostEstimate(
            flops=1_000_000_000 if embed else 2_000_000_000, bytes_accessed=1024, transcendentals=0
        ),
    )(owner, *left, *grad, root)


def stats_kernel(rows, cols, paired, owner, *refs):
    tensor = lax.axis_size("tensor")
    grad, count = refs[:tensor], 1 if paired else 2
    stats, outs = refs[tensor : tensor + count], refs[tensor + count : tensor + 2 * count]
    square, held, (arrived, sent) = refs[tensor + 2 * count], refs[-count - 2 : -2], refs[-2:]

    def sides(group):
        return [group[0].at[0, 0], group[0].at[0, 1]] if paired else [ref.at[0] for ref in group]

    left, right = sides(held)
    fetches, stores = [], []
    for i, (source, slot, target) in enumerate(zip(sides(stats), (left, right), sides(outs))):
        fetches.append(pltpu.make_async_copy(source, slot, arrived.at[i]))
        stores.append(pltpu.make_async_copy(slot, target, sent.at[i]))
        fetches[-1].start()
    part = lax.axis_index("tensor")

    @pl.when(holds(owner))
    def _():
        high = left.shape[0]
        total = jnp.zeros(left.shape, f32)
        mine = unpack(grad[0], rows, cols)
        for k in range(tensor):
            columns = unpack(grad[k], rows, cols)
            slots = high // rows
            band = unpack(grad[k], rows, cols, part * slots, slots)
            total = total + lax.dot_general(
                band, columns, (((1,), (1,)), ((), ())), preferred_element_type=f32
            )
            square[part ^ k] = lax.dot_general(
                mine, columns, (((0,), (0,)), ((), ())), preferred_element_type=f32
            )
        fetches[0].wait()
        left[...] = beta_stat * left[...] + (1.0 - beta_stat) * total
        stores[0].start()
        fetches[1].wait()
        for k in range(tensor):
            span = slice(k * cols, (k + 1) * cols)
            right[:, span] = beta_stat * right[:, span] + (1.0 - beta_stat) * square[k]
        stores[1].start()
        for store in stores:
            store.wait()

    @pl.when(jnp.logical_not(holds(owner)))
    def _():
        for fetch, store in zip(fetches, stores):
            fetch.wait()
            store.start()
        for store in stores:
            store.wait()


def stats_part(owner, grad, stats, rows, cols):
    tensor = len(grad)
    depth = tensor * cols
    return pl.pallas_call(
        functools.partial(stats_kernel, rows, cols, len(stats) == 1),
        out_shape=tuple(jax.ShapeDtypeStruct(value.shape, f32) for value in stats),
        in_specs=[SMEM] + [VMEM] * tensor + [HBM] * len(stats),
        out_specs=(HBM,) * len(stats),
        scratch_shapes=[pltpu.VMEM((tensor, cols, cols), f32)]
        + [pltpu.VMEM(value.shape, f32) for value in stats]
        + [pltpu.SemaphoreType.DMA((2,)), pltpu.SemaphoreType.DMA((2,))],
        compiler_params=LIMIT,
        cost_estimate=pl.CostEstimate(
            flops=1_000_000_000,
            bytes_accessed=1024,
            transcendentals=0,
        ),
    )(owner, *grad, *[in_hbm(value) for value in stats])


def weight_kernel(owner, weight, back, *refs):
    *norm, out = refs
    rows, cols = weight.shape[1:]

    def unit(u, carry):
        update = unpack(back, rows, cols, owner[u], 1).astype(f32)
        if norm:
            adam, *norms = norm
            total = norms[0][u]
            for other in norms[1:]:
                total = total + other[u]
            update = jnp.sqrt(adam[u] / (total + graft_eps))[:1, :1] * update
        out[u] = weight[u] - learn_rate * update
        return carry

    lax.fori_loop(0, weight.shape[0], unit, 0, unroll=weight.shape[0] <= 4)


def weight_part(owner, weight, back, *norm):
    return pl.pallas_call(
        weight_kernel,
        out_shape=jax.ShapeDtypeStruct(weight.shape, f32),
        in_specs=[SMEM] + [VMEM] * (2 + len(norm)),
        out_specs=VMEM,
        compiler_params=LIMIT,
        cost_estimate=pl.CostEstimate(
            flops=2 * weight.size, bytes_accessed=12 * weight.size, transcendentals=0
        ),
    )(owner, weight, back, *norm)


def totals_kernel(rows, cols, owner, back, norm, adam):
    def unit(u, carry):
        for n, ref in enumerate((norm, adam)):
            total = unpack_total(back, rows, cols, n, owner[u], 1)
            ref[u] = jnp.broadcast_to(total, ref.shape[1:])
        return carry

    lax.fori_loop(0, norm.shape[0], unit, 0, unroll=norm.shape[0] <= 4)


def totals_part(owner, back, rows, cols):
    small = jax.ShapeDtypeStruct((owner.shape[0], 8, LANES), f32)
    norm, adam = pl.pallas_call(
        functools.partial(totals_kernel, rows, cols),
        out_shape=(small, small),
        in_specs=[SMEM, VMEM],
        out_specs=(VMEM, VMEM),
        compiler_params=LIMIT,
        cost_estimate=BRIEF,
    )(owner, back)
    return adam, *all_norms(norm)


def all_norms(norm):
    return [norm] + [flip(norm, k) for k in range(1, lax.axis_size("tensor"))]


def flip(value, bits):
    size = lax.axis_size("tensor")
    return lax.ppermute(value, "tensor", [(i, i ^ bits) for i in range(size)])


def spread_first(value):
    return value, flip(value, lax.axis_size("tensor") // 2)


def spread_rest(value, far):
    bit = lax.axis_size("tensor") // 2
    held = {0: value, bit: far}
    bit //= 2
    while bit:
        for k in sorted(held):
            held[k | bit] = flip(held[k], bit)
        bit //= 2
    return [held[k] for k in range(len(held))]


def after(value, *others):
    return lax.optimization_barrier((value, *others))[0]


def over_shard(value):
    return lax.all_to_all(value, "shard", split_axis=0, concat_axis=0, tiled=True)


def scale_kernel(done, adam, *refs):
    norm, out = refs[:-1], refs[-1]
    total = norm[0][...]
    for other in norm[1:]:
        total = total + other[...]
    scale = jnp.sqrt(adam[...] / (total + graft_eps))[:1, :1]
    rows = done.shape[0] // out.shape[0]
    for slot in range(out.shape[0]):
        pack(out.at[slot], scale * done[slot * rows : (slot + 1) * rows, :], ())


def grafted(done, norm, adam, owners):
    depth, cols = done.shape
    norms = all_norms(norm)
    return pl.pallas_call(
        scale_kernel,
        out_shape=jax.ShapeDtypeStruct((owners, *packed_shape(depth // owners, cols, 0)), bf16),
        in_specs=[VMEM] * (2 + len(norms)),
        out_specs=VMEM,
        compiler_params=LIMIT,
        cost_estimate=pl.CostEstimate(
            flops=done.size, bytes_accessed=6 * done.size, transcendentals=0
        ),
    )(done, adam, *norms)


def per_device(
    att_grads,
    glu_grads,
    att_weight,
    att_moment,
    att_second,
    glu_weight,
    glu_moment,
    glu_second,
    att_stats,
    att_left_root,
    att_right_root,
    glu_left_stat,
    glu_right_stat,
    glu_left_root,
    glu_right_root,
    att_owner,
    glu_owner,
):
    owners = lax.axis_size("shard")
    rows = att_weight.shape[1]
    glu_packed = send_part(glu_owner, glu_grads, glu_moment, glu_second, owners)
    glu_root, glu_root_far = spread_first(glu_left_root[0])
    att_packed, att_moment_out, att_second_out = adam_part(
        att_owner,
        att_grads,
        att_moment,
        att_second,
        owners,
        LIMIT,
    )
    glu_moment_out, glu_second_out = moments_part(
        after(glu_grads, att_packed), glu_moment, glu_second
    )
    glu_near, glu_far = spread_first(
        after(over_shard(glu_packed), glu_moment_out, glu_root_far)
    )
    att_root, att_root_far = spread_first(after(att_left_root[0], glu_far))
    glu_beside = flip(glu_near, 1)
    glu_root, glu_root_far, _ = lax.optimization_barrier((glu_root, glu_root_far, glu_beside))
    glu_left = spread_rest(glu_root, glu_root_far)
    glu_grad = spread_rest(glu_near, glu_far)
    (glu_done,) = shampoo_part(glu_owner, glu_left, glu_grad, glu_right_root, rows, True)
    att_near, att_far = spread_first(after(over_shard(att_packed), glu_done))
    att_left = spread_rest(*lax.optimization_barrier((att_root, att_root_far, att_near))[:2])
    att_beside = flip(att_near, 1)
    glu_back = over_shard(after(glu_done, att_beside))
    glu_left_out, glu_right_out = stats_part(
        glu_owner,
        [after(glu_grad[0], att_beside), *glu_grad[1:]],
        (glu_left_stat, glu_right_stat),
        rows,
        glu_weight.shape[2],
    )
    att_grad = spread_rest(att_near, after(att_far, glu_left_out, *att_left[1:]))
    att_done = shampoo_part(att_owner, att_left, att_grad, att_right_root, rows, False)
    (att_stats_out,) = stats_part(att_owner, att_grad, (att_stats,), rows, att_weight.shape[2])
    att_back = over_shard(grafted(*att_done, owners))
    glu_totals = totals_part(glu_owner, glu_back, rows, glu_weight.shape[2])
    glu_weight_out = weight_part(glu_owner, glu_weight, glu_back, *glu_totals)
    att_weight_out = weight_part(att_owner, att_weight, att_back)
    return (
        att_weight_out,
        att_moment_out,
        att_second_out,
        glu_weight_out,
        glu_moment_out,
        glu_second_out,
        att_stats_out,
        glu_left_out,
        glu_right_out,
    )


def solution(mesh):
    placed = (
        P(None, None, "shard", "tensor"),
        P(None, None, "shard", "tensor"),
        P(None, "shard", "tensor"),
        P(None, "shard", "tensor"),
        P(None, "shard", "tensor"),
        P(None, "shard", "tensor"),
        P(None, "shard", "tensor"),
        P(None, "shard", "tensor"),
        P("shard", None, "tensor", None),
        P("shard", "tensor", None),
        P("shard", None, "tensor"),
        P("shard", "tensor", None),
        P("shard", "tensor", None),
        P("shard", "tensor", None),
        P("shard", None, "tensor"),
        P(),
        P(),
    )
    return jax.shard_map(
        per_device,
        mesh=mesh,
        in_specs=placed,
        out_specs=(
            P(None, "shard", "tensor"),
            P(None, "shard", "tensor"),
            P(None, "shard", "tensor"),
            P(None, "shard", "tensor"),
            P(None, "shard", "tensor"),
            P(None, "shard", "tensor"),
            P("shard", None, "tensor", None),
            P("shard", "tensor", None),
            P("shard", "tensor", None),
        ),
        check_vma=False,
    )
```
